32 devices in a mesh: dom: 8 (over z, y), samp: 4 (over x, core).
Axes of the slice: x: 2, y: 2, z: 4, core: 2. Of those that a mesh axis runs over, the one named last changes fastest.
Arguments:
- residual: float32 [256, 32768], P('samp', 'dom'), may hold values from -60 to 60
- conductance: float32 [256, 32768], P('samp', 'dom'), may hold values from 0.2 to 2
- capacitance: float32 [256, 32768], P('samp', 'dom'), may hold values from 0.2 to 2
- stamps: float32 [512, 4, 64, 128], P('dom'), may hold values from -0.375 to 0.375
- block_cols: int32 [512, 4], P('dom'), may hold values from 0 to 95, as said below
- send_blocks: int32 [8, 8, 4], P('dom'), may hold values from 0 to 63
Outputs:
- update: float32 [256, 32768], P('samp', 'dom')
The draws below stay inside these ranges and needn't reach their ends.
Inputs may be any that keep to these rules, and one draw needn't show every extreme that they name: `block_cols`: entries below 64 name the partition's own block rows; an entry 64 + s * 4 + j names slot j that partition s sends to this partition, s never the partition itself; entry 0 of a row is the row's own block.
All inputs are finite; a program needn't handle non-finite values.
Results may differ from the reference program's by a relative error of at most 0.00005.
Values sent between devices are 32-bit elements; how exact they have to be, the bound alone decides.
No kernel may reach another device: no remote copies, remote signals or barrier semaphores. Data moves between devices by JAX's collectives and lax.ppermute only.
A program may use at most 64 MiB of HBM per device.

```python
import math
import jax
import jax.numpy as jnp
from jax import lax

BLK = 64
PER_ROW = 4
SLOTS = 4
SAMPLES = 256
ROWS_DEV = 64
BLOCKS = 512
UNKNOWNS = 32768
N_DOM = 8


def draw_block_cols(key, part):
    domains = BLOCKS // ROWS_DEV
    rows = jnp.arange(BLOCKS, dtype=jnp.int32)
    owner = rows // ROWS_DEV
    local = rows % ROWS_DEV
    columns = [local]
    for entry in range(1, PER_ROW):
        keys = jax.random.split(jax.random.fold_in(key, entry), 4)
        position = local * (PER_ROW - 1) + (entry - 1)
        forced = position < domains - 1
        forced_value = ROWS_DEV + (owner + 1 + position) % domains * SLOTS + SLOTS - 1
        remote_flag = jax.random.randint(keys[0], (BLOCKS,), 0, 2)
        offset = jax.random.randint(keys[1], (BLOCKS,), 1, domains)
        slot = jax.random.randint(keys[2], (BLOCKS,), 0, SLOTS)
        near = jax.random.randint(keys[3], (BLOCKS,), 0, ROWS_DEV)
        random_far = ROWS_DEV + (owner + offset) % domains * SLOTS + slot
        chosen = jnp.where(remote_flag == 1, random_far, near)
        columns.append(jnp.where(forced, forced_value, chosen))
    return jnp.stack(columns, axis=1).astype(jnp.int32)


def draw_residual(key, part):
    keys = jax.random.split(jax.random.fold_in(key, 7), 3)
    ramp_rows = 1.0 + 2.0 * jnp.arange(SAMPLES, dtype=jnp.float32) / SAMPLES
    ramp_columns = 1.0 + 2.0 * jnp.arange(UNKNOWNS, dtype=jnp.float32) / UNKNOWNS
    row_scale = jnp.exp(jax.random.uniform(keys[0], (SAMPLES,), jnp.float32, 0.0, math.log(10.0))) * ramp_rows
    column_scale = jnp.exp(jax.random.uniform(keys[1], (UNKNOWNS,), jnp.float32, 0.0, math.log(10.0))) * ramp_columns
    base = jax.random.normal(keys[2], (SAMPLES, UNKNOWNS), jnp.float32)
    value = 0.3 * base * row_scale[:, None] * column_scale[None, :]
    return jnp.clip(value, -60.0, 60.0).astype(jnp.float32)


def plant(result, stream_key, smallest, high):
    longest = result.shape.index(max(result.shape))
    spots = []
    for shift in (0, 1):
        where = [jax.random.randint(jax.random.fold_in(stream_key, axis), (), 0, length) for axis, length in enumerate(result.shape)]
        where[longest] = (where[longest] + shift) % result.shape[longest]
        spots.append(tuple(where))
    return result.at[spots[0]].set(smallest).at[spots[1]].set(high)


def level_of(key, dims, cuts, low, largest):
    level = 1.0
    for axis_at, blocks in cuts:
        steps = jax.random.uniform(jax.random.fold_in(jax.random.fold_in(key, 6), axis_at), (blocks,), jnp.float32, low / len(cuts), largest / len(cuts))
        level = level * jnp.repeat(jnp.exp(steps), dims[axis_at] // blocks).reshape((-1,) + (1,) * (len(dims) - 1 - axis_at))
    return level


def centred(own_key, shape, deviation, limit, shards=(), kind=jnp.bfloat16):
    values = deviation * jax.random.normal(own_key, shape, jnp.float32)
    if shards:
        values = values * level_of(own_key, shape, shards, -0.22, 0.18)
    return jnp.clip(values, -limit, limit).astype(kind)


def setup_inputs(seed: int = 0) -> dict:
    splits = jax.random.split(jax.random.key(seed), 7)
    residual = draw_residual(jax.random.fold_in(splits[6], 71), 0)
    conductance = jnp.clip(jnp.exp(math.log(2.0) - 2.3025851 * jax.random.uniform(splits[1], (SAMPLES, UNKNOWNS), jnp.float32) ** level_of(splits[1], (SAMPLES, UNKNOWNS), ((0, 4), (1, 8)), -0.2, 0.2)), 0.2, 2.0)
    capacitance = jnp.clip(jnp.exp(math.log(2.0) - 2.3025851 * jax.random.uniform(splits[2], (SAMPLES, UNKNOWNS), jnp.float32) ** level_of(splits[2], (SAMPLES, UNKNOWNS), ((0, 4), (1, 8)), -0.2, 0.2)), 0.2, 2.0)
    stamps = centred(splits[3], (BLOCKS, PER_ROW, BLK, 2 * BLK), (PER_ROW * BLK) ** -0.5, 0.375, ((0, 8),), jnp.float32)
    block_cols = draw_block_cols(jax.random.fold_in(splits[6], 71), 0)
    send_blocks = plant(jax.random.randint(splits[5], (N_DOM, N_DOM, SLOTS), 0, ROWS_DEV), jax.random.fold_in(splits[5], 1), 0, ROWS_DEV - 1).astype(jnp.int32)
    return dict(residual=residual, conductance=conductance, capacitance=capacitance, stamps=stamps, block_cols=block_cols, send_blocks=send_blocks)


def spectral_block(first_row, rows, first_column, columns, order):
    row_ids = first_row + jnp.arange(rows, dtype=jnp.int32)
    column_ids = first_column + jnp.arange(columns, dtype=jnp.int32)
    offset = row_ids[:, None] - column_ids[None, :]
    parity = (offset % 2).astype(jnp.float32)
    sign = 1.0 - 2.0 * parity
    angle = jnp.pi / order * offset.astype(jnp.float32)
    nonzero = offset != 0
    safe = jnp.where(nonzero, angle, 0.5)
    value = sign * jnp.cos(safe) / jnp.sin(safe) / order
    return jnp.where(nonzero, value, 0.0).astype(jnp.float32)

def global_columns(block_cols, send_blocks):
    rows = jnp.arange(BLOCKS, dtype=jnp.int32)
    owner = jnp.broadcast_to((rows // ROWS_DEV)[:, None], block_cols.shape).astype(jnp.int32)
    remote = block_cols - ROWS_DEV
    source = jnp.clip(remote // SLOTS, 0, N_DOM - 1).astype(jnp.int32)
    slot = jnp.clip(remote % SLOTS, 0, SLOTS - 1).astype(jnp.int32)
    far = source * ROWS_DEV + send_blocks[source, owner, slot]
    near = owner * ROWS_DEV + block_cols
    return jnp.where(block_cols < ROWS_DEV, near, far).astype(jnp.int32)

def apply_jacobian(field, conductance, capacitance, weights, columns, matrix):
    group = math.gcd(SAMPLES, 32)
    flat = columns.reshape(-1)
    blocked = field.reshape(SAMPLES // group, group, BLOCKS, BLK)

    def one_group(part):
        picked = jnp.take(part, flat, axis=1).reshape(group, BLOCKS, PER_ROW * BLK)
        return jnp.einsum('srm,rmo->sro', picked, weights, precision=lax.Precision.HIGHEST, preferred_element_type=jnp.float32)
    product = lax.map(one_group, blocked).reshape(SAMPLES, BLOCKS, 2 * BLK)
    direct = product[:, :, :BLK].reshape(SAMPLES, UNKNOWNS)
    charge = product[:, :, BLK:].reshape(SAMPLES, UNKNOWNS) + capacitance * field
    slope = jnp.dot(matrix, charge, precision=lax.Precision.HIGHEST, preferred_element_type=jnp.float32)
    return direct + conductance * field + slope

def reference(residual, conductance, capacitance, stamps, block_cols, send_blocks):
    columns = global_columns(block_cols, send_blocks)
    weights = stamps.reshape(BLOCKS, PER_ROW * BLK, 2 * BLK)
    matrix = spectral_block(0, SAMPLES, 0, SAMPLES, SAMPLES)
    scale_norm = jnp.sqrt(jnp.sum(residual * residual))
    basis_one = residual / scale_norm
    image = apply_jacobian(basis_one, conductance, capacitance, weights, columns, matrix)
    upper_one = jnp.sum(basis_one * image)
    image = image - upper_one * basis_one
    lower_one = jnp.sqrt(jnp.sum(image * image))
    basis_two = image / lower_one
    image = apply_jacobian(basis_two, conductance, capacitance, weights, columns, matrix)
    upper_two = jnp.sum(basis_one * image)
    middle_two = jnp.sum(basis_two * image)
    image = image - upper_two * basis_one - middle_two * basis_two
    lower_two = jnp.sqrt(jnp.sum(image * image))
    gram_first = upper_one * upper_one + lower_one * lower_one
    gram_cross = upper_one * upper_two + lower_one * middle_two
    gram_second = upper_two * upper_two + middle_two * middle_two + lower_two * lower_two
    target_first = scale_norm * upper_one
    target_second = scale_norm * upper_two
    determinant = gram_first * gram_second - gram_cross * gram_cross
    weight_first = (gram_second * target_first - gram_cross * target_second) / determinant
    weight_second = (gram_first * target_second - gram_cross * target_first) / determinant
    return weight_first * basis_one + weight_second * basis_two
```

```python
import functools

import jax
import jax.numpy as jnp
from jax import lax
from jax.experimental import pallas as pl
from jax.experimental.pallas import tpu as pltpu
from jax.sharding import PartitionSpec as P

LANES = 128
HALF = 64
GROUP = 8
SUMS = 8


def whole(shape=None):
    return pl.BlockSpec(memory_space=pltpu.VMEM)


def scalars():
    return pl.BlockSpec(memory_space=pltpu.SMEM)


def split(x):
    high = x.astype(jnp.bfloat16)
    low = (x - high.astype(jnp.float32)).astype(jnp.bfloat16)
    return high, low


def spectral_rows(me, sources, samples, period):
    row = me * samples + lax.broadcasted_iota(jnp.int32, (samples, samples), 0)
    column = lax.broadcasted_iota(jnp.int32, (samples, samples), 1)
    blocks = []
    for source in sources:
        offset = row - (source * samples + column)
        parity = (offset % 2).astype(jnp.float32)
        sign = 1.0 - 2.0 * parity
        angle = jnp.pi / period * offset.astype(jnp.float32)
        nonzero = offset != 0
        safe = jnp.where(nonzero, angle, 0.5)
        value = sign * jnp.cos(safe) / jnp.sin(safe) / period
        blocks.append(jnp.where(nonzero, value, 0.0))
    exact = jnp.concatenate(blocks, axis=1)
    high = lax.reduce_precision(exact, exponent_bits=8, mantissa_bits=7)
    return jnp.concatenate([high, exact - high], axis=0).astype(jnp.bfloat16)


def prepare_kernel(stamps_ref, out_ref):
    high, low = split(stamps_ref[...])
    width = stamps_ref.shape[-1]
    out_ref[:, :, :width] = high
    out_ref[:, :, width:] = low


def prepare(stamps):
    rows, depth, width = stamps.shape
    group = GROUP if rows % GROUP == 0 else 1
    return pl.pallas_call(
        prepare_kernel,
        grid=(rows // group,),
        in_specs=[pl.BlockSpec((group, depth, width), lambda i: (i, 0, 0))],
        out_specs=pl.BlockSpec((group, depth, 2 * width), lambda i: (i, 0, 0)),
        out_shape=jax.ShapeDtypeStruct((rows, depth, 2 * width), jnp.bfloat16),
        name="prepare",
    )(stamps)


def gather_blocks(send_ref, field_ref, out_ref):
    domains, samples, wide = out_ref.shape
    slots = wide // HALF
    lane = lax.broadcasted_iota(jnp.int32, (samples, LANES), 1)

    def placed(block, upper):
        start = pl.multiple_of((block // 2) * LANES, LANES)
        tile = field_ref[:, pl.ds(start, LANES)]
        turned = pltpu.roll(tile, HALF, 1)
        return jnp.where((block % 2) == upper, tile, turned)

    for d in range(domains):
        for j in range(0, slots, 2):
            first = placed(send_ref[d * slots + j], 0)
            second = placed(send_ref[d * slots + j + 1], 1)
            out_ref[d, :, j * HALF : j * HALF + LANES] = jnp.where(lane < HALF, first, second)


def send_call(send, field, domains):
    samples = field.shape[0]
    slots = send.shape[0] // domains
    return pl.pallas_call(
        gather_blocks,
        in_specs=[scalars(), whole()],
        out_specs=whole(),
        out_shape=jax.ShapeDtypeStruct((domains, samples, slots * HALF), jnp.float32),
        name="gather_blocks",
    )(send, field)


def product_kernel(per_entry, cols_ref, field_ref, inc_ref, g_ref, c_ref, w_ref, p_ref, q_ref, ext):
    samples, unknowns = field_ref.shape
    step = pl.program_id(0)
    tiles = ext.shape[1]
    own_tiles = unknowns // LANES
    domains, _, wide = inc_ref.shape
    per_domain = wide // LANES
    group = w_ref.shape[0]

    def store(index, x):
        high, low = split(x)
        ext[0, index] = jnp.concatenate([high, low], axis=0)
        high, low = split(pltpu.roll(x, HALF, 1))
        ext[1, index] = jnp.concatenate([high, low], axis=0)

    @pl.when(step == 0)
    def _():
        for i in range(own_tiles):
            store(i, field_ref[:, i * LANES : (i + 1) * LANES])
        for d in range(domains):
            for j in range(per_domain):
                store(own_tiles + d * per_domain + j, inc_ref[d, :, j * LANES : (j + 1) * LANES])

    lane = lax.broadcasted_iota(jnp.int32, (2 * samples, LANES), 1)
    low_lane = lax.broadcasted_iota(jnp.int32, (samples, LANES), 1) < HALF

    def row_product(local):
        base = (step * group + local) * per_entry
        parts = []
        for k in range(0, per_entry, 2):
            first = cols_ref[base + k]
            second = cols_ref[base + k + 1]
            a = ext[first % 2, first // 2]
            b = ext[1 - second % 2, second // 2]
            parts.append(jnp.where(lane < HALF, a, b))
        left = jnp.concatenate(parts, axis=1)
        full = jnp.dot(left, w_ref[local], preferred_element_type=jnp.float32)
        width = full.shape[1] // 2
        rows = full[:, :width] + full[:, width:]
        return rows[:samples] + rows[samples:]

    for pair in range(group // 2):
        first = row_product(2 * pair)
        second = row_product(2 * pair + 1)
        direct = jnp.where(low_lane, first, pltpu.roll(second, HALF, 1))
        charge = jnp.where(low_lane, pltpu.roll(first, HALF, 1), second)
        inside = slice(pair * LANES, (pair + 1) * LANES)
        start = pl.multiple_of((step * (group // 2) + pair) * LANES, LANES)
        own = field_ref[:, pl.ds(start, LANES)]
        p_ref[:, inside] = direct + g_ref[:, inside] * own
        q_ref[:, inside] = charge + c_ref[:, inside] * own


def product(cols, field, incoming, conductance, capacitance, weights):
    samples, unknowns = field.shape
    domains, _, wide = incoming.shape
    rows, depth, double = weights.shape
    group = GROUP
    tiles = unknowns // LANES + domains * wide // LANES
    columns = pl.BlockSpec((samples, group * HALF), lambda i, *_: (0, i))
    return pl.pallas_call(
        functools.partial(product_kernel, depth // HALF),
        grid_spec=pltpu.PrefetchScalarGridSpec(
            num_scalar_prefetch=1,
            grid=(rows // group,),
            in_specs=[
                whole(),
                whole(),
                columns,
                columns,
                pl.BlockSpec((group, depth, double), lambda i, *_: (i, 0, 0)),
            ],
            out_specs=[columns, columns],
            scratch_shapes=[pltpu.VMEM((2, tiles, 2 * samples, LANES), jnp.bfloat16)],
        ),
        out_shape=[jax.ShapeDtypeStruct(field.shape, jnp.float32)] * 2,
        name="product",
    )(cols, field, incoming, conductance, capacitance, weights)


def slope_columns(matrix, charges):
    samples = charges[0].shape[0]
    parts = [split(x) for x in charges]
    high = jnp.concatenate([h for h, _ in parts], axis=0)
    low = jnp.concatenate([l for _, l in parts], axis=0)
    first = jnp.dot(matrix, high, preferred_element_type=jnp.float32)
    second = jnp.dot(matrix[:samples], low, preferred_element_type=jnp.float32)
    return first[:samples] + first[samples:] + second


CHUNK = 512


def near_kernel(count, *refs):
    matrix_ref, p_ref = refs[:2]
    charge_refs, out_ref = refs[2 : 2 + count], refs[-1]
    matrix = matrix_ref[...]
    for start in range(0, p_ref.shape[1], CHUNK):
        inside = slice(start, start + CHUNK)
        out_ref[:, inside] = p_ref[:, inside] + slope_columns(matrix, [c[:, inside] for c in charge_refs])


def near(matrix, p, charges):
    return pl.pallas_call(
        functools.partial(near_kernel, len(charges)),
        in_specs=[whole()] * (2 + len(charges)),
        out_specs=whole(),
        out_shape=jax.ShapeDtypeStruct(p.shape, jnp.float32),
        name="near",
    )(matrix, p, *charges)


def far_send_kernel(count, *refs):
    send_ref = refs[0]
    u_ref, out_ref = refs[-2:]
    near_kernel(count, *refs[1:-1])
    gather_blocks(send_ref, u_ref, out_ref)


def far_send(send, matrix, p, charges, domains):
    samples = p.shape[0]
    slots = send.shape[0] // domains
    return pl.pallas_call(
        functools.partial(far_send_kernel, len(charges)),
        in_specs=[scalars()] + [whole()] * (2 + len(charges)),
        out_specs=[whole(), whole()],
        out_shape=[
            jax.ShapeDtypeStruct(p.shape, jnp.float32),
            jax.ShapeDtypeStruct((domains, samples, slots * HALF), jnp.float32),
        ],
        name="far_send",
    )(send, matrix, p, *charges)


def far_dots_kernel(count, *refs):
    matrix_ref, p_ref = refs[:2]
    charge_refs = refs[2 : 2 + count]
    r_ref, u_ref, out_ref = refs[2 + count :]
    matrix = matrix_ref[...]
    samples, unknowns = p_ref.shape
    totals = [jnp.zeros((samples, LANES), jnp.float32) for _ in range(5)]
    for start in range(0, unknowns, CHUNK):
        inside = slice(start, start + CHUNK)
        v = p_ref[:, inside] + slope_columns(matrix, [c[:, inside] for c in charge_refs])
        for i in range(0, CHUNK, LANES):
            vv = v[:, i : i + LANES]
            rr = r_ref[:, start + i : start + i + LANES]
            uu = u_ref[:, start + i : start + i + LANES]
            for n, (a, b) in enumerate(((uu, uu), (uu, vv), (vv, vv), (rr, uu), (rr, vv))):
                totals[n] = totals[n] + a * b
    row = lax.broadcasted_iota(jnp.int32, (SUMS, LANES), 0)
    packed = jnp.zeros((SUMS, LANES), jnp.float32)
    for n, total in enumerate(totals):
        packed = jnp.where(row == n, jnp.sum(total), packed)
    for d in range(out_ref.shape[0]):
        out_ref[d] = packed


def far_dots(matrix, p, charges, r, u, devices):
    return pl.pallas_call(
        functools.partial(far_dots_kernel, len(charges)),
        in_specs=[whole()] * (4 + len(charges)),
        out_specs=whole(),
        out_shape=jax.ShapeDtypeStruct((devices, SUMS, LANES), jnp.float32),
        name="far_dots",
    )(matrix, p, *charges, r, u)


def update_kernel(sums_ref, r_ref, u_ref, out_ref):
    total = sums_ref[0]
    for d in range(1, sums_ref.shape[0]):
        total = total + sums_ref[d]
    uu, uv, vv, ru, rv = [total[n : n + 1, :] for n in range(5)]
    length_u = jnp.sqrt(uu)
    length_v = jnp.sqrt(vv)
    cross = uv / length_u / length_v
    target_u = ru / length_u
    target_v = rv / length_v
    determinant = 1.0 - cross * cross
    weight_r = (target_u - cross * target_v) / determinant / length_u
    weight_u = (target_v - cross * target_u) / determinant / length_v
    for start in range(0, r_ref.shape[1], LANES):
        inside = slice(start, start + LANES)
        out_ref[:, inside] = weight_r * r_ref[:, inside] + weight_u * u_ref[:, inside]


def update(sums, r, u):
    return pl.pallas_call(
        update_kernel,
        in_specs=[whole()] * 3,
        out_specs=whole(),
        out_shape=jax.ShapeDtypeStruct(r.shape, jnp.float32),
        name="update",
    )(sums, r, u)


def body(residual, conductance, capacitance, stamps, block_cols, send_blocks):
    samples, unknowns = residual.shape
    rows, per_entry = block_cols.shape
    width = stamps.shape[2]
    domains = lax.axis_size("dom")
    groups = lax.axis_size("samp")
    period = samples * groups
    me = lax.axis_index("samp")
    send = send_blocks.reshape(-1)
    cols = block_cols.reshape(-1)
    pairs = [(i, i ^ 1) for i in range(groups)]
    partner = me + 1 - 2 * (me % 2)
    near_matrix = spectral_rows(me, [me, partner], samples, period)
    shifts = range(2, groups, 2)
    far_sources = [s for k in shifts for s in ((me - k) % groups, (partner - k) % groups)]
    far_matrix = spectral_rows(me, far_sources, samples, period)

    def exchange(outgoing):
        return lax.all_to_all(outgoing, "dom", split_axis=0, concat_axis=0, tiled=True)

    def apply(field, incoming, weights):
        p, q = product(cols, field, incoming, conductance, capacitance, weights)
        far = []
        for k in shifts:
            there = lax.ppermute(q, "samp", [(i, (i + k) % groups) for i in range(groups)])
            far.append(there)
        mate = lax.ppermute(q, "samp", pairs)
        p = near(near_matrix, p, [q, mate])
        charges = []
        for there in far:
            charges += [there, lax.ppermute(there, "samp", pairs)]
        return p, charges

    outgoing = send_call(send, residual, domains)
    incoming = exchange(outgoing)
    weights = prepare(stamps.reshape(rows, per_entry * width, 2 * width))
    p, charges = apply(residual, incoming, weights)
    u, outgoing = far_send(send, far_matrix, p, charges, domains)
    incoming = exchange(outgoing)
    p, charges = apply(u, incoming, weights)
    sums = far_dots(far_matrix, p, charges, residual, u, domains * groups)
    sums = lax.all_to_all(sums, ("dom", "samp"), split_axis=0, concat_axis=0, tiled=True)
    return update(sums, residual, u)


def solution(mesh):
    in_specs = (
        P("samp", "dom"),
        P("samp", "dom"),
        P("samp", "dom"),
        P("dom", None, None, None),
        P("dom", None),
        P("dom", None, None),
    )
    out_specs = P("samp", "dom")
    return jax.shard_map(body, mesh=mesh, in_specs=in_specs, out_specs=out_specs, check_vma=False)
```

```python
import functools

import jax
import jax.numpy as jnp
from jax import lax
from jax.experimental import pallas as pl
from jax.experimental.pallas import tpu as pltpu
from jax.sharding import PartitionSpec as P

LANES = 128
HALF = 64
GROUP = 8
SUMS = 8


LIMIT = 24 * 1024 * 1024


def whole():
    return pl.BlockSpec(memory_space=pltpu.VMEM)


def scalars():
    return pl.BlockSpec(memory_space=pltpu.SMEM)


def near_memory(x):
    return pltpu.with_memory_space_constraint(x, pltpu.VMEM)


def kernel_call(kernel, name, inputs, outputs, aliases=None, hbm=()):
    specs = []
    operands = []
    for x in inputs:
        if x.dtype == jnp.int32:
            specs.append(scalars())
            operands.append(x)
        else:
            specs.append(whole())
            operands.append(near_memory(x))
    out = [
        jax.ShapeDtypeStruct(shape, dtype) if n in hbm else pltpu.VMEM(shape, dtype)
        for n, (shape, dtype) in enumerate(outputs)
    ]
    return pl.pallas_call(
        kernel,
        in_specs=specs,
        out_specs=[whole()] * len(outputs),
        out_shape=out,
        input_output_aliases=aliases or {},
        compiler_params=pltpu.CompilerParams(vmem_limit_bytes=LIMIT),
        name=name,
    )(*operands)


def split(x):
    high = x.astype(jnp.bfloat16)
    low = (x - high.astype(jnp.float32)).astype(jnp.bfloat16)
    return high, low


def spectral_rows(me, sources, samples, period):
    row = me * samples + lax.broadcasted_iota(jnp.int32, (samples, samples), 0)
    column = lax.broadcasted_iota(jnp.int32, (samples, samples), 1)
    blocks = []
    for source in sources:
        offset = row - (source * samples + column)
        parity = (offset % 2).astype(jnp.float32)
        sign = 1.0 - 2.0 * parity
        angle = jnp.pi / period * offset.astype(jnp.float32)
        nonzero = offset != 0
        safe = jnp.where(nonzero, angle, 0.5)
        value = sign * jnp.cos(safe) / jnp.sin(safe) / period
        blocks.append(jnp.where(nonzero, value, 0.0))
    exact = jnp.concatenate(blocks, axis=1)
    high = lax.reduce_precision(exact, exponent_bits=8, mantissa_bits=7)
    return jnp.concatenate([high, exact - high], axis=0).astype(jnp.bfloat16)


def prepare_kernel(stamps_ref, out_ref):
    group, _, width = stamps_ref.shape
    rows = pl.ds(pl.program_id(0) * group, group)
    high, low = split(stamps_ref[...])
    out_ref[rows, :, :width] = high
    out_ref[rows, :, width:] = low


def prepare(stamps):
    rows, depth, width = stamps.shape
    return pl.pallas_call(
        prepare_kernel,
        grid=(rows // GROUP,),
        in_specs=[pl.BlockSpec((GROUP, depth, width), lambda i: (i, 0, 0))],
        out_specs=whole(),
        out_shape=pltpu.VMEM((rows, depth, 2 * width), jnp.bfloat16),
        compiler_params=pltpu.CompilerParams(vmem_limit_bytes=LIMIT),
        name="prepare",
    )(stamps)


def gather_blocks(send_ref, field_ref, out_ref):
    domains, samples, wide = out_ref.shape
    slots = wide // HALF
    lane = lax.broadcasted_iota(jnp.int32, (samples, LANES), 1)

    def placed(block, upper):
        start = pl.multiple_of((block // 2) * LANES, LANES)
        tile = field_ref[:, pl.ds(start, LANES)]
        turned = pltpu.roll(tile, HALF, 1)
        return jnp.where((block % 2) == upper, tile, turned)

    for d in range(domains):
        for j in range(0, slots, 2):
            first = placed(send_ref[d * slots + j], 0)
            second = placed(send_ref[d * slots + j + 1], 1)
            out_ref[d, :, j * HALF : j * HALF + LANES] = jnp.where(lane < HALF, first, second)


def extend_kernel(field_ref, inc_ref, ext):
    own_tiles = field_ref.shape[1] // LANES
    domains, _, wide = inc_ref.shape
    per_domain = wide // LANES

    def store(index, x):
        high, low = split(x)
        ext[0, index] = jnp.concatenate([high, low], axis=0)
        high, low = split(pltpu.roll(x, HALF, 1))
        ext[1, index] = jnp.concatenate([high, low], axis=0)

    for i in range(own_tiles):
        store(i, field_ref[:, i * LANES : (i + 1) * LANES])
    for d in range(domains):
        for j in range(per_domain):
            store(own_tiles + d * per_domain + j, inc_ref[d, :, j * LANES : (j + 1) * LANES])


def product_kernel(first_row, cols_ref, field_ref, ext, g_ref, c_ref, w_ref, p_ref, q_ref):
    samples = field_ref.shape[0]
    per_entry = w_ref.shape[1] // HALF
    lane = lax.broadcasted_iota(jnp.int32, (2 * samples, LANES), 1)
    low_lane = lax.broadcasted_iota(jnp.int32, (samples, LANES), 1) < HALF

    def row_product(row):
        parts = []
        for k in range(0, per_entry, 2):
            first = cols_ref[row * per_entry + k]
            second = cols_ref[row * per_entry + k + 1]
            a = ext[first % 2, first // 2]
            b = ext[1 - second % 2, second // 2]
            parts.append(jnp.where(lane < HALF, a, b))
        left = jnp.concatenate(parts, axis=1)
        full = jnp.dot(left, w_ref[row], preferred_element_type=jnp.float32)
        width = full.shape[1] // 2
        rows = full[:, :width] + full[:, width:]
        return rows[:samples] + rows[samples:]

    def block(step, carry):
        for pair in range(GROUP // 2):
            row = first_row + step * GROUP + 2 * pair
            first = row_product(row)
            second = row_product(row + 1)
            direct = jnp.where(low_lane, first, pltpu.roll(second, HALF, 1))
            charge = jnp.where(low_lane, pltpu.roll(first, HALF, 1), second)
            here = pl.ds(pl.multiple_of(step * GROUP * HALF + pair * LANES, LANES), LANES)
            there = pl.ds(pl.multiple_of(first_row * HALF + step * GROUP * HALF + pair * LANES, LANES), LANES)
            own = field_ref[:, there]
            p_ref[:, here] = direct + g_ref[:, there] * own
            q_ref[:, here] = charge + c_ref[:, there] * own
        return carry

    lax.fori_loop(0, p_ref.shape[1] // (GROUP * HALF), block, 0)


def slope_columns(matrix, charges):
    samples = charges[0].shape[0]
    parts = [split(x) for x in charges]
    high = jnp.concatenate([h for h, _ in parts], axis=0)
    low = jnp.concatenate([l for _, l in parts], axis=0)
    first = jnp.dot(matrix, high, preferred_element_type=jnp.float32)
    second = jnp.dot(matrix[:samples], low, preferred_element_type=jnp.float32)
    return first[:samples] + first[samples:] + second


CHUNK = 512


def near_kernel(chunks, *refs):
    matrix = refs[0][...]
    p_refs, q_refs, mate_refs, out_refs = [refs[1 + n * chunks : 1 + (n + 1) * chunks] for n in range(4)]
    for p_ref, q_ref, mate_ref, out_ref in zip(p_refs, q_refs, mate_refs, out_refs):
        for start in range(0, p_ref.shape[1], CHUNK):
            inside = slice(start, start + CHUNK)
            out_ref[:, inside] = p_ref[:, inside] + slope_columns(matrix, [q_ref[:, inside], mate_ref[:, inside]])


def far_columns(matrix, p_ref, charge_refs):
    for start in range(0, p_ref.shape[1], CHUNK):
        inside = slice(start, start + CHUNK)
        yield start, p_ref[:, inside] + slope_columns(matrix, [c[:, inside] for c in charge_refs])


def far_kernel(count, *refs):
    matrix = refs[0][...]
    out_ref = refs[-1]
    groups = [refs[i : i + 1 + count] for i in range(1, len(refs) - 1, 1 + count)]
    base = 0
    for p_ref, *charge_refs in groups:
        for start, value in far_columns(matrix, p_ref, charge_refs):
            out_ref[:, base + start : base + start + CHUNK] = value
        base += p_ref.shape[1]


def far_send_kernel(count, send_ref, matrix_ref, p_ref, *refs):
    charge_refs = refs[:count]
    u_ref, out_ref = refs[-2:]
    base = u_ref.shape[1] - p_ref.shape[1]
    for start, value in far_columns(matrix_ref[...], p_ref, charge_refs):
        u_ref[:, base + start : base + start + CHUNK] = value
    gather_blocks(send_ref, u_ref, out_ref)


def dot_totals(totals, r_ref, u_ref, base, v):
    for i in range(0, v.shape[1], LANES):
        vv = v[:, i : i + LANES]
        rr = r_ref[:, base + i : base + i + LANES]
        uu = u_ref[:, base + i : base + i + LANES]
        for n, (a, b) in enumerate(((uu, uu), (uu, vv), (vv, vv), (rr, uu), (rr, vv))):
            totals[n] = totals[n] + a * b


def far_dots_kernel(count, *refs):
    matrix = refs[0][...]
    r_ref, u_ref, out_ref = refs[-3:]
    groups = [refs[i : i + 1 + count] for i in range(1, len(refs) - 3, 1 + count)]
    totals = [jnp.zeros((r_ref.shape[0], LANES), jnp.float32) for _ in range(5)]
    base = 0
    for p_ref, *charge_refs in groups:
        for start, value in far_columns(matrix, p_ref, charge_refs):
            dot_totals(totals, r_ref, u_ref, base + start, value)
        base += p_ref.shape[1]
    for n in range(5):
        out_ref[n] = totals[n]


def last_dots_kernel(count, matrix_ref, p_ref, *refs):
    charge_refs = refs[:count]
    r_ref, u_ref, before_ref, out_ref = refs[count:]
    totals = [before_ref[n] for n in range(5)]
    base = u_ref.shape[1] - p_ref.shape[1]
    for start, value in far_columns(matrix_ref[...], p_ref, charge_refs):
        dot_totals(totals, r_ref, u_ref, base + start, value)
    row = lax.broadcasted_iota(jnp.int32, (SUMS, LANES), 0)
    packed = jnp.zeros((SUMS, LANES), jnp.float32)
    for n, total in enumerate(totals):
        packed = jnp.where(row == n, jnp.sum(total), packed)
    for d in range(out_ref.shape[0]):
        out_ref[d] = packed


def update_kernel(sums_ref, r_ref, u_ref, out_ref):
    total = sums_ref[0]
    for d in range(1, sums_ref.shape[0]):
        total = total + sums_ref[d]
    uu, uv, vv, ru, rv = [total[n : n + 1, :] for n in range(5)]
    length_u = jnp.sqrt(uu)
    length_v = jnp.sqrt(vv)
    cross = uv / length_u / length_v
    target_u = ru / length_u
    target_v = rv / length_v
    determinant = 1.0 - cross * cross
    weight_r = (target_u - cross * target_v) / determinant / length_u
    weight_u = (target_v - cross * target_u) / determinant / length_v
    for start in range(0, r_ref.shape[1], LANES):
        inside = slice(start, start + LANES)
        out_ref[:, inside] = weight_r * r_ref[:, inside] + weight_u * u_ref[:, inside]


SHARES = (1, 2, 3, 2)


def body(residual, conductance, capacitance, stamps, block_cols, send_blocks):
    samples, unknowns = residual.shape
    rows, per_entry = block_cols.shape
    width = stamps.shape[2]
    slots = send_blocks.shape[2]
    domains = lax.axis_size("dom")
    groups = lax.axis_size("samp")
    period = samples * groups
    me = lax.axis_index("samp")
    send = send_blocks.reshape(-1)
    cols = block_cols.reshape(-1)
    pairs = [(i, i ^ 1) for i in range(groups)]
    partner = me + 1 - 2 * (me % 2)
    near_matrix = spectral_rows(me, [me, partner], samples, period)
    shifts = range(2, groups, 2)
    count = 2 * len(shifts)
    far_sources = [s for k in shifts for s in ((me - k) % groups, (partner - k) % groups)]
    far_matrix = spectral_rows(me, far_sources, samples, period)
    unit = rows // sum(SHARES)
    sizes = [unit * share for share in SHARES]
    f32 = jnp.float32
    outgoing_shape = ((domains, samples, slots * width), f32)
    field_shape = ((samples, unknowns), f32)

    def exchange(outgoing):
        return lax.all_to_all(outgoing, "dom", split_axis=0, concat_axis=0, tiled=True)

    def apply(field, incoming, weights):
        tiles = unknowns // LANES + domains * slots * width // LANES
        (ext,) = kernel_call(
            extend_kernel, "extend", (field, incoming), [((2, tiles, 2 * samples, LANES), jnp.bfloat16)]
        )
        direct, charge, mates, far = [], [], [], []
        first = 0
        for n, size in enumerate(sizes):
            shape = ((samples, size * width), f32)
            p, q = kernel_call(
                functools.partial(product_kernel, first),
                f"product_{n}",
                (cols, field, ext, conductance, capacitance, weights),
                [shape, shape],
            )
            first += size
            direct.append(p)
            charge.append(q)
            with jax.named_scope(f"cross_{n}"):
                far.append([lax.ppermute(q, "samp", [(i, (i + k) % groups) for i in range(groups)]) for k in shifts])
            with jax.named_scope(f"mate_{n}"):
                mates.append(lax.ppermute(q, "samp", pairs))
        direct = kernel_call(
            functools.partial(near_kernel, len(sizes)),
            "near",
            (near_matrix, *direct, *charge, *mates),
            [(p.shape, f32) for p in direct],
        )
        pieces = []
        for n, there in enumerate(far):
            charges = []
            for x in there:
                with jax.named_scope(f"forward_{n}"):
                    charges += [x, lax.ppermute(x, "samp", pairs)]
            pieces.append((direct[n], *charges))
        return pieces

    (outgoing,) = kernel_call(gather_blocks, "gather_blocks", (send, residual), [outgoing_shape])
    incoming = exchange(outgoing)
    weights = prepare(stamps.reshape(rows, per_entry * width, 2 * width))
    pieces = apply(residual, incoming, weights)
    (u,) = kernel_call(
        functools.partial(far_kernel, count), "far", (far_matrix, *[x for piece in pieces[:-1] for x in piece]), [field_shape]
    )
    u, outgoing = kernel_call(
        functools.partial(far_send_kernel, count),
        "far_send",
        (send, far_matrix, *pieces[-1], u),
        [field_shape, outgoing_shape],
        aliases={3 + count: 0},
    )
    incoming = exchange(outgoing)
    pieces = apply(u, incoming, weights)
    (sums,) = kernel_call(
        functools.partial(far_dots_kernel, count),
        "far_dots",
        (far_matrix, *[x for piece in pieces[:-1] for x in piece], residual, u),
        [((5, samples, LANES), f32)],
    )
    (sums,) = kernel_call(
        functools.partial(last_dots_kernel, count),
        "last_dots",
        (far_matrix, *pieces[-1], residual, u, sums),
        [((domains * groups, SUMS, LANES), f32)],
    )
    sums = lax.all_to_all(sums, ("dom", "samp"), split_axis=0, concat_axis=0, tiled=True)
    (out,) = kernel_call(update_kernel, "update", (sums, residual, u), [field_shape], hbm=(0,))
    return out


def solution(mesh):
    in_specs = (
        P("samp", "dom"),
        P("samp", "dom"),
        P("samp", "dom"),
        P("dom", None, None, None),
        P("dom", None),
        P("dom", None, None),
    )
    out_specs = P("samp", "dom")
    return jax.shard_map(body, mesh=mesh, in_specs=in_specs, out_specs=out_specs, check_vma=False)
```

```python
import functools

import jax
import jax.numpy as jnp
from jax import lax
from jax.experimental import pallas as pl
from jax.experimental.pallas import tpu as pltpu
from jax.sharding import PartitionSpec as P


LANES = 128
HALF = 64
GROUP = 4


LIMIT = 24 * 1024 * 1024


def whole():
    return pl.BlockSpec(memory_space=pltpu.VMEM)


def scalars():
    return pl.BlockSpec(memory_space=pltpu.SMEM)


def near_memory(x):
    return pltpu.with_memory_space_constraint(x, pltpu.VMEM)


def far_memory(x):
    return pltpu.with_memory_space_constraint(x, pltpu.HBM)


def kernel_call(kernel, inputs, outputs, aliases=None, table_copied=False, scratch=(), far_first=False):
    specs = []
    operands = []
    for x in inputs:
        if x.dtype == jnp.int32 and table_copied:
            specs.append(pl.BlockSpec(memory_space=pl.ANY))
            operands.append(near_memory(x))
            scratch = (*scratch, pltpu.SMEM(x.shape, x.dtype), pltpu.SemaphoreType.DMA)
        elif x.dtype == jnp.int32:
            specs.append(scalars())
            operands.append(x)
        elif far_first and not specs:
            specs.append(pl.BlockSpec(memory_space=pl.ANY))
            operands.append(far_memory(x))
        else:
            specs.append(whole())
            operands.append(near_memory(x))
    integer = [dtype == jnp.int32 for _, dtype in outputs]
    out = [
        jax.ShapeDtypeStruct(shape, dtype) if number else pltpu.VMEM(shape, dtype)
        for (shape, dtype), number in zip(outputs, integer)
    ]
    return pl.pallas_call(
        kernel,
        in_specs=specs,
        out_specs=[scalars() if number else whole() for number in integer],
        out_shape=out,
        input_output_aliases=aliases or {},
        scratch_shapes=scratch,
        compiler_params=pltpu.CompilerParams(vmem_limit_bytes=LIMIT),
    )(*operands)


def split(x):
    high = x.astype(jnp.bfloat16)
    low = (x - high.astype(jnp.float32)).astype(jnp.bfloat16)
    return high, low


def spectral_rows(me, sources, samples, period):
    row = me * samples + lax.broadcasted_iota(jnp.int32, (samples, samples), 0)
    column = lax.broadcasted_iota(jnp.int32, (samples, samples), 1)
    blocks = []
    for source in sources:
        offset = row - (source * samples + column)
        sign = (1 - 2 * (offset & 1)).astype(jnp.float32)
        angle = jnp.pi / period * offset.astype(jnp.float32)
        nonzero = offset != 0
        safe = jnp.where(nonzero, angle, 0.5)
        value = sign * jnp.cos(safe) / jnp.sin(safe) / period
        blocks.append(jnp.where(nonzero, value, 0.0))
    high, low = split(jnp.concatenate(blocks, axis=1))
    return jnp.concatenate([high, low], axis=0)


def tables_kernel(groups, near_ref, far_ref):
    samples = near_ref.shape[1] // 2
    me = lax.axis_index("samp")
    partner = me + 1 - 2 * (me & 1)
    near_ref[...] = spectral_rows(me, [me, partner], samples, samples * groups)
    far = []
    for k in range(2, groups, 2):
        for source in (me - k, partner - k):
            far.append(jnp.where(source < 0, source + groups, source))
    far_ref[...] = spectral_rows(me, far, samples, samples * groups)


def load_stamps(first_row, stamps_hbm, perm_ref, out_ref, buffer, sems, meanwhile=None):
    rows, _, width = out_ref.shape
    copies = []
    for n in range(rows):
        source = stamps_hbm.at[perm_ref[first_row + n]]
        copies.append(pltpu.make_async_copy(source, buffer.at[n], sems.at[n]))
        copies[-1].start()
    if meanwhile is not None:
        meanwhile()
    for n, copy in enumerate(copies):
        copy.wait()
        high, low = split(buffer[n])
        out_ref[n, :, : width // 2] = high
        out_ref[n, :, width // 2 :] = low


def prepare_first_kernel(stamps_hbm, perm_ref, inv_ref, cols_ref, send_ref, out_ref, new_cols, new_send, buffer, sems):
    per_entry, rows = cols_ref.shape

    def tables():
        def one_row(i, carry):
            for k in range(per_entry):
                entry = cols_ref[k, perm_ref[i]]
                own = inv_ref[jnp.minimum(entry, rows - 1)]
                new_cols[k, i] = jnp.where(entry < rows, own, entry)
            return carry

        lax.fori_loop(0, rows, one_row, 0, unroll=2)
        for j in range(send_ref.shape[0]):
            for d in range(send_ref.shape[1]):
                new_send[j, d] = inv_ref[send_ref[j, d]]

    load_stamps(0, stamps_hbm, perm_ref, out_ref, buffer, sems, tables)


def prepare_rest_kernel(first_row, stamps_hbm, perm_ref, out_ref, buffer, sems):
    load_stamps(first_row, stamps_hbm, perm_ref, out_ref, buffer, sems)


def pair_tile(ref, first, second):
    samples = ref.shape[0]
    lane = lax.broadcasted_iota(jnp.int32, (samples, LANES), 1)

    def placed(block, upper):
        start = pl.multiple_of((block // 2) * LANES, LANES)
        tile = ref[:, pl.ds(start, LANES)]
        turned = pltpu.roll(tile, HALF, 1)
        return jnp.where((block & 1) == upper, tile, turned)

    return jnp.where(lane < HALF, placed(first, 0), placed(second, 1))


def gather_blocks(targets, send_ref, field_ref, out_refs):
    slots = send_ref.shape[0]
    for d, out_ref in zip(targets, out_refs):
        for j in range(0, slots, 2):
            out_ref[:, j * HALF : j * HALF + LANES] = pair_tile(field_ref, send_ref[j, d], send_ref[j + 1, d])


def halo_offsets(domains):
    return sorted(range(1, domains), key=lambda k: (-(k >= domains // 2), k if k >= domains // 2 else -k))


def few(domains):
    return domains <= 8 and domains & (domains - 1) == 0


def gather_all(domains, send_ref, field_ref, out_refs):
    if few(domains):
        me = lax.axis_index("dom")
        gather_blocks([me ^ k for k in halo_offsets(domains)], send_ref, field_ref, out_refs)
    else:
        gather_blocks(range(domains), send_ref, field_ref, [out_refs[0].at[d] for d in range(domains)])


COPIES = 4


def order_rows(domains, send_ref, perm_ref, inv_ref, flags):
    rows = perm_ref.shape[0]
    if not few(domains):

        def keep(row, carry):
            perm_ref[row] = row
            inv_ref[row] = row
            return carry

        lax.fori_loop(0, rows, keep, 0)
        return
    me = lax.axis_index("dom")

    def clear(row, carry):
        flags[row] = 0
        return carry

    lax.fori_loop(0, rows + 1, clear, 0, unroll=5)
    for d in range(domains):
        for j in range(send_ref.shape[0]):
            flags[jnp.where(d == me, rows, send_ref[j, d])] = 1

    sent = lax.fori_loop(0, rows, lambda row, total: total + flags[row], 0, unroll=4)

    def place(row, carry):
        first, later = carry
        flag = flags[row]
        position = jnp.where(flag == 1, first, later)
        inv_ref[row] = position
        perm_ref[position] = row
        return first + flag, later + 1 - flag

    lax.fori_loop(0, rows, place, (jnp.int32(0), sent), unroll=4)


def gather_kernel(domains, send_hbm, field_hbm, field_ref, perm_ref, inv_ref, *refs):
    *out_refs, field_sem, send_ref, send_sem, flags = refs
    table = pltpu.make_async_copy(send_hbm, send_ref, send_sem)
    table.start()
    width = field_ref.shape[1] // COPIES
    copies = []
    for n in range(COPIES):
        inside = pl.ds(n * width, width)
        copies.append(pltpu.make_async_copy(field_hbm.at[:, inside], field_ref.at[:, inside], field_sem.at[n]))
        copies[-1].start()
    table.wait()
    order_rows(domains, send_ref, perm_ref, inv_ref, flags)
    for copy in copies:
        copy.wait()
    gather_all(domains, send_ref, field_ref, out_refs)


def gather(send, field, rows, domains, outputs):
    table = jax.ShapeDtypeStruct((rows,), jnp.int32)
    return pl.pallas_call(
        functools.partial(gather_kernel, domains),
        in_specs=[pl.BlockSpec(memory_space=pl.ANY)] * 2,
        out_specs=[whole(), scalars(), scalars()] + [whole()] * len(outputs),
        out_shape=[
            pltpu.VMEM(field.shape, field.dtype),
            table,
            table,
            *[pltpu.VMEM(shape, dtype) for shape, dtype in outputs],
        ],
        scratch_shapes=[
            pltpu.SemaphoreType.DMA((COPIES,)),
            pltpu.SMEM(send.shape, send.dtype),
            pltpu.SemaphoreType.DMA,
            pltpu.SMEM((rows + 8,), jnp.int32),
        ],
        compiler_params=pltpu.CompilerParams(vmem_limit_bytes=LIMIT),
        name="gather",
    )(far_memory(send), far_memory(field))


def store_tile(ext, index, x):
    high, low = split(x)
    ext[0, index] = jnp.concatenate([high, low], axis=0)
    high, low = split(pltpu.roll(x, HALF, 1))
    ext[1, index] = jnp.concatenate([high, low], axis=0)


def arrange_kernel(perm_ref, field_ref, g_ref, c_ref, field_out, g_out, c_out, ext):
    for i in range(field_ref.shape[1] // LANES):
        inside = slice(i * LANES, (i + 1) * LANES)
        first, second = perm_ref[2 * i], perm_ref[2 * i + 1]
        tile = pair_tile(field_ref, first, second)
        field_out[:, inside] = tile
        store_tile(ext, i, tile)
        g_out[:, inside] = pair_tile(g_ref, first, second)
        c_out[:, inside] = pair_tile(c_ref, first, second)


def extend_kernel(field_ref, ext):
    for i in range(field_ref.shape[1] // LANES):
        store_tile(ext, i, field_ref[:, i * LANES : (i + 1) * LANES])


def extend_arrived(domains, own_tiles, inc_refs, ext):
    if few(domains):
        me = lax.axis_index("dom")
        arrived = [(me ^ k, ref) for k, ref in zip(halo_offsets(domains), inc_refs)]
    else:
        arrived = [(d, inc_refs[0].at[d]) for d in range(domains)]
    for source, ref in arrived:
        per_domain = ref.shape[1] // LANES
        for j in range(per_domain):
            store_tile(ext, own_tiles + source * per_domain + j, ref[:, j * LANES : (j + 1) * LANES])


def first_product_kernel(domains, cols_hbm, field_ref, own_ref, g_ref, c_ref, w_ref, *refs):
    *inc_refs, ext, p_ref, q_ref, cols_ref, cols_sem = refs
    table = pltpu.make_async_copy(cols_hbm, cols_ref, cols_sem)
    table.start()
    extend_arrived(domains, field_ref.shape[1] // LANES, inc_refs, ext)
    table.wait()
    product_kernel(0, 0, cols_ref, field_ref, ext, g_ref, c_ref, w_ref, p_ref, q_ref)


def product_kernel(first_row, weight_row, cols_ref, field_ref, ext, g_ref, c_ref, w_ref, p_ref, q_ref):
    samples = field_ref.shape[0]
    per_entry = cols_ref.shape[0]
    lane = lax.broadcasted_iota(jnp.int32, (2 * samples, LANES), 1)
    low_lane = lax.broadcasted_iota(jnp.int32, (samples, LANES), 1) < HALF

    def row_product(row):
        parts = []
        for k in range(0, per_entry, 2):
            first = cols_ref[k, row]
            second = cols_ref[k + 1, row]
            a = ext[first & 1, first // 2]
            b = ext[1 - (second & 1), second // 2]
            parts.append(jnp.where(lane < HALF, a, b))
        left = jnp.concatenate(parts, axis=1)
        full = jnp.dot(left, w_ref[row - weight_row], preferred_element_type=jnp.float32)
        width = full.shape[1] // 2
        rows = full[:, :width] + full[:, width:]
        return rows[:samples] + rows[samples:]

    def block(step, carry):
        for pair in range(GROUP // 2):
            row = first_row + step * GROUP + 2 * pair
            first = row_product(row)
            second = row_product(row + 1)
            direct = jnp.where(low_lane, first, pltpu.roll(second, HALF, 1))
            charge = jnp.where(low_lane, pltpu.roll(first, HALF, 1), second)
            here = pl.ds(pl.multiple_of(step * GROUP * HALF + pair * LANES, LANES), LANES)
            there = pl.ds(pl.multiple_of(first_row * HALF + step * GROUP * HALF + pair * LANES, LANES), LANES)
            own = field_ref[:, there]
            p_ref[:, here] = direct + g_ref[:, there] * own
            q_ref[:, here] = charge + c_ref[:, there] * own
        return carry

    lax.fori_loop(0, p_ref.shape[1] // (GROUP * HALF), block, 0)


def slope_columns(matrix, charges):
    samples = charges[0].shape[0]
    parts = [split(x) for x in charges]
    high = jnp.concatenate([h for h, _ in parts], axis=0)
    low = jnp.concatenate([l for _, l in parts], axis=0)
    first = jnp.dot(matrix, high, preferred_element_type=jnp.float32)
    second = jnp.dot(matrix[:samples], low, preferred_element_type=jnp.float32)
    return first[:samples] + first[samples:] + second


CHUNK = 256


def near_kernel(chunks, *refs):
    matrix = refs[0][...]
    p_refs, q_refs, mate_refs, out_refs = [refs[1 + n * chunks : 1 + (n + 1) * chunks] for n in range(4)]
    for p_ref, q_ref, mate_ref, out_ref in zip(p_refs, q_refs, mate_refs, out_refs):
        for start in range(0, p_ref.shape[1], CHUNK):
            inside = slice(start, start + CHUNK)
            out_ref[:, inside] = p_ref[:, inside] + slope_columns(matrix, [q_ref[:, inside], mate_ref[:, inside]])


def far_columns(matrix, p_ref, charge_refs):
    for start in range(0, p_ref.shape[1], CHUNK):
        inside = slice(start, start + CHUNK)
        yield start, p_ref[:, inside] + slope_columns(matrix, [c[:, inside] for c in charge_refs])


def far_kernel(count, base, chunks, *refs):
    matrix = refs[0][...]
    out_ref = refs[-1]
    size = 1 + count
    for n in range(chunks):
        p_ref, *charge_refs = refs[1 + n * size : 1 + (n + 1) * size]
        for start, value in far_columns(matrix, p_ref, charge_refs):
            out_ref[:, base + start : base + start + CHUNK] = value
        base += p_ref.shape[1]


def far_send_kernel(count, chunks, domains, send_near, *refs):
    size = 1 + count
    u_ref, *out_refs, send_ref, send_sem = refs[1 + chunks * size :]
    table = pltpu.make_async_copy(send_near, send_ref, send_sem)
    table.start()
    far_kernel(count, 0, chunks, *refs[: 1 + chunks * size], u_ref)
    table.wait()
    gather_all(domains, send_ref, u_ref, out_refs)


def dot_totals(totals, r_ref, u_ref, base, v):
    for i in range(0, v.shape[1], LANES):
        vv = v[:, i : i + LANES]
        rr = r_ref[:, base + i : base + i + LANES]
        uu = u_ref[:, base + i : base + i + LANES]
        for n, (a, b) in enumerate(((uu, uu), (uu, vv), (vv, vv), (rr, uu), (rr, vv))):
            totals[n] = totals[n] + a * b


def far_dots_kernel(count, base, chunks, *refs):
    matrix = refs[0][...]
    out_ref = refs[-1]
    size = 1 + count
    r_ref, u_ref, *before = refs[1 + chunks * size : -1]
    samples = r_ref.shape[0]
    totals = [before[0][n] if before else jnp.zeros((samples, LANES), jnp.float32) for n in range(5)]
    for n in range(chunks):
        p_ref, *charge_refs = refs[1 + n * size : 1 + (n + 1) * size]
        for start, value in far_columns(matrix, p_ref, charge_refs):
            dot_totals(totals, r_ref, u_ref, base + start, value)
        base += p_ref.shape[1]
    if base < u_ref.shape[1]:
        for n in range(5):
            out_ref[n] = totals[n]
        return
    lane = lax.broadcasted_iota(jnp.int32, (1, LANES), 1)
    packed = jnp.zeros((1, LANES), jnp.float32)
    for n, total in enumerate(totals):
        packed = jnp.where(lane == n, jnp.sum(total), packed)
    for d in range(out_ref.shape[0]):
        out_ref[d] = packed


def update_kernel(inv_near, sums_ref, r_ref, u_ref, out_hbm, out_ref, sems, inv_ref, inv_sem):
    table = pltpu.make_async_copy(inv_near, inv_ref, inv_sem)
    table.start()
    total = jnp.sum(sums_ref[...], axis=0)
    lane = lax.broadcasted_iota(jnp.int32, total.shape, 1)
    uu, uv, vv, ru, rv = [jnp.sum(jnp.where(lane == n, total, 0.0), axis=1, keepdims=True) for n in range(5)]
    length_u = jnp.sqrt(uu)
    length_v = jnp.sqrt(vv)
    cross = uv / length_u / length_v
    target_u = ru / length_u
    target_v = rv / length_v
    determinant = 1.0 - cross * cross
    weight_r = (target_u - cross * target_v) / determinant / length_u
    weight_u = (target_v - cross * target_u) / determinant / length_v
    table.wait()
    width = r_ref.shape[1] // COPIES
    copies = []
    for n in range(COPIES):
        for start in range(n * width, (n + 1) * width, LANES):
            inside = slice(start, start + LANES)
            tile = pair_tile(u_ref, inv_ref[start // HALF], inv_ref[start // HALF + 1])
            out_ref[:, inside] = weight_r * r_ref[:, inside] + weight_u * tile
        inside = pl.ds(n * width, width)
        copies.append(pltpu.make_async_copy(out_ref.at[:, inside], out_hbm.at[:, inside], sems.at[n]))
        copies[-1].start()
    for copy in copies:
        copy.wait()


def update(inv, sums, r, u):
    return pl.pallas_call(
        update_kernel,
        in_specs=[pl.BlockSpec(memory_space=pl.ANY)] + [whole()] * 3,
        out_specs=pl.BlockSpec(memory_space=pl.ANY),
        out_shape=jax.ShapeDtypeStruct(r.shape, r.dtype),
        scratch_shapes=[
            pltpu.VMEM(r.shape, r.dtype),
            pltpu.SemaphoreType.DMA((COPIES,)),
            pltpu.SMEM(inv.shape, inv.dtype),
            pltpu.SemaphoreType.DMA,
        ],
        compiler_params=pltpu.CompilerParams(vmem_limit_bytes=LIMIT),
        name="update",
    )(near_memory(inv), near_memory(sums), near_memory(r), near_memory(u))


CHUNKS = 4


def chunk_sizes(rows, domains, slots):
    unit = rows // 8
    early = (domains - 1) * slots if few(domains) else 3 * unit
    return [unit, early - unit, rows - unit - early, unit]


def body(residual, conductance, capacitance, stamps, block_cols, send_blocks):
    samples, unknowns = residual.shape
    rows, per_entry = block_cols.shape
    width = stamps.shape[2]
    slots = send_blocks.shape[2]
    domains = lax.axis_size("dom")
    groups = lax.axis_size("samp")
    pairs = [(i, i ^ 1) for i in range(groups)]
    shifts = range(2, groups, 2)
    count = 2 * len(shifts)
    sizes = chunk_sizes(rows, domains, slots)
    f32 = jnp.float32
    if few(domains):
        outgoing_shapes = [((samples, slots * width), f32)] * (domains - 1)
    else:
        outgoing_shapes = [((domains, samples, slots * width), f32)]
    field_shape = ((samples, unknowns), f32)
    tiles = unknowns // LANES + domains * slots * width // LANES
    ext_shape = ((2, tiles, 2 * samples, LANES), jnp.bfloat16)

    def exchange(outgoing):
        if not few(domains):
            return [lax.all_to_all(outgoing[0], "dom", split_axis=0, concat_axis=0, tiled=True)]
        incoming = []
        for k, x in zip(halo_offsets(domains), outgoing):
            incoming.append(lax.ppermute(x, "dom", [(i, i ^ k) for i in range(domains)]))
        return incoming

    def charges_of(field, ext, incoming, cols, g, c, weights):
        direct, charge, mates, far = [], [], [], []
        first = 0
        for n, size in enumerate(sizes):
            shape = ((samples, size * width), f32)
            weight_row, weight = next((at, w) for at, w in reversed(weights) if at <= first)
            operands = (cols, field, ext, g, c, weight)
            if n == 0:
                ext, p, q = kernel_call(
                    functools.partial(first_product_kernel, domains),
                    operands + tuple(incoming),
                    [ext_shape, shape, shape],
                    aliases={2: 0},
                    table_copied=True,
                )
            else:
                p, q = kernel_call(functools.partial(product_kernel, first, weight_row), operands, [shape, shape])
            first += size
            direct.append(p)
            charge.append(q)
            far.append([lax.ppermute(q, "samp", [(i, (i + k) % groups) for i in range(groups)]) for k in shifts])
            mates.append(lax.ppermute(q, "samp", pairs))
        half = []
        for low, high in ((0, 2), (2, CHUNKS)):
            half += kernel_call(
                functools.partial(near_kernel, high - low),
                (near_matrix, *direct[low:high], *charge[low:high], *mates[low:high]),
                [(p.shape, f32) for p in direct[low:high]],
            )
        pieces = []
        for n, there in enumerate(far):
            charges = []
            for x in there:
                charges += [x, lax.ppermute(x, "samp", pairs)]
            pieces.append((half[n], *charges))
        return pieces

    starts = [sum(sizes[:n]) * width for n in range(CHUNKS)]

    cols = block_cols.T
    send = send_blocks[0].T
    field, perm, inv, *outgoing = gather(send, residual, rows, domains, outgoing_shapes)
    incoming = exchange(outgoing)
    blocks = stamps.reshape(rows, per_entry * width, 2 * width)
    early = sizes[0] + sizes[1]
    loading = lambda n: (pltpu.VMEM((n, *blocks.shape[1:]), f32), pltpu.SemaphoreType.DMA((n,)))
    weight_shape = lambda n: ((n, per_entry * width, 4 * width), jnp.bfloat16)
    first_weights, cols, send = kernel_call(
        prepare_first_kernel,
        (blocks, perm, inv, cols, send),
        [weight_shape(early), (cols.shape, jnp.int32), (send.shape, jnp.int32)],
        scratch=loading(early),
        far_first=True,
    )
    (other_weights,) = kernel_call(
        functools.partial(prepare_rest_kernel, early),
        (blocks, perm),
        [weight_shape(rows - early)],
        scratch=loading(rows - early),
        far_first=True,
    )
    weights = [(0, first_weights), (early, other_weights)]
    near_matrix, far_matrix = kernel_call(
        functools.partial(tables_kernel, groups),
        (),
        [((2 * samples, 2 * samples), jnp.bfloat16), ((2 * samples, count * samples), jnp.bfloat16)],
    )
    ordered, g, c, ext = kernel_call(
        arrange_kernel, (perm, field, conductance, capacitance), [field_shape] * 3 + [ext_shape]
    )
    pieces = charges_of(ordered, ext, incoming, cols, g, c, weights)
    ready = 2 if few(domains) else CHUNKS
    u, *outgoing = kernel_call(
        functools.partial(far_send_kernel, count, ready, domains),
        (send, far_matrix, *[x for piece in pieces[:ready] for x in piece]),
        [field_shape, *outgoing_shapes],
        table_copied=True,
    )
    incoming = exchange(outgoing)
    if ready < CHUNKS:
        operands = [far_matrix, *[x for piece in pieces[ready:] for x in piece]]
        (u,) = kernel_call(
            functools.partial(far_kernel, count, starts[ready], CHUNKS - ready),
            operands + [u],
            [field_shape],
            aliases={len(operands): 0},
        )
    (ext,) = kernel_call(extend_kernel, (u,), [ext_shape])
    pieces = charges_of(u, ext, incoming, cols, g, c, weights)
    sums = None
    steps = [(0, CHUNKS - 2), (CHUNKS - 2, CHUNKS - 1), (CHUNKS - 1, CHUNKS)]
    for n, (low, high) in enumerate(steps):
        operands = [far_matrix, *[x for piece in pieces[low:high] for x in piece], ordered, u]
        final = n == len(steps) - 1
        (sums,) = kernel_call(
            functools.partial(far_dots_kernel, count, starts[low], high - low),
            operands + [sums] * (n > 0),
            [((domains * groups, 1, LANES) if final else (5, samples, LANES), f32)],
        )
    sums = lax.all_to_all(sums, ("dom", "samp"), split_axis=0, concat_axis=0, tiled=True)
    return update(inv, sums, field, u)


def solution(mesh):
    in_specs = (
        P("samp", "dom"),
        P("samp", "dom"),
        P("samp", "dom"),
        P("dom", None, None, None),
        P("dom", None),
        P("dom", None, None),
    )
    out_specs = P("samp", "dom")
    return jax.shard_map(body, mesh=mesh, in_specs=in_specs, out_specs=out_specs, check_vma=False)
```

```python
import functools

import jax
import jax.numpy as jnp
from jax import lax
from jax.experimental import pallas as pl
from jax.experimental.pallas import tpu as pltpu
from jax.sharding import PartitionSpec as P


LANES = 128
HALF = 64
GROUP = 4


LIMIT = 24 * 1024 * 1024


def whole():
    return pl.BlockSpec(memory_space=pltpu.VMEM)


def scalars():
    return pl.BlockSpec(memory_space=pltpu.SMEM)


def near_memory(x):
    return pltpu.with_memory_space_constraint(x, pltpu.VMEM)


def far_memory(x):
    return pltpu.with_memory_space_constraint(x, pltpu.HBM)


def kernel_call(kernel, inputs, outputs, aliases=None, table_copied=False):
    specs = []
    operands = []
    scratch = []
    for x in inputs:
        if x.dtype == jnp.int32 and table_copied:
            specs.append(pl.BlockSpec(memory_space=pl.ANY))
            operands.append(near_memory(x))
            scratch += [pltpu.SMEM(x.shape, x.dtype), pltpu.SemaphoreType.DMA]
        elif x.dtype == jnp.int32:
            specs.append(scalars())
            operands.append(x)
        else:
            specs.append(whole())
            operands.append(near_memory(x))
    integer = [dtype == jnp.int32 for _, dtype in outputs]
    out = [
        jax.ShapeDtypeStruct(shape, dtype) if number else pltpu.VMEM(shape, dtype)
        for (shape, dtype), number in zip(outputs, integer)
    ]
    return pl.pallas_call(
        kernel,
        in_specs=specs,
        out_specs=[scalars() if number else whole() for number in integer],
        out_shape=out,
        input_output_aliases=aliases or {},
        scratch_shapes=scratch,
        compiler_params=pltpu.CompilerParams(vmem_limit_bytes=LIMIT),
    )(*operands)


def split(x):
    high = x.astype(jnp.bfloat16)
    low = (x - high.astype(jnp.float32)).astype(jnp.bfloat16)
    return high, low


def spectral_rows(me, sources, samples, period):
    row = me * samples + lax.broadcasted_iota(jnp.int32, (samples, samples), 0)
    column = lax.broadcasted_iota(jnp.int32, (samples, samples), 1)
    blocks = []
    for source in sources:
        offset = row - (source * samples + column)
        sign = (1 - 2 * (offset & 1)).astype(jnp.float32)
        angle = jnp.pi / period * offset.astype(jnp.float32)
        nonzero = offset != 0
        safe = jnp.where(nonzero, angle, 0.5)
        value = sign * jnp.cos(safe) / jnp.sin(safe) / period
        blocks.append(jnp.where(nonzero, value, 0.0))
    high, low = split(jnp.concatenate(blocks, axis=1))
    return jnp.concatenate([high, low], axis=0)


def tables_kernel(groups, near_ref, far_ref):
    samples = near_ref.shape[1] // 2
    me = lax.axis_index("samp")
    partner = me + 1 - 2 * (me & 1)
    near_ref[...] = spectral_rows(me, [me, partner], samples, samples * groups)
    far = []
    for k in range(2, groups, 2):
        for source in (me - k, partner - k):
            far.append(jnp.where(source < 0, source + groups, source))
    far_ref[...] = spectral_rows(me, far, samples, samples * groups)


def prepare_kernel(first_row, last_row, perm_ref, stamps_ref, *refs):
    out_ref = refs[-1]
    width = stamps_ref.shape[2]

    def convert(row, carry):
        high, low = split(stamps_ref[perm_ref[row]])
        out_ref[row, :, :width] = high
        out_ref[row, :, width:] = low
        return carry

    lax.fori_loop(first_row, last_row, convert, 0, unroll=2)


def fetch_kernel(perm_ref, stamps_hbm, out_ref, buffer, sems):
    rows, _, width = buffer.shape
    copies = []
    for n in range(rows):
        copies.append(pltpu.make_async_copy(stamps_hbm.at[perm_ref[n]], buffer.at[n], sems.at[n]))
        copies[-1].start()
    for n, copy in enumerate(copies):
        copy.wait()
        high, low = split(buffer[n])
        out_ref[n, :, :width] = high
        out_ref[n, :, width:] = low


def fetch(perm, stamps, rows):
    total, depth, width = stamps.shape
    return pl.pallas_call(
        fetch_kernel,
        in_specs=[scalars(), pl.BlockSpec(memory_space=pl.ANY)],
        out_specs=whole(),
        out_shape=pltpu.VMEM((total, depth, 2 * width), jnp.bfloat16),
        scratch_shapes=[pltpu.VMEM((rows, depth, width), stamps.dtype), pltpu.SemaphoreType.DMA((rows,))],
        compiler_params=pltpu.CompilerParams(vmem_limit_bytes=LIMIT),
        name="prepare_0",
    )(perm, far_memory(stamps))


def pair_tile(ref, first, second):
    samples = ref.shape[0]
    lane = lax.broadcasted_iota(jnp.int32, (samples, LANES), 1)

    def placed(block, upper):
        start = pl.multiple_of((block // 2) * LANES, LANES)
        tile = ref[:, pl.ds(start, LANES)]
        turned = pltpu.roll(tile, HALF, 1)
        return jnp.where((block & 1) == upper, tile, turned)

    return jnp.where(lane < HALF, placed(first, 0), placed(second, 1))


def gather_blocks(targets, send_ref, field_ref, out_refs, inv_ref=None):
    slots = send_ref.shape[0]
    for d, out_ref in zip(targets, out_refs):
        for j in range(0, slots, 2):
            first, second = send_ref[j, d], send_ref[j + 1, d]
            if inv_ref is not None:
                first, second = inv_ref[first], inv_ref[second]
            out_ref[:, j * HALF : j * HALF + LANES] = pair_tile(field_ref, first, second)


def halo_offsets(domains):
    return sorted(range(1, domains), key=lambda k: (-(k >= domains // 2), k if k >= domains // 2 else -k))


def few(domains):
    return domains <= 8 and domains & (domains - 1) == 0


def gather_all(domains, send_ref, field_ref, out_refs, inv_ref=None):
    if few(domains):
        me = lax.axis_index("dom")
        gather_blocks([me ^ k for k in halo_offsets(domains)], send_ref, field_ref, out_refs, inv_ref)
    else:
        gather_blocks(range(domains), send_ref, field_ref, [out_refs[0].at[d] for d in range(domains)], inv_ref)


COPIES = 4


WORD = 32


def order_rows(domains, send_ref, perm_ref, inv_ref):
    rows = perm_ref.shape[0]
    masks = [jnp.int32(0)] * (rows // WORD)
    if few(domains):
        me = lax.axis_index("dom")
        for d in range(domains):
            for j in range(send_ref.shape[0]):
                block = send_ref[j, d]
                bit = jnp.where(d == me, 0, jnp.left_shift(jnp.int32(1), block & (WORD - 1)))
                masks = [m | jnp.where(block // WORD == n, bit, 0) for n, m in enumerate(masks)]
    flags = [lax.shift_right_logical(masks[row // WORD], jnp.int32(row % WORD)) & 1 for row in range(rows)]
    first = jnp.int32(0)
    later = sum(flags)
    for row, flag in enumerate(flags):
        position = jnp.where(flag == 1, first, later)
        inv_ref[row] = position
        perm_ref[position] = row
        first = first + flag
        later = later + 1 - flag


def gather_kernel(domains, send_hbm, field_hbm, field_ref, perm_ref, inv_ref, *refs):
    *out_refs, field_sem, send_ref, send_sem = refs
    table = pltpu.make_async_copy(send_hbm, send_ref, send_sem)
    table.start()
    width = field_ref.shape[1] // COPIES
    copies = []
    for n in range(COPIES):
        inside = pl.ds(n * width, width)
        copies.append(pltpu.make_async_copy(field_hbm.at[:, inside], field_ref.at[:, inside], field_sem.at[n]))
        copies[-1].start()
    table.wait()
    order_rows(domains, send_ref, perm_ref, inv_ref)
    for copy in copies:
        copy.wait()
    gather_all(domains, send_ref, field_ref, out_refs)


def gather(send, field, rows, domains, outputs):
    table = jax.ShapeDtypeStruct((rows,), jnp.int32)
    return pl.pallas_call(
        functools.partial(gather_kernel, domains),
        in_specs=[pl.BlockSpec(memory_space=pl.ANY)] * 2,
        out_specs=[whole(), scalars(), scalars()] + [whole()] * len(outputs),
        out_shape=[
            pltpu.VMEM(field.shape, field.dtype),
            table,
            table,
            *[pltpu.VMEM(shape, dtype) for shape, dtype in outputs],
        ],
        scratch_shapes=[
            pltpu.SemaphoreType.DMA((COPIES,)),
            pltpu.SMEM(send.shape, send.dtype),
            pltpu.SemaphoreType.DMA,
        ],
        compiler_params=pltpu.CompilerParams(vmem_limit_bytes=LIMIT),
        name="gather",
    )(far_memory(send), far_memory(field))


def store_tile(ext, index, x):
    high, low = split(x)
    ext[0, index] = jnp.concatenate([high, low], axis=0)
    high, low = split(pltpu.roll(x, HALF, 1))
    ext[1, index] = jnp.concatenate([high, low], axis=0)


def arrange_kernel(first_row, perm_ref, field_ref, g_ref, c_ref, g_out, c_out):
    samples = field_ref.shape[0]
    lane = lax.broadcasted_iota(jnp.int32, (samples, LANES), 1)

    def placed(block, upper):
        here = pl.ds(pl.multiple_of((block // 2) * LANES, LANES), LANES)
        own = field_ref[:, here]
        keep = (block & 1) == upper
        return [jnp.where(keep, x, pltpu.roll(x, HALF, 1)) for x in (g_ref[:, here] * own, c_ref[:, here] * own)]

    for i in range(g_out.shape[1] // LANES):
        inside = slice(i * LANES, (i + 1) * LANES)
        low = placed(perm_ref[first_row + 2 * i], 0)
        high = placed(perm_ref[first_row + 2 * i + 1], 1)
        g_out[:, inside] = jnp.where(lane < HALF, low[0], high[0])
        c_out[:, inside] = jnp.where(lane < HALF, low[1], high[1])


def restore_kernel(inv_ref, u_ref, out_ref, ext):
    for i in range(u_ref.shape[1] // LANES):
        tile = pair_tile(u_ref, inv_ref[2 * i], inv_ref[2 * i + 1])
        out_ref[:, i * LANES : (i + 1) * LANES] = tile
        store_tile(ext, i, tile)


def extend_kernel(field_ref, ext):
    for i in range(field_ref.shape[1] // LANES):
        store_tile(ext, i, field_ref[:, i * LANES : (i + 1) * LANES])


def extend_arrived(domains, own_tiles, inc_refs, ext):
    if few(domains):
        me = lax.axis_index("dom")
        arrived = [(me ^ k, ref) for k, ref in zip(halo_offsets(domains), inc_refs)]
    else:
        arrived = [(d, inc_refs[0].at[d]) for d in range(domains)]
    for source, ref in arrived:
        per_domain = ref.shape[1] // LANES
        for j in range(per_domain):
            store_tile(ext, own_tiles + source * per_domain + j, ref[:, j * LANES : (j + 1) * LANES])


def with_arrived(domains, product, own_tiles, cols_near, order_near, *refs):
    *inputs, out_ext, p_ref, q_ref, cols_ref, cols_sem, order_ref, order_sem = refs
    tables = [
        pltpu.make_async_copy(cols_near, cols_ref, cols_sem),
        pltpu.make_async_copy(order_near, order_ref, order_sem),
    ]
    for table in tables:
        table.start()
    offsets = domains - 1 if few(domains) else 1
    own_ext, *inputs = inputs
    extend_arrived(domains, own_tiles, inputs[len(inputs) - offsets :], out_ext)
    for table in tables:
        table.wait()
    product(cols_ref, order_ref, out_ext, *inputs[: len(inputs) - offsets], p_ref, q_ref)


def product_rows(first_row, permuted, cols_ref, order_ref, ext, w_ref, p_ref, q_ref, own_terms):
    samples = p_ref.shape[0]
    per_entry = cols_ref.shape[0]
    lane = lax.broadcasted_iota(jnp.int32, (2 * samples, LANES), 1)
    low_lane = lax.broadcasted_iota(jnp.int32, (samples, LANES), 1) < HALF

    def row_product(row):
        other = order_ref[row]
        source, place = (other, row) if permuted else (row, other)
        parts = []
        for k in range(0, per_entry, 2):
            first = cols_ref[k, source]
            second = cols_ref[k + 1, source]
            a = ext[first & 1, first // 2]
            b = ext[1 - (second & 1), second // 2]
            parts.append(jnp.where(lane < HALF, a, b))
        left = jnp.concatenate(parts, axis=1)
        full = jnp.dot(left, w_ref[place], preferred_element_type=jnp.float32)
        width = full.shape[1] // 2
        rows = full[:, :width] + full[:, width:]
        return rows[:samples] + rows[samples:]

    def block(step, carry):
        for pair in range(GROUP // 2):
            row = step * GROUP + 2 * pair
            first = row_product(first_row + row)
            second = row_product(first_row + row + 1)
            direct = jnp.where(low_lane, first, pltpu.roll(second, HALF, 1))
            charge = jnp.where(low_lane, pltpu.roll(first, HALF, 1), second)
            here = pl.ds(pl.multiple_of(row * HALF, LANES), LANES)
            g_term, c_term = own_terms(row)
            p_ref[:, here] = direct + g_term
            q_ref[:, here] = charge + c_term
        return carry

    lax.fori_loop(0, p_ref.shape[1] // (GROUP * HALF), block, 0)


def permuted_product(first_row, base_row, cols_ref, order_ref, ext, w_ref, g_ref, c_ref, p_ref, q_ref):
    def own_terms(row):
        there = pl.ds(pl.multiple_of((first_row - base_row + row) * HALF, LANES), LANES)
        return g_ref[:, there], c_ref[:, there]

    product_rows(first_row, True, cols_ref, order_ref, ext, w_ref, p_ref, q_ref, own_terms)


def plain_product(first_row, cols_ref, order_ref, ext, w_ref, field_ref, g_ref, c_ref, p_ref, q_ref):
    def own_terms(row):
        there = pl.ds(pl.multiple_of((first_row + row) * HALF, LANES), LANES)
        own = field_ref[:, there]
        return g_ref[:, there] * own, c_ref[:, there] * own

    product_rows(first_row, False, cols_ref, order_ref, ext, w_ref, p_ref, q_ref, own_terms)


def slope_columns(matrix, charges):
    samples = charges[0].shape[0]
    parts = [split(x) for x in charges]
    high = jnp.concatenate([h for h, _ in parts], axis=0)
    low = jnp.concatenate([l for _, l in parts], axis=0)
    first = jnp.dot(matrix, high, preferred_element_type=jnp.float32)
    second = jnp.dot(matrix[:samples], low, preferred_element_type=jnp.float32)
    return first[:samples] + first[samples:] + second


CHUNK = 256


def near_kernel(chunks, *refs):
    matrix = refs[0][...]
    p_refs, q_refs, mate_refs, out_refs = [refs[1 + n * chunks : 1 + (n + 1) * chunks] for n in range(4)]
    for p_ref, q_ref, mate_ref, out_ref in zip(p_refs, q_refs, mate_refs, out_refs):
        for start in range(0, p_ref.shape[1], CHUNK):
            inside = slice(start, start + CHUNK)
            out_ref[:, inside] = p_ref[:, inside] + slope_columns(matrix, [q_ref[:, inside], mate_ref[:, inside]])


def far_columns(matrix, p_ref, charge_refs):
    for start in range(0, p_ref.shape[1], CHUNK):
        inside = slice(start, start + CHUNK)
        yield start, p_ref[:, inside] + slope_columns(matrix, [c[:, inside] for c in charge_refs])


def far_kernel(count, base, chunks, *refs):
    matrix = refs[0][...]
    out_ref = refs[-1]
    size = 1 + count
    for n in range(chunks):
        p_ref, *charge_refs = refs[1 + n * size : 1 + (n + 1) * size]
        for start, value in far_columns(matrix, p_ref, charge_refs):
            out_ref[:, base + start : base + start + CHUNK] = value
        base += p_ref.shape[1]


def far_send_kernel(count, chunks, domains, send_near, inv_near, *refs):
    size = 1 + count
    u_ref, *out_refs, send_ref, send_sem, inv_ref, inv_sem = refs[1 + chunks * size :]
    tables = [
        pltpu.make_async_copy(send_near, send_ref, send_sem),
        pltpu.make_async_copy(inv_near, inv_ref, inv_sem),
    ]
    for table in tables:
        table.start()
    far_kernel(count, 0, chunks, *refs[: 1 + chunks * size], u_ref)
    for table in tables:
        table.wait()
    gather_all(domains, send_ref, u_ref, out_refs, inv_ref)


def dot_totals(totals, r_ref, u_ref, base, v):
    for i in range(0, v.shape[1], LANES):
        vv = v[:, i : i + LANES]
        rr = r_ref[:, base + i : base + i + LANES]
        uu = u_ref[:, base + i : base + i + LANES]
        for n, (a, b) in enumerate(((uu, uu), (uu, vv), (vv, vv), (rr, uu), (rr, vv))):
            totals[n] = totals[n] + a * b


def far_dots_kernel(count, base, chunks, *refs):
    matrix = refs[0][...]
    out_ref = refs[-1]
    size = 1 + count
    r_ref, u_ref, *before = refs[1 + chunks * size : -1]
    samples = r_ref.shape[0]
    totals = [before[0][n] if before else jnp.zeros((samples, LANES), jnp.float32) for n in range(5)]
    for n in range(chunks):
        p_ref, *charge_refs = refs[1 + n * size : 1 + (n + 1) * size]
        for start, value in far_columns(matrix, p_ref, charge_refs):
            dot_totals(totals, r_ref, u_ref, base + start, value)
        base += p_ref.shape[1]
    if base < u_ref.shape[1]:
        for n in range(5):
            out_ref[n] = totals[n]
        return
    lane = lax.broadcasted_iota(jnp.int32, (1, LANES), 1)
    packed = jnp.zeros((1, LANES), jnp.float32)
    for n, total in enumerate(totals):
        packed = jnp.where(lane == n, jnp.sum(total), packed)
    for d in range(out_ref.shape[0]):
        out_ref[d] = packed


def update_kernel(sums_ref, r_ref, u_ref, out_hbm, out_ref, sems):
    total = jnp.sum(sums_ref[...], axis=0)
    lane = lax.broadcasted_iota(jnp.int32, total.shape, 1)
    uu, uv, vv, ru, rv = [jnp.sum(jnp.where(lane == n, total, 0.0), axis=1, keepdims=True) for n in range(5)]
    length_u = jnp.sqrt(uu)
    length_v = jnp.sqrt(vv)
    cross = uv / length_u / length_v
    target_u = ru / length_u
    target_v = rv / length_v
    determinant = 1.0 - cross * cross
    weight_r = (target_u - cross * target_v) / determinant / length_u
    weight_u = (target_v - cross * target_u) / determinant / length_v
    part = r_ref.shape[0] // COPIES
    copies = []
    for n in range(COPIES):
        rows = slice(n * part, (n + 1) * part)
        for start in range(0, r_ref.shape[1], LANES):
            inside = slice(start, start + LANES)
            out_ref[rows, inside] = weight_r * r_ref[rows, inside] + weight_u * u_ref[rows, inside]
        copies.append(pltpu.make_async_copy(out_ref.at[rows], out_hbm.at[rows], sems.at[n]))
        copies[-1].start()
    for copy in copies:
        copy.wait()


def update(sums, r, u):
    return pl.pallas_call(
        update_kernel,
        in_specs=[whole()] * 3,
        out_specs=pl.BlockSpec(memory_space=pl.ANY),
        out_shape=jax.ShapeDtypeStruct(r.shape, r.dtype),
        scratch_shapes=[pltpu.VMEM(r.shape, r.dtype), pltpu.SemaphoreType.DMA((COPIES,))],
        compiler_params=pltpu.CompilerParams(vmem_limit_bytes=LIMIT),
        name="update",
    )(near_memory(sums), near_memory(r), near_memory(u))


def chunk_sizes(rows, domains, slots):
    unit = rows // 8
    early = (domains - 1) * slots if few(domains) else 3 * unit
    return [unit, early - unit, rows - early], [unit, 2 * unit, 4 * unit, unit]


def body(residual, conductance, capacitance, stamps, block_cols, send_blocks):
    samples, unknowns = residual.shape
    rows, per_entry = block_cols.shape
    width = stamps.shape[2]
    slots = send_blocks.shape[2]
    domains = lax.axis_size("dom")
    groups = lax.axis_size("samp")
    pairs = [(i, i ^ 1) for i in range(groups)]
    shifts = range(2, groups, 2)
    count = 2 * len(shifts)
    sizes_one, sizes_two = chunk_sizes(rows, domains, slots)
    early = sizes_one[0] + sizes_one[1]
    f32 = jnp.float32
    if few(domains):
        outgoing_shapes = [((samples, slots * width), f32)] * (domains - 1)
    else:
        outgoing_shapes = [((domains, samples, slots * width), f32)]
    field_shape = ((samples, unknowns), f32)
    own_tiles = unknowns // LANES
    tiles = own_tiles + domains * slots * width // LANES
    ext_shape = ((2, tiles, 2 * samples, LANES), jnp.bfloat16)
    weight_shape = ((rows, per_entry * width, 4 * width), jnp.bfloat16)
    cols = block_cols.T
    send = send_blocks[0].T

    def exchange(outgoing):
        if not few(domains):
            return [lax.all_to_all(outgoing[0], "dom", split_axis=0, concat_axis=0, tiled=True)]
        incoming = []
        for k, x in zip(halo_offsets(domains), outgoing):
            incoming.append(lax.ppermute(x, "dom", [(i, i ^ k) for i in range(domains)]))
        return incoming

    def product_call(n, size, product, operands, incoming):
        shape = ((samples, size * width), f32)
        if n:
            p, q = kernel_call(product, operands, [shape, shape])
            return operands[2], p, q
        return kernel_call(
            functools.partial(with_arrived, domains, product, own_tiles),
            (*operands, *incoming),
            [ext_shape, shape, shape],
            aliases={2: 0},
            table_copied=True,
        )

    def spread(q):
        far = [lax.ppermute(q, "samp", [(i, (i + k) % groups) for i in range(groups)]) for k in shifts]
        return far, lax.ppermute(q, "samp", pairs)

    def near_call(chunks):
        return kernel_call(
            functools.partial(near_kernel, len(chunks)),
            (near_matrix, *[p for p, _, _, _ in chunks], *[q for _, q, _, _ in chunks], *[m for _, _, _, m in chunks]),
            [(p.shape, f32) for p, _, _, _ in chunks],
        )

    def forward(half, far):
        charges = []
        for x in far:
            charges += [x, lax.ppermute(x, "samp", pairs)]
        return [half, *charges]

    field, perm, inv, *outgoing = gather(send, residual, rows, domains, outgoing_shapes)
    incoming = exchange(outgoing)
    near_matrix, far_matrix = kernel_call(
        functools.partial(tables_kernel, groups),
        (),
        [((2 * samples, 2 * samples), jnp.bfloat16), ((2 * samples, count * samples), jnp.bfloat16)],
    )
    blocks = stamps.reshape(rows, per_entry * width, 2 * width)
    (ext,) = kernel_call(extend_kernel, (field,), [ext_shape])
    weights = None
    own = []
    for n, (low, high) in enumerate(((0, early), (early, rows))):
        if n == 0:
            weights = fetch(perm, blocks, early)
        else:
            (weights,) = kernel_call(
                functools.partial(prepare_kernel, low, high), (perm, blocks, weights), [weight_shape], aliases={2: 0}
            )
        terms = kernel_call(
            functools.partial(arrange_kernel, low),
            (perm, field, conductance, capacitance),
            [((samples, (high - low) * width), f32)] * 2,
        )
        own.append((low, weights, terms))
    chunks = []
    first = 0
    for n, size in enumerate(sizes_one):
        base, w, terms = own[first >= early]
        ext, p, q = product_call(
            n, size, functools.partial(permuted_product, first, base), (cols, perm, ext, w, *terms), incoming
        )
        chunks.append((p, q, *spread(q)))
        first += size
    half = near_call(chunks[:2]) + near_call(chunks[2:])
    pieces = [forward(half[n], chunk[2]) for n, chunk in enumerate(chunks)]
    ready = 2 if few(domains) else len(chunks)
    u, *outgoing = kernel_call(
        functools.partial(far_send_kernel, count, ready, domains),
        (send, inv, far_matrix, *[x for piece in pieces[:ready] for x in piece]),
        [field_shape, *outgoing_shapes],
        table_copied=True,
    )
    incoming = exchange(outgoing)
    if ready < len(chunks):
        operands = [far_matrix, *[x for piece in pieces[ready:] for x in piece]]
        (u,) = kernel_call(
            functools.partial(far_kernel, count, early * width, len(chunks) - ready),
            operands + [u],
            [field_shape],
            aliases={len(operands): 0},
        )
    u, ext = kernel_call(restore_kernel, (inv, u), [field_shape, ext_shape])
    chunks = []
    first = 0
    for n, size in enumerate(sizes_two):
        operands = (cols, inv, ext, weights, u, conductance, capacitance)
        ext, p, q = product_call(n, size, functools.partial(plain_product, first), operands, incoming)
        chunks.append((p, q, *spread(q)))
        first += size
    half = near_call(chunks)
    pieces = [forward(half[n], chunk[2]) for n, chunk in enumerate(chunks)]
    sums = None
    last = len(chunks) - 1
    for n, (low, high) in enumerate(((0, last - 1), (last - 1, last), (last, last + 1))):
        final = high > last
        (sums,) = kernel_call(
            functools.partial(far_dots_kernel, count, sum(sizes_two[:low]) * width, high - low),
            [far_matrix, *[x for piece in pieces[low:high] for x in piece], field, u] + [sums] * (n > 0),
            [((domains * groups, 1, LANES) if final else (5, samples, LANES), f32)],
        )
    sums = lax.all_to_all(sums, ("dom", "samp"), split_axis=0, concat_axis=0, tiled=True)
    return update(sums, field, u)


def solution(mesh):
    in_specs = (
        P("samp", "dom"),
        P("samp", "dom"),
        P("samp", "dom"),
        P("dom", None, None, None),
        P("dom", None),
        P("dom", None, None),
    )
    out_specs = P("samp", "dom")
    return jax.shard_map(body, mesh=mesh, in_specs=in_specs, out_specs=out_specs, check_vma=False)
```

```python
import functools

import jax
import jax.numpy as jnp
from jax import lax
from jax.experimental import pallas as pl
from jax.experimental.pallas import tpu as pltpu
from jax.sharding import PartitionSpec as P


LANES = 128
HALF = 64
GROUP = 4


LIMIT = 24 * 1024 * 1024


def whole():
    return pl.BlockSpec(memory_space=pltpu.VMEM)


def scalars():
    return pl.BlockSpec(memory_space=pltpu.SMEM)


def near_memory(x):
    return pltpu.with_memory_space_constraint(x, pltpu.VMEM)


def far_memory(x):
    return pltpu.with_memory_space_constraint(x, pltpu.HBM)


def kernel_call(kernel, inputs, outputs, aliases=None, table_copied=False):
    specs = []
    operands = []
    scratch = []
    for x in inputs:
        if x.dtype == jnp.int32 and table_copied:
            specs.append(pl.BlockSpec(memory_space=pl.ANY))
            operands.append(near_memory(x))
            scratch += [pltpu.SMEM(x.shape, x.dtype), pltpu.SemaphoreType.DMA]
        elif x.dtype == jnp.int32:
            specs.append(scalars())
            operands.append(x)
        else:
            specs.append(whole())
            operands.append(near_memory(x))
    integer = [dtype == jnp.int32 for _, dtype in outputs]
    out = [
        jax.ShapeDtypeStruct(shape, dtype) if number else pltpu.VMEM(shape, dtype)
        for (shape, dtype), number in zip(outputs, integer)
    ]
    return pl.pallas_call(
        kernel,
        in_specs=specs,
        out_specs=[scalars() if number else whole() for number in integer],
        out_shape=out,
        input_output_aliases=aliases or {},
        scratch_shapes=scratch,
        compiler_params=pltpu.CompilerParams(vmem_limit_bytes=LIMIT),
    )(*operands)


def split(x):
    high = x.astype(jnp.bfloat16)
    low = (x - high.astype(jnp.float32)).astype(jnp.bfloat16)
    return high, low


def spectral_rows(me, sources, samples, period):
    row = me * samples + lax.broadcasted_iota(jnp.int32, (samples, samples), 0)
    column = lax.broadcasted_iota(jnp.int32, (samples, samples), 1)
    blocks = []
    for source in sources:
        offset = row - (source * samples + column)
        sign = (1 - 2 * (offset & 1)).astype(jnp.float32)
        angle = jnp.pi / period * offset.astype(jnp.float32)
        nonzero = offset != 0
        safe = jnp.where(nonzero, angle, 0.5)
        value = sign * jnp.cos(safe) / jnp.sin(safe) / period
        blocks.append(jnp.where(nonzero, value, 0.0))
    high, low = split(jnp.concatenate(blocks, axis=1))
    return jnp.concatenate([high, low], axis=0)


def tables_kernel(groups, near_ref, far_ref):
    samples = near_ref.shape[1] // 2
    me = lax.axis_index("samp")
    partner = me + 1 - 2 * (me & 1)
    near_ref[...] = spectral_rows(me, [me, partner], samples, samples * groups)
    far = []
    for k in range(2, groups, 2):
        for source in (me - k, partner - k):
            far.append(jnp.where(source < 0, source + groups, source))
    far_ref[...] = spectral_rows(me, far, samples, samples * groups)


def prepare_kernel(first_row, last_row, order_ref, stamps_ref, *refs):
    out_ref = refs[-1]
    width = stamps_ref.shape[2]

    def convert(row, carry):
        high, low = split(stamps_ref[order_ref[0, row]])
        out_ref[row, :, :width] = high
        out_ref[row, :, width:] = low
        return carry

    lax.fori_loop(first_row, last_row, convert, 0, unroll=2)


def fetch_kernel(order_ref, stamps_hbm, out_ref, buffer, sems):
    rows, _, width = buffer.shape
    copies = []
    for n in range(rows):
        copies.append(pltpu.make_async_copy(stamps_hbm.at[order_ref[0, n]], buffer.at[n], sems.at[n]))
        copies[-1].start()
    for n, copy in enumerate(copies):
        copy.wait()
        high, low = split(buffer[n])
        out_ref[n, :, :width] = high
        out_ref[n, :, width:] = low


def fetch(order, stamps, rows):
    total, depth, width = stamps.shape
    return pl.pallas_call(
        fetch_kernel,
        in_specs=[scalars(), pl.BlockSpec(memory_space=pl.ANY)],
        out_specs=whole(),
        out_shape=pltpu.VMEM((total, depth, 2 * width), jnp.bfloat16),
        scratch_shapes=[pltpu.VMEM((rows, depth, width), stamps.dtype), pltpu.SemaphoreType.DMA((rows,))],
        compiler_params=pltpu.CompilerParams(vmem_limit_bytes=LIMIT),
        name="prepare_0",
    )(order, far_memory(stamps))


def pair_tile(ref, first, second):
    samples = ref.shape[0]
    lane = lax.broadcasted_iota(jnp.int32, (samples, LANES), 1)

    def placed(block, upper):
        start = pl.multiple_of((block // 2) * LANES, LANES)
        tile = ref[:, pl.ds(start, LANES)]
        turned = pltpu.roll(tile, HALF, 1)
        return jnp.where((block & 1) == upper, tile, turned)

    return jnp.where(lane < HALF, placed(first, 0), placed(second, 1))


def gather_blocks(targets, send_ref, field_ref, out_refs, order_ref=None):
    slots = send_ref.shape[0]
    for d, out_ref in zip(targets, out_refs):
        for j in range(0, slots, 2):
            first, second = send_ref[j, d], send_ref[j + 1, d]
            if order_ref is not None:
                first, second = order_ref[1, first], order_ref[1, second]
            out_ref[:, j * HALF : j * HALF + LANES] = pair_tile(field_ref, first, second)


def halo_offsets(domains):
    return sorted(range(1, domains), key=lambda k: (-(k >= domains // 2), k if k >= domains // 2 else -k))


def few(domains):
    return domains <= 8 and domains & (domains - 1) == 0


def gather_all(domains, send_ref, field_ref, out_refs, order_ref=None):
    if few(domains):
        me = lax.axis_index("dom")
        gather_blocks([me ^ k for k in halo_offsets(domains)], send_ref, field_ref, out_refs, order_ref)
    else:
        gather_blocks(range(domains), send_ref, field_ref, [out_refs[0].at[d] for d in range(domains)], order_ref)


COPIES = 4


WORD = 32


def order_rows(domains, send_ref, order_ref):
    rows = order_ref.shape[1]
    masks = [jnp.int32(0)] * (rows // WORD)
    if few(domains):
        me = lax.axis_index("dom")
        for d in range(domains):
            for j in range(send_ref.shape[0]):
                block = send_ref[j, d]
                bit = jnp.where(d == me, 0, jnp.left_shift(jnp.int32(1), block & (WORD - 1)))
                masks = [m | jnp.where(block // WORD == n, bit, 0) for n, m in enumerate(masks)]
    flags = [lax.shift_right_logical(masks[row // WORD], jnp.int32(row % WORD)) & 1 for row in range(rows)]
    first = jnp.int32(0)
    later = sum(flags)
    for row, flag in enumerate(flags):
        position = jnp.where(flag == 1, first, later)
        order_ref[0, position] = row
        order_ref[1, row] = position
        first = first + flag
        later = later + 1 - flag


def gather_kernel(domains, send_hbm, field_hbm, field_ref, order_ref, *refs):
    *out_refs, field_sem, send_ref, send_sem = refs
    table = pltpu.make_async_copy(send_hbm, send_ref, send_sem)
    table.start()
    width = field_ref.shape[1] // COPIES
    copies = []
    for n in range(COPIES):
        inside = pl.ds(n * width, width)
        copies.append(pltpu.make_async_copy(field_hbm.at[:, inside], field_ref.at[:, inside], field_sem.at[n]))
        copies[-1].start()
    table.wait()
    order_rows(domains, send_ref, order_ref)
    for copy in copies:
        copy.wait()
    gather_all(domains, send_ref, field_ref, out_refs)


def gather(send, field, rows, domains, outputs):
    table = jax.ShapeDtypeStruct((2, rows), jnp.int32)
    return pl.pallas_call(
        functools.partial(gather_kernel, domains),
        in_specs=[pl.BlockSpec(memory_space=pl.ANY)] * 2,
        out_specs=[whole(), scalars()] + [whole()] * len(outputs),
        out_shape=[
            pltpu.VMEM(field.shape, field.dtype),
            table,
            *[pltpu.VMEM(shape, dtype) for shape, dtype in outputs],
        ],
        scratch_shapes=[
            pltpu.SemaphoreType.DMA((COPIES,)),
            pltpu.SMEM(send.shape, send.dtype),
            pltpu.SemaphoreType.DMA,
        ],
        compiler_params=pltpu.CompilerParams(vmem_limit_bytes=LIMIT),
        name="gather",
    )(far_memory(send), far_memory(field))


def store_tile(ext, index, x):
    high, low = split(x)
    ext[0, index] = jnp.concatenate([high, low], axis=0)
    high, low = split(pltpu.roll(x, HALF, 1))
    ext[1, index] = jnp.concatenate([high, low], axis=0)


def arrange_kernel(first_row, order_ref, field_ref, g_ref, c_ref, g_out, c_out):
    samples = field_ref.shape[0]
    lane = lax.broadcasted_iota(jnp.int32, (samples, LANES), 1)

    def placed(block, upper):
        here = pl.ds(pl.multiple_of((block // 2) * LANES, LANES), LANES)
        own = field_ref[:, here]
        keep = (block & 1) == upper
        return [jnp.where(keep, x, pltpu.roll(x, HALF, 1)) for x in (g_ref[:, here] * own, c_ref[:, here] * own)]

    for i in range(g_out.shape[1] // LANES):
        inside = slice(i * LANES, (i + 1) * LANES)
        low = placed(order_ref[0, first_row + 2 * i], 0)
        high = placed(order_ref[0, first_row + 2 * i + 1], 1)
        g_out[:, inside] = jnp.where(lane < HALF, low[0], high[0])
        c_out[:, inside] = jnp.where(lane < HALF, low[1], high[1])


def restore_kernel(order_ref, u_ref, out_ref):
    for i in range(u_ref.shape[1] // LANES):
        inside = slice(i * LANES, (i + 1) * LANES)
        out_ref[:, inside] = pair_tile(u_ref, order_ref[1, 2 * i], order_ref[1, 2 * i + 1])


def extend_kernel(field_ref, ext):
    for i in range(field_ref.shape[1] // LANES):
        store_tile(ext, i, field_ref[:, i * LANES : (i + 1) * LANES])


def extend_arrived(domains, own_tiles, inc_refs, ext):
    if few(domains):
        me = lax.axis_index("dom")
        arrived = [(me ^ k, ref) for k, ref in zip(halo_offsets(domains), inc_refs)]
    else:
        arrived = [(d, inc_refs[0].at[d]) for d in range(domains)]
    for source, ref in arrived:
        per_domain = ref.shape[1] // LANES
        for j in range(per_domain):
            store_tile(ext, own_tiles + source * per_domain + j, ref[:, j * LANES : (j + 1) * LANES])


def with_arrived(domains, product, own_tiles, cols_near, order_near, *refs):
    *inputs, out_ext, p_ref, q_ref, cols_ref, cols_sem, order_ref, order_sem = refs
    tables = [
        pltpu.make_async_copy(cols_near, cols_ref, cols_sem),
        pltpu.make_async_copy(order_near, order_ref, order_sem),
    ]
    for table in tables:
        table.start()
    offsets = domains - 1 if few(domains) else 1
    own_ext, *inputs = inputs
    extend_arrived(domains, own_tiles, inputs[len(inputs) - offsets :], out_ext)
    for table in tables:
        table.wait()
    product(cols_ref, order_ref, out_ext, *inputs[: len(inputs) - offsets], p_ref, q_ref)


def product_rows(first_row, permuted, cols_ref, order_ref, ext, w_ref, p_ref, q_ref, own_terms):
    samples = p_ref.shape[0]
    per_entry = cols_ref.shape[0]
    lane = lax.broadcasted_iota(jnp.int32, (2 * samples, LANES), 1)
    low_lane = lax.broadcasted_iota(jnp.int32, (samples, LANES), 1) < HALF

    rows = cols_ref.shape[1]

    def entry_of(k, row):
        entry = cols_ref[k, row]
        if permuted:
            return entry
        return jnp.where(entry < rows, order_ref[1, jnp.minimum(entry, rows - 1)], entry)

    def row_product(row):
        source, place = (order_ref[0, row], row) if permuted else (row, order_ref[1, row])
        parts = []
        for k in range(0, per_entry, 2):
            first = entry_of(k, source)
            second = entry_of(k + 1, source)
            a = ext[first & 1, first // 2]
            b = ext[1 - (second & 1), second // 2]
            parts.append(jnp.where(lane < HALF, a, b))
        left = jnp.concatenate(parts, axis=1)
        full = jnp.dot(left, w_ref[place], preferred_element_type=jnp.float32)
        width = full.shape[1] // 2
        both = full[:, :width] + full[:, width:]
        return both[:samples] + both[samples:]

    def block(step, carry):
        for pair in range(GROUP // 2):
            row = step * GROUP + 2 * pair
            first = row_product(first_row + row)
            second = row_product(first_row + row + 1)
            direct = jnp.where(low_lane, first, pltpu.roll(second, HALF, 1))
            charge = jnp.where(low_lane, pltpu.roll(first, HALF, 1), second)
            here = pl.ds(pl.multiple_of(row * HALF, LANES), LANES)
            g_term, c_term = own_terms(row)
            p_ref[:, here] = direct + g_term
            q_ref[:, here] = charge + c_term
        return carry

    lax.fori_loop(0, p_ref.shape[1] // (GROUP * HALF), block, 0)


def permuted_product(first_row, base_row, cols_ref, order_ref, ext, w_ref, g_ref, c_ref, p_ref, q_ref):
    def own_terms(row):
        there = pl.ds(pl.multiple_of((first_row - base_row + row) * HALF, LANES), LANES)
        return g_ref[:, there], c_ref[:, there]

    product_rows(first_row, True, cols_ref, order_ref, ext, w_ref, p_ref, q_ref, own_terms)


def plain_product(first_row, cols_ref, order_ref, ext, w_ref, field_ref, g_ref, c_ref, p_ref, q_ref):
    def own_terms(row):
        there = pl.ds(pl.multiple_of((first_row + row) * HALF, LANES), LANES)
        own = pair_tile(field_ref, order_ref[1, first_row + row], order_ref[1, first_row + row + 1])
        return g_ref[:, there] * own, c_ref[:, there] * own

    product_rows(first_row, False, cols_ref, order_ref, ext, w_ref, p_ref, q_ref, own_terms)


def slope_columns(matrix, charges):
    samples = charges[0].shape[0]
    parts = [split(x) for x in charges]
    high = jnp.concatenate([h for h, _ in parts], axis=0)
    low = jnp.concatenate([l for _, l in parts], axis=0)
    first = jnp.dot(matrix, high, preferred_element_type=jnp.float32)
    second = jnp.dot(matrix[:samples], low, preferred_element_type=jnp.float32)
    return first[:samples] + first[samples:] + second


CHUNK = 256


def near_kernel(chunks, *refs):
    matrix = refs[0][...]
    p_refs, q_refs, mate_refs, out_refs = [refs[1 + n * chunks : 1 + (n + 1) * chunks] for n in range(4)]
    for p_ref, q_ref, mate_ref, out_ref in zip(p_refs, q_refs, mate_refs, out_refs):
        for start in range(0, p_ref.shape[1], CHUNK):
            inside = slice(start, start + CHUNK)
            out_ref[:, inside] = p_ref[:, inside] + slope_columns(matrix, [q_ref[:, inside], mate_ref[:, inside]])


def far_columns(matrix, p_ref, charge_refs):
    for start in range(0, p_ref.shape[1], CHUNK):
        inside = slice(start, start + CHUNK)
        yield start, p_ref[:, inside] + slope_columns(matrix, [c[:, inside] for c in charge_refs])


def far_kernel(count, base, chunks, *refs):
    matrix = refs[0][...]
    out_ref = refs[-1]
    size = 1 + count
    for n in range(chunks):
        p_ref, *charge_refs = refs[1 + n * size : 1 + (n + 1) * size]
        for start, value in far_columns(matrix, p_ref, charge_refs):
            out_ref[:, base + start : base + start + CHUNK] = value
        base += p_ref.shape[1]


def far_send_kernel(count, chunks, domains, send_near, order_near, *refs):
    size = 1 + count
    u_ref, *out_refs, send_ref, send_sem, order_ref, order_sem = refs[1 + chunks * size :]
    tables = [
        pltpu.make_async_copy(send_near, send_ref, send_sem),
        pltpu.make_async_copy(order_near, order_ref, order_sem),
    ]
    for table in tables:
        table.start()
    far_kernel(count, 0, chunks, *refs[: 1 + chunks * size], u_ref)
    for table in tables:
        table.wait()
    gather_all(domains, send_ref, u_ref, out_refs, order_ref)


def dot_totals(totals, r_ref, u_ref, base, v):
    for i in range(0, v.shape[1], LANES):
        vv = v[:, i : i + LANES]
        rr = r_ref[:, base + i : base + i + LANES]
        uu = u_ref[:, base + i : base + i + LANES]
        for n, (a, b) in enumerate(((uu, uu), (uu, vv), (vv, vv), (rr, uu), (rr, vv))):
            totals[n] = totals[n] + a * b


def far_dots_kernel(count, base, chunks, *refs):
    matrix = refs[0][...]
    out_ref = refs[-1]
    size = 1 + count
    r_ref, u_ref, *before = refs[1 + chunks * size : -1]
    samples = r_ref.shape[0]
    totals = [before[0][n] if before else jnp.zeros((samples, LANES), jnp.float32) for n in range(5)]
    for n in range(chunks):
        p_ref, *charge_refs = refs[1 + n * size : 1 + (n + 1) * size]
        for start, value in far_columns(matrix, p_ref, charge_refs):
            dot_totals(totals, r_ref, u_ref, base + start, value)
        base += p_ref.shape[1]
    if base < u_ref.shape[1]:
        for n in range(5):
            out_ref[n] = totals[n]
        return
    lane = lax.broadcasted_iota(jnp.int32, (1, LANES), 1)
    packed = jnp.zeros((1, LANES), jnp.float32)
    for n, total in enumerate(totals):
        packed = jnp.where(lane == n, jnp.sum(total), packed)
    for d in range(out_ref.shape[0]):
        out_ref[d] = packed


def update_kernel(sums_ref, r_ref, u_ref, out_hbm, out_ref, sems):
    total = jnp.sum(sums_ref[...], axis=0)
    lane = lax.broadcasted_iota(jnp.int32, total.shape, 1)
    uu, uv, vv, ru, rv = [jnp.sum(jnp.where(lane == n, total, 0.0), axis=1, keepdims=True) for n in range(5)]
    length_u = jnp.sqrt(uu)
    length_v = jnp.sqrt(vv)
    cross = uv / length_u / length_v
    target_u = ru / length_u
    target_v = rv / length_v
    determinant = 1.0 - cross * cross
    weight_r = (target_u - cross * target_v) / determinant / length_u
    weight_u = (target_v - cross * target_u) / determinant / length_v
    part = r_ref.shape[0] // COPIES
    copies = []
    for n in range(COPIES):
        rows = slice(n * part, (n + 1) * part)
        for start in range(0, r_ref.shape[1], LANES):
            inside = slice(start, start + LANES)
            out_ref[rows, inside] = weight_r * r_ref[rows, inside] + weight_u * u_ref[rows, inside]
        copies.append(pltpu.make_async_copy(out_ref.at[rows], out_hbm.at[rows], sems.at[n]))
        copies[-1].start()
    for copy in copies:
        copy.wait()


def update(sums, r, u):
    return pl.pallas_call(
        update_kernel,
        in_specs=[whole()] * 3,
        out_specs=pl.BlockSpec(memory_space=pl.ANY),
        out_shape=jax.ShapeDtypeStruct(r.shape, r.dtype),
        scratch_shapes=[pltpu.VMEM(r.shape, r.dtype), pltpu.SemaphoreType.DMA((COPIES,))],
        compiler_params=pltpu.CompilerParams(vmem_limit_bytes=LIMIT),
        name="update",
    )(near_memory(sums), near_memory(r), near_memory(u))


def chunk_sizes(rows, domains, slots):
    unit = rows // 8
    early = (domains - 1) * slots if few(domains) else 3 * unit
    return [unit, early - unit, rows - early], [unit, 2 * unit, 4 * unit, unit]


def body(residual, conductance, capacitance, stamps, block_cols, send_blocks):
    samples, unknowns = residual.shape
    rows, per_entry = block_cols.shape
    width = stamps.shape[2]
    slots = send_blocks.shape[2]
    domains = lax.axis_size("dom")
    groups = lax.axis_size("samp")
    pairs = [(i, i ^ 1) for i in range(groups)]
    shifts = range(2, groups, 2)
    count = 2 * len(shifts)
    sizes_one, sizes_two = chunk_sizes(rows, domains, slots)
    early = sizes_one[0] + sizes_one[1]
    f32 = jnp.float32
    if few(domains):
        outgoing_shapes = [((samples, slots * width), f32)] * (domains - 1)
    else:
        outgoing_shapes = [((domains, samples, slots * width), f32)]
    field_shape = ((samples, unknowns), f32)
    own_tiles = unknowns // LANES
    tiles = own_tiles + domains * slots * width // LANES
    ext_shape = ((2, tiles, 2 * samples, LANES), jnp.bfloat16)
    weight_shape = ((rows, per_entry * width, 4 * width), jnp.bfloat16)
    cols = block_cols.T
    send = send_blocks[0].T

    def exchange(outgoing):
        if not few(domains):
            return [lax.all_to_all(outgoing[0], "dom", split_axis=0, concat_axis=0, tiled=True)]
        incoming = []
        for k, x in zip(halo_offsets(domains), outgoing):
            incoming.append(lax.ppermute(x, "dom", [(i, i ^ k) for i in range(domains)]))
        return incoming

    def product_call(n, size, product, operands, incoming):
        shape = ((samples, size * width), f32)
        if n:
            p, q = kernel_call(product, operands, [shape, shape])
            return operands[2], p, q
        return kernel_call(
            functools.partial(with_arrived, domains, product, own_tiles),
            (*operands, *incoming),
            [ext_shape, shape, shape],
            aliases={2: 0},
            table_copied=True,
        )

    def spread(q):
        far = [lax.ppermute(q, "samp", [(i, (i + k) % groups) for i in range(groups)]) for k in shifts]
        return far, lax.ppermute(q, "samp", pairs)

    def near_call(chunks):
        return kernel_call(
            functools.partial(near_kernel, len(chunks)),
            (near_matrix, *[p for p, _, _, _ in chunks], *[q for _, q, _, _ in chunks], *[m for _, _, _, m in chunks]),
            [(p.shape, f32) for p, _, _, _ in chunks],
        )

    def forward(half, far):
        charges = []
        for x in far:
            charges += [x, lax.ppermute(x, "samp", pairs)]
        return [half, *charges]

    field, order, *outgoing = gather(send, residual, rows, domains, outgoing_shapes)
    incoming = exchange(outgoing)
    near_matrix, far_matrix = kernel_call(
        functools.partial(tables_kernel, groups),
        (),
        [((2 * samples, 2 * samples), jnp.bfloat16), ((2 * samples, count * samples), jnp.bfloat16)],
    )
    blocks = stamps.reshape(rows, per_entry * width, 2 * width)
    (ext,) = kernel_call(extend_kernel, (field,), [ext_shape])
    weights = None
    own = []
    for n, (low, high) in enumerate(((0, early), (early, rows))):
        if n == 0:
            weights = fetch(order, blocks, early)
        else:
            (weights,) = kernel_call(
                functools.partial(prepare_kernel, low, high), (order, blocks, weights), [weight_shape], aliases={2: 0}
            )
        terms = kernel_call(
            functools.partial(arrange_kernel, low),
            (order, field, conductance, capacitance),
            [((samples, (high - low) * width), f32)] * 2,
        )
        own.append((low, weights, terms))
    chunks = []
    first = 0
    for n, size in enumerate(sizes_one):
        base, w, terms = own[first >= early]
        ext, p, q = product_call(
            n, size, functools.partial(permuted_product, first, base), (cols, order, ext, w, *terms), incoming
        )
        chunks.append((p, q, *spread(q)))
        first += size
    half = near_call(chunks[:2]) + near_call(chunks[2:])
    pieces = [forward(half[n], chunk[2]) for n, chunk in enumerate(chunks)]
    ready = 2 if few(domains) else len(chunks)
    u, *outgoing = kernel_call(
        functools.partial(far_send_kernel, count, ready, domains),
        (send, order, far_matrix, *[x for piece in pieces[:ready] for x in piece]),
        [field_shape, *outgoing_shapes],
        table_copied=True,
    )
    incoming = exchange(outgoing)
    if ready < len(chunks):
        operands = [far_matrix, *[x for piece in pieces[ready:] for x in piece]]
        (u,) = kernel_call(
            functools.partial(far_kernel, count, early * width, len(chunks) - ready),
            operands + [u],
            [field_shape],
            aliases={len(operands): 0},
        )
    (ext,) = kernel_call(extend_kernel, (u,), [ext_shape])
    chunks = []
    first = 0
    for n, size in enumerate(sizes_two):
        operands = (cols, order, ext, weights, u, conductance, capacitance)
        ext, p, q = product_call(n, size, functools.partial(plain_product, first), operands, incoming)
        chunks.append((p, q, *spread(q)))
        first += size
    (u,) = kernel_call(restore_kernel, (order, u), [field_shape])
    half = near_call(chunks)
    pieces = [forward(half[n], chunk[2]) for n, chunk in enumerate(chunks)]
    sums = None
    last = len(chunks) - 1
    for n, (low, high) in enumerate(((0, last - 1), (last - 1, last), (last, last + 1))):
        final = high > last
        (sums,) = kernel_call(
            functools.partial(far_dots_kernel, count, sum(sizes_two[:low]) * width, high - low),
            [far_matrix, *[x for piece in pieces[low:high] for x in piece], field, u] + [sums] * (n > 0),
            [((domains * groups, 1, LANES) if final else (5, samples, LANES), f32)],
        )
    sums = lax.all_to_all(sums, ("dom", "samp"), split_axis=0, concat_axis=0, tiled=True)
    return update(sums, field, u)


def solution(mesh):
    in_specs = (
        P("samp", "dom"),
        P("samp", "dom"),
        P("samp", "dom"),
        P("dom", None, None, None),
        P("dom", None),
        P("dom", None, None),
    )
    out_specs = P("samp", "dom")
    return jax.shard_map(body, mesh=mesh, in_specs=in_specs, out_specs=out_specs, check_vma=False)
```

```python
import functools

import jax
import jax.numpy as jnp
from jax import lax
from jax.experimental import pallas as pl
from jax.experimental.pallas import tpu as pltpu
from jax.sharding import PartitionSpec as P


LANES = 128
HALF = 64
GROUP = 12


LIMIT = 24 * 1024 * 1024


def whole():
    return pl.BlockSpec(memory_space=pltpu.VMEM)


def scalars():
    return pl.BlockSpec(memory_space=pltpu.SMEM)


def near_memory(x):
    return pltpu.with_memory_space_constraint(x, pltpu.VMEM)


def far_memory(x):
    return pltpu.with_memory_space_constraint(x, pltpu.HBM)


def kernel_call(kernel, inputs, outputs, aliases=None, table_copied=False):
    specs = []
    operands = []
    scratch = []
    for x in inputs:
        if x.dtype == jnp.int32 and table_copied:
            specs.append(pl.BlockSpec(memory_space=pl.ANY))
            operands.append(near_memory(x))
            scratch += [pltpu.SMEM(x.shape, x.dtype), pltpu.SemaphoreType.DMA]
        elif x.dtype == jnp.int32:
            specs.append(scalars())
            operands.append(x)
        else:
            specs.append(whole())
            operands.append(near_memory(x))
    integer = [dtype == jnp.int32 for _, dtype in outputs]
    out = [
        jax.ShapeDtypeStruct(shape, dtype) if number else pltpu.VMEM(shape, dtype)
        for (shape, dtype), number in zip(outputs, integer)
    ]
    return pl.pallas_call(
        kernel,
        in_specs=specs,
        out_specs=[scalars() if number else whole() for number in integer],
        out_shape=out,
        input_output_aliases=aliases or {},
        scratch_shapes=scratch,
        compiler_params=pltpu.CompilerParams(vmem_limit_bytes=LIMIT),
    )(*operands)


def split(x):
    high = x.astype(jnp.bfloat16)
    low = (x - high.astype(jnp.float32)).astype(jnp.bfloat16)
    return high, low


def spectral_rows(me, sources, samples, period):
    row = me * samples + lax.broadcasted_iota(jnp.int32, (samples, samples), 0)
    column = lax.broadcasted_iota(jnp.int32, (samples, samples), 1)
    blocks = []
    for source in sources:
        offset = row - (source * samples + column)
        sign = (1 - 2 * (offset & 1)).astype(jnp.float32)
        angle = jnp.pi / period * offset.astype(jnp.float32)
        nonzero = offset != 0
        safe = jnp.where(nonzero, angle, 0.5)
        value = sign * jnp.cos(safe) / jnp.sin(safe) / period
        blocks.append(jnp.where(nonzero, value, 0.0))
    high, low = split(jnp.concatenate(blocks, axis=1))
    return jnp.concatenate([high, low], axis=0)


def tables_kernel(groups, near_ref, far_ref):
    samples = near_ref.shape[1] // 2
    me = lax.axis_index("samp")
    partner = me + 1 - 2 * (me & 1)
    near_ref[...] = spectral_rows(me, [me, partner], samples, samples * groups)
    far = []
    for k in range(2, groups, 2):
        for source in (me - k, partner - k):
            far.append(jnp.where(source < 0, source + groups, source))
    far_ref[...] = spectral_rows(me, far, samples, samples * groups)


def prepare_kernel(first_row, last_row, order_ref, stamps_ref, *refs):
    out_ref = refs[-1]
    width = stamps_ref.shape[2]

    def convert(row, carry):
        high, low = split(stamps_ref[order_ref[0, row]])
        out_ref[row, :, :width] = high
        out_ref[row, :, width:] = low
        return carry

    lax.fori_loop(first_row, last_row, convert, 0, unroll=2)


def fetch_kernel(order_ref, stamps_hbm, out_ref, buffer, sems):
    rows, _, width = buffer.shape
    copies = []
    for n in range(rows):
        copies.append(pltpu.make_async_copy(stamps_hbm.at[order_ref[0, n]], buffer.at[n], sems.at[n]))
        copies[-1].start()
    for n, copy in enumerate(copies):
        copy.wait()
        high, low = split(buffer[n])
        out_ref[n, :, :width] = high
        out_ref[n, :, width:] = low


def fetch(order, stamps, rows):
    total, depth, width = stamps.shape
    return pl.pallas_call(
        fetch_kernel,
        in_specs=[scalars(), pl.BlockSpec(memory_space=pl.ANY)],
        out_specs=whole(),
        out_shape=pltpu.VMEM((total, depth, 2 * width), jnp.bfloat16),
        scratch_shapes=[pltpu.VMEM((rows, depth, width), stamps.dtype), pltpu.SemaphoreType.DMA((rows,))],
        compiler_params=pltpu.CompilerParams(vmem_limit_bytes=LIMIT),
        name="prepare_0",
    )(order, far_memory(stamps))


def pair_tile(ref, first, second):
    samples = ref.shape[0]
    lane = lax.broadcasted_iota(jnp.int32, (samples, LANES), 1)

    def placed(block, upper):
        start = pl.multiple_of((block // 2) * LANES, LANES)
        tile = ref[:, pl.ds(start, LANES)]
        turned = pltpu.roll(tile, HALF, 1)
        return jnp.where((block & 1) == upper, tile, turned)

    return jnp.where(lane < HALF, placed(first, 0), placed(second, 1))


def gather_blocks(targets, send_ref, field_ref, out_refs, order_ref=None):
    slots = send_ref.shape[0]
    for d, out_ref in zip(targets, out_refs):
        for j in range(0, slots, 2):
            first, second = send_ref[j, d], send_ref[j + 1, d]
            if order_ref is not None:
                first, second = order_ref[1, first], order_ref[1, second]
            out_ref[:, j * HALF : j * HALF + LANES] = pair_tile(field_ref, first, second)


def halo_offsets(domains):
    return sorted(range(1, domains), key=lambda k: (-(k >= domains // 2), k if k >= domains // 2 else -k))


def few(domains):
    return domains <= 8 and domains & (domains - 1) == 0


def gather_all(domains, send_ref, field_ref, out_refs, order_ref=None):
    if few(domains):
        me = lax.axis_index("dom")
        gather_blocks([me ^ k for k in halo_offsets(domains)], send_ref, field_ref, out_refs, order_ref)
    else:
        gather_blocks(range(domains), send_ref, field_ref, [out_refs[0].at[d] for d in range(domains)], order_ref)


COPIES = 4


WORD = 32


def order_rows(domains, send_ref, order_ref):
    rows = order_ref.shape[1]
    masks = [jnp.int32(0)] * (rows // WORD)
    if few(domains):
        me = lax.axis_index("dom")
        for d in range(domains):
            for j in range(send_ref.shape[0]):
                block = send_ref[j, d]
                bit = jnp.where(d == me, 0, jnp.left_shift(jnp.int32(1), block & (WORD - 1)))
                masks = [m | jnp.where(block // WORD == n, bit, 0) for n, m in enumerate(masks)]
    flags = [lax.shift_right_logical(masks[row // WORD], jnp.int32(row % WORD)) & 1 for row in range(rows)]
    first = jnp.int32(0)
    later = sum(flags)
    for row, flag in enumerate(flags):
        position = jnp.where(flag == 1, first, later)
        order_ref[0, position] = row
        order_ref[1, row] = position
        first = first + flag
        later = later + 1 - flag


def gather_kernel(domains, send_hbm, field_hbm, field_ref, order_ref, *refs):
    *out_refs, field_sem, send_ref, send_sem = refs
    table = pltpu.make_async_copy(send_hbm, send_ref, send_sem)
    table.start()
    width = field_ref.shape[1] // COPIES
    copies = []
    for n in range(COPIES):
        inside = pl.ds(n * width, width)
        copies.append(pltpu.make_async_copy(field_hbm.at[:, inside], field_ref.at[:, inside], field_sem.at[n]))
        copies[-1].start()
    table.wait()
    for copy in copies:
        copy.wait()
    gather_all(domains, send_ref, field_ref, out_refs)
    order_rows(domains, send_ref, order_ref)


def gather(send, field, rows, domains, outputs):
    table = jax.ShapeDtypeStruct((2, rows), jnp.int32)
    return pl.pallas_call(
        functools.partial(gather_kernel, domains),
        in_specs=[pl.BlockSpec(memory_space=pl.ANY)] * 2,
        out_specs=[whole(), scalars()] + [whole()] * len(outputs),
        out_shape=[
            pltpu.VMEM(field.shape, field.dtype),
            table,
            *[pltpu.VMEM(shape, dtype) for shape, dtype in outputs],
        ],
        scratch_shapes=[
            pltpu.SemaphoreType.DMA((COPIES,)),
            pltpu.SMEM(send.shape, send.dtype),
            pltpu.SemaphoreType.DMA,
        ],
        compiler_params=pltpu.CompilerParams(vmem_limit_bytes=LIMIT),
        name="gather",
    )(far_memory(send), far_memory(field))


def store_tile(ext, index, x):
    high, low = split(x)
    ext[0, index] = jnp.concatenate([high, low], axis=0)
    high, low = split(pltpu.roll(x, HALF, 1))
    ext[1, index] = jnp.concatenate([high, low], axis=0)


def arrange_kernel(first_row, order_ref, field_ref, g_ref, c_ref, g_out, c_out):
    samples = field_ref.shape[0]
    lane = lax.broadcasted_iota(jnp.int32, (samples, LANES), 1)

    def placed(block, upper):
        here = pl.ds(pl.multiple_of((block // 2) * LANES, LANES), LANES)
        own = field_ref[:, here]
        keep = (block & 1) == upper
        return [jnp.where(keep, x, pltpu.roll(x, HALF, 1)) for x in (g_ref[:, here] * own, c_ref[:, here] * own)]

    for i in range(g_out.shape[1] // LANES):
        inside = slice(i * LANES, (i + 1) * LANES)
        low = placed(order_ref[0, first_row + 2 * i], 0)
        high = placed(order_ref[0, first_row + 2 * i + 1], 1)
        g_out[:, inside] = jnp.where(lane < HALF, low[0], high[0])
        c_out[:, inside] = jnp.where(lane < HALF, low[1], high[1])


def restore_kernel(order_ref, u_ref, out_ref):
    for i in range(u_ref.shape[1] // LANES):
        inside = slice(i * LANES, (i + 1) * LANES)
        out_ref[:, inside] = pair_tile(u_ref, order_ref[1, 2 * i], order_ref[1, 2 * i + 1])


def first_extend_kernel(groups, field_ref, ext, near_ref, far_ref):
    extend_kernel(field_ref, ext)
    tables_kernel(groups, near_ref, far_ref)


def extend_kernel(field_ref, ext):
    for i in range(field_ref.shape[1] // LANES):
        store_tile(ext, i, field_ref[:, i * LANES : (i + 1) * LANES])


def extend_arrived(domains, own_tiles, inc_refs, ext):
    if few(domains):
        me = lax.axis_index("dom")
        arrived = [(me ^ k, ref) for k, ref in zip(halo_offsets(domains), inc_refs)]
    else:
        arrived = [(d, inc_refs[0].at[d]) for d in range(domains)]
    for source, ref in arrived:
        per_domain = ref.shape[1] // LANES
        for j in range(per_domain):
            store_tile(ext, own_tiles + source * per_domain + j, ref[:, j * LANES : (j + 1) * LANES])


def with_arrived(domains, product, own_tiles, cols_near, order_near, *refs):
    *inputs, out_ext, p_ref, q_ref, cols_ref, cols_sem, order_ref, order_sem = refs
    tables = [
        pltpu.make_async_copy(cols_near, cols_ref, cols_sem),
        pltpu.make_async_copy(order_near, order_ref, order_sem),
    ]
    for table in tables:
        table.start()
    offsets = domains - 1 if few(domains) else 1
    own_ext, *inputs = inputs
    extend_arrived(domains, own_tiles, inputs[len(inputs) - offsets :], out_ext)
    for table in tables:
        table.wait()
    product(cols_ref, order_ref, out_ext, *inputs[: len(inputs) - offsets], p_ref, q_ref)


def product_rows(first_row, permuted, cols_ref, order_ref, ext, w_ref, p_ref, q_ref, own_terms):
    samples = p_ref.shape[0]
    per_entry = cols_ref.shape[0]
    lane = lax.broadcasted_iota(jnp.int32, (2 * samples, LANES), 1)
    low_lane = lax.broadcasted_iota(jnp.int32, (samples, LANES), 1) < HALF

    rows = cols_ref.shape[1]

    def entry_of(k, row):
        entry = cols_ref[k, row]
        if permuted:
            return entry
        return jnp.where(entry < rows, order_ref[1, jnp.minimum(entry, rows - 1)], entry)

    def row_product(row):
        source, place = (order_ref[0, row], row) if permuted else (row, order_ref[1, row])
        parts = []
        for k in range(0, per_entry, 2):
            first = entry_of(k, source)
            second = entry_of(k + 1, source)
            a = ext[first & 1, first // 2]
            b = ext[1 - (second & 1), second // 2]
            parts.append(jnp.where(lane < HALF, a, b))
        left = jnp.concatenate(parts, axis=1)
        full = jnp.dot(left, w_ref[place], preferred_element_type=jnp.float32)
        width = full.shape[1] // 2
        both = full[:, :width] + full[:, width:]
        return both[:samples] + both[samples:]

    count = p_ref.shape[1] // HALF
    group = max(n for n in range(2, GROUP + 1, 2) if count % n == 0)

    def block(step, carry):
        for pair in range(group // 2):
            row = step * group + 2 * pair
            first = row_product(first_row + row)
            second = row_product(first_row + row + 1)
            direct = jnp.where(low_lane, first, pltpu.roll(second, HALF, 1))
            charge = jnp.where(low_lane, pltpu.roll(first, HALF, 1), second)
            here = pl.ds(pl.multiple_of(row * HALF, LANES), LANES)
            g_term, c_term = own_terms(row)
            p_ref[:, here] = direct + g_term
            q_ref[:, here] = charge + c_term
        return carry

    lax.fori_loop(0, count // group, block, 0)


def permuted_product(first_row, base_row, cols_ref, order_ref, ext, w_ref, g_ref, c_ref, p_ref, q_ref):
    def own_terms(row):
        there = pl.ds(pl.multiple_of((first_row - base_row + row) * HALF, LANES), LANES)
        return g_ref[:, there], c_ref[:, there]

    product_rows(first_row, True, cols_ref, order_ref, ext, w_ref, p_ref, q_ref, own_terms)


def plain_product(first_row, cols_ref, order_ref, ext, w_ref, field_ref, g_ref, c_ref, p_ref, q_ref):
    def own_terms(row):
        there = pl.ds(pl.multiple_of((first_row + row) * HALF, LANES), LANES)
        own = pair_tile(field_ref, order_ref[1, first_row + row], order_ref[1, first_row + row + 1])
        return g_ref[:, there] * own, c_ref[:, there] * own

    product_rows(first_row, False, cols_ref, order_ref, ext, w_ref, p_ref, q_ref, own_terms)


def slope_columns(matrix, charges):
    samples = charges[0].shape[0]
    parts = [split(x) for x in charges]
    high = jnp.concatenate([h for h, _ in parts], axis=0)
    low = jnp.concatenate([l for _, l in parts], axis=0)
    first = jnp.dot(matrix, high, preferred_element_type=jnp.float32)
    second = jnp.dot(matrix[:samples], low, preferred_element_type=jnp.float32)
    return first[:samples] + first[samples:] + second


CHUNK = 256


def near_kernel(chunks, *refs):
    matrix = refs[0][...]
    p_refs, q_refs, mate_refs, out_refs = [refs[1 + n * chunks : 1 + (n + 1) * chunks] for n in range(4)]
    for p_ref, q_ref, mate_ref, out_ref in zip(p_refs, q_refs, mate_refs, out_refs):
        for start in range(0, p_ref.shape[1], CHUNK):
            inside = slice(start, start + CHUNK)
            out_ref[:, inside] = p_ref[:, inside] + slope_columns(matrix, [q_ref[:, inside], mate_ref[:, inside]])


def far_columns(matrix, p_ref, charge_refs):
    for start in range(0, p_ref.shape[1], CHUNK):
        inside = slice(start, start + CHUNK)
        yield start, p_ref[:, inside] + slope_columns(matrix, [c[:, inside] for c in charge_refs])


def far_kernel(count, base, chunks, *refs):
    matrix = refs[0][...]
    out_ref = refs[-1]
    size = 1 + count
    for n in range(chunks):
        p_ref, *charge_refs = refs[1 + n * size : 1 + (n + 1) * size]
        for start, value in far_columns(matrix, p_ref, charge_refs):
            out_ref[:, base + start : base + start + CHUNK] = value
        base += p_ref.shape[1]


def far_send_kernel(count, chunks, domains, send_near, order_near, *refs):
    size = 1 + count
    u_ref, *out_refs, send_ref, send_sem, order_ref, order_sem = refs[1 + chunks * size :]
    tables = [
        pltpu.make_async_copy(send_near, send_ref, send_sem),
        pltpu.make_async_copy(order_near, order_ref, order_sem),
    ]
    for table in tables:
        table.start()
    far_kernel(count, 0, chunks, *refs[: 1 + chunks * size], u_ref)
    for table in tables:
        table.wait()
    gather_all(domains, send_ref, u_ref, out_refs, order_ref)


def dot_totals(totals, r_ref, u_ref, base, v):
    for i in range(0, v.shape[1], LANES):
        vv = v[:, i : i + LANES]
        rr = r_ref[:, base + i : base + i + LANES]
        uu = u_ref[:, base + i : base + i + LANES]
        for n, (a, b) in enumerate(((uu, uu), (uu, vv), (vv, vv), (rr, uu), (rr, vv))):
            totals[n] = totals[n] + a * b


def far_dots_kernel(count, base, chunks, *refs):
    matrix = refs[0][...]
    out_ref = refs[-1]
    size = 1 + count
    r_ref, u_ref, *before = refs[1 + chunks * size : -1]
    samples = r_ref.shape[0]
    totals = [before[0][n] if before else jnp.zeros((samples, LANES), jnp.float32) for n in range(5)]
    for n in range(chunks):
        p_ref, *charge_refs = refs[1 + n * size : 1 + (n + 1) * size]
        for start, value in far_columns(matrix, p_ref, charge_refs):
            dot_totals(totals, r_ref, u_ref, base + start, value)
        base += p_ref.shape[1]
    if base < u_ref.shape[1]:
        for n in range(5):
            out_ref[n] = totals[n]
        return
    lane = lax.broadcasted_iota(jnp.int32, (1, LANES), 1)
    packed = jnp.zeros((1, LANES), jnp.float32)
    for n, total in enumerate(totals):
        packed = jnp.where(lane == n, jnp.sum(total), packed)
    for d in range(out_ref.shape[0]):
        out_ref[d] = packed


def update_kernel(sums_ref, r_ref, u_ref, out_hbm, out_ref, sems):
    total = jnp.sum(sums_ref[...], axis=0)
    lane = lax.broadcasted_iota(jnp.int32, total.shape, 1)
    uu, uv, vv, ru, rv = [jnp.sum(jnp.where(lane == n, total, 0.0), axis=1, keepdims=True) for n in range(5)]
    length_u = jnp.sqrt(uu)
    length_v = jnp.sqrt(vv)
    cross = uv / length_u / length_v
    target_u = ru / length_u
    target_v = rv / length_v
    determinant = 1.0 - cross * cross
    weight_r = (target_u - cross * target_v) / determinant / length_u
    weight_u = (target_v - cross * target_u) / determinant / length_v
    part = r_ref.shape[0] // COPIES
    copies = []
    for n in range(COPIES):
        rows = slice(n * part, (n + 1) * part)
        for start in range(0, r_ref.shape[1], LANES):
            inside = slice(start, start + LANES)
            out_ref[rows, inside] = weight_r * r_ref[rows, inside] + weight_u * u_ref[rows, inside]
        copies.append(pltpu.make_async_copy(out_ref.at[rows], out_hbm.at[rows], sems.at[n]))
        copies[-1].start()
    for copy in copies:
        copy.wait()


def update(sums, r, u):
    return pl.pallas_call(
        update_kernel,
        in_specs=[whole()] * 3,
        out_specs=pl.BlockSpec(memory_space=pl.ANY),
        out_shape=jax.ShapeDtypeStruct(r.shape, r.dtype),
        scratch_shapes=[pltpu.VMEM(r.shape, r.dtype), pltpu.SemaphoreType.DMA((COPIES,))],
        compiler_params=pltpu.CompilerParams(vmem_limit_bytes=LIMIT),
        name="update",
    )(near_memory(sums), near_memory(r), near_memory(u))


def chunk_sizes(rows, domains, slots):
    unit = rows // 8
    early = (domains - 1) * slots if few(domains) else 3 * unit
    return [unit, early - unit, rows - early], [unit, rows // 16 * 3, 2 * unit, rows // 16 * 5, unit]


def body(residual, conductance, capacitance, stamps, block_cols, send_blocks):
    samples, unknowns = residual.shape
    rows, per_entry = block_cols.shape
    width = stamps.shape[2]
    slots = send_blocks.shape[2]
    domains = lax.axis_size("dom")
    groups = lax.axis_size("samp")
    pairs = [(i, i ^ 1) for i in range(groups)]
    shifts = range(2, groups, 2)
    count = 2 * len(shifts)
    sizes_one, sizes_two = chunk_sizes(rows, domains, slots)
    early = sizes_one[0] + sizes_one[1]
    f32 = jnp.float32
    if few(domains):
        outgoing_shapes = [((samples, slots * width), f32)] * (domains - 1)
    else:
        outgoing_shapes = [((domains, samples, slots * width), f32)]
    field_shape = ((samples, unknowns), f32)
    own_tiles = unknowns // LANES
    tiles = own_tiles + domains * slots * width // LANES
    ext_shape = ((2, tiles, 2 * samples, LANES), jnp.bfloat16)
    weight_shape = ((rows, per_entry * width, 4 * width), jnp.bfloat16)
    cols = block_cols.T
    send = send_blocks[0].T

    def exchange(outgoing):
        if not few(domains):
            return [lax.all_to_all(outgoing[0], "dom", split_axis=0, concat_axis=0, tiled=True)]
        incoming = []
        for k, x in zip(halo_offsets(domains), outgoing):
            incoming.append(lax.ppermute(x, "dom", [(i, i ^ k) for i in range(domains)]))
        return incoming

    def product_call(n, size, product, operands, incoming):
        shape = ((samples, size * width), f32)
        if n:
            p, q = kernel_call(product, operands, [shape, shape])
            return operands[2], p, q
        return kernel_call(
            functools.partial(with_arrived, domains, product, own_tiles),
            (*operands, *incoming),
            [ext_shape, shape, shape],
            aliases={2: 0},
            table_copied=True,
        )

    def spread(q):
        far = [lax.ppermute(q, "samp", [(i, (i + k) % groups) for i in range(groups)]) for k in shifts]
        return far, lax.ppermute(q, "samp", pairs)

    def near_call(chunks):
        return kernel_call(
            functools.partial(near_kernel, len(chunks)),
            (near_matrix, *[p for p, _, _, _ in chunks], *[q for _, q, _, _ in chunks], *[m for _, _, _, m in chunks]),
            [(p.shape, f32) for p, _, _, _ in chunks],
        )

    def forward(half, far):
        charges = []
        for x in far:
            charges += [x, lax.ppermute(x, "samp", pairs)]
        return [half, *charges]

    field, order, *outgoing = gather(send, residual, rows, domains, outgoing_shapes)
    incoming = exchange(outgoing)
    blocks = stamps.reshape(rows, per_entry * width, 2 * width)
    ext, near_matrix, far_matrix = kernel_call(
        functools.partial(first_extend_kernel, groups),
        (field,),
        [
            ext_shape,
            ((2 * samples, 2 * samples), jnp.bfloat16),
            ((2 * samples, count * samples), jnp.bfloat16),
        ],
    )
    weights = None
    own = []
    for n, (low, high) in enumerate(((0, early), (early, rows))):
        if n == 0:
            weights = fetch(order, blocks, early)
        else:
            (weights,) = kernel_call(
                functools.partial(prepare_kernel, low, high), (order, blocks, weights), [weight_shape], aliases={2: 0}
            )
        terms = kernel_call(
            functools.partial(arrange_kernel, low),
            (order, field, conductance, capacitance),
            [((samples, (high - low) * width), f32)] * 2,
        )
        own.append((low, weights, terms))
    chunks = []
    first = 0
    for n, size in enumerate(sizes_one):
        base, w, terms = own[first >= early]
        ext, p, q = product_call(
            n, size, functools.partial(permuted_product, first, base), (cols, order, ext, w, *terms), incoming
        )
        chunks.append((p, q, *spread(q)))
        first += size
    half = near_call(chunks[:2]) + near_call(chunks[2:])
    pieces = [forward(half[n], chunk[2]) for n, chunk in enumerate(chunks)]
    ready = 2 if few(domains) else len(chunks)
    u, *outgoing = kernel_call(
        functools.partial(far_send_kernel, count, ready, domains),
        (send, order, far_matrix, *[x for piece in pieces[:ready] for x in piece]),
        [field_shape, *outgoing_shapes],
        table_copied=True,
    )
    incoming = exchange(outgoing)
    if ready < len(chunks):
        operands = [far_matrix, *[x for piece in pieces[ready:] for x in piece]]
        (u,) = kernel_call(
            functools.partial(far_kernel, count, early * width, len(chunks) - ready),
            operands + [u],
            [field_shape],
            aliases={len(operands): 0},
        )
    (ext,) = kernel_call(extend_kernel, (u,), [ext_shape])
    chunks = []
    first = 0
    for n, size in enumerate(sizes_two):
        operands = (cols, order, ext, weights, u, conductance, capacitance)
        ext, p, q = product_call(n, size, functools.partial(plain_product, first), operands, incoming)
        chunks.append((p, q, *spread(q)))
        first += size
    (u,) = kernel_call(restore_kernel, (order, u), [field_shape])
    half = near_call(chunks)
    pieces = [forward(half[n], chunk[2]) for n, chunk in enumerate(chunks)]
    sums = None
    last = len(chunks) - 1
    for n, (low, high) in enumerate(((0, last - 1), (last - 1, last), (last, last + 1))):
        final = high > last
        (sums,) = kernel_call(
            functools.partial(far_dots_kernel, count, sum(sizes_two[:low]) * width, high - low),
            [far_matrix, *[x for piece in pieces[low:high] for x in piece], field, u] + [sums] * (n > 0),
            [((domains * groups, 1, LANES) if final else (5, samples, LANES), f32)],
        )
    sums = lax.all_to_all(sums, ("dom", "samp"), split_axis=0, concat_axis=0, tiled=True)
    return update(sums, field, u)


def solution(mesh):
    in_specs = (
        P("samp", "dom"),
        P("samp", "dom"),
        P("samp", "dom"),
        P("dom", None, None, None),
        P("dom", None),
        P("dom", None, None),
    )
    out_specs = P("samp", "dom")
    return jax.shard_map(body, mesh=mesh, in_specs=in_specs, out_specs=out_specs, check_vma=False)
```

```python
import functools

import jax
import jax.numpy as jnp
from jax import lax
from jax.experimental import pallas as pl
from jax.experimental.pallas import tpu as pltpu
from jax.sharding import PartitionSpec as P


LANES = 128
HALF = 64
GROUP = 12


LIMIT = 24 * 1024 * 1024


def whole():
    return pl.BlockSpec(memory_space=pltpu.VMEM)


def scalars():
    return pl.BlockSpec(memory_space=pltpu.SMEM)


def near_memory(x):
    return pltpu.with_memory_space_constraint(x, pltpu.VMEM)


def far_memory(x):
    return pltpu.with_memory_space_constraint(x, pltpu.HBM)


def kernel_call(kernel, inputs, outputs, aliases=None, table_copied=False):
    specs = []
    operands = []
    scratch = []
    for x in inputs:
        if x.dtype == jnp.int32 and table_copied:
            specs.append(pl.BlockSpec(memory_space=pl.ANY))
            operands.append(near_memory(x))
            scratch += [pltpu.SMEM(x.shape, x.dtype), pltpu.SemaphoreType.DMA]
        elif x.dtype == jnp.int32:
            specs.append(scalars())
            operands.append(x)
        else:
            specs.append(whole())
            operands.append(near_memory(x))
    integer = [dtype == jnp.int32 for _, dtype in outputs]
    out = [
        jax.ShapeDtypeStruct(shape, dtype) if number else pltpu.VMEM(shape, dtype)
        for (shape, dtype), number in zip(outputs, integer)
    ]
    return pl.pallas_call(
        kernel,
        in_specs=specs,
        out_specs=[scalars() if number else whole() for number in integer],
        out_shape=out,
        input_output_aliases=aliases or {},
        scratch_shapes=scratch,
        compiler_params=pltpu.CompilerParams(vmem_limit_bytes=LIMIT),
    )(*operands)


def split(x):
    high = x.astype(jnp.bfloat16)
    low = (x - high.astype(jnp.float32)).astype(jnp.bfloat16)
    return high, low


def spectral_rows(me, sources, samples, period):
    row = me * samples + lax.broadcasted_iota(jnp.int32, (samples, samples), 0)
    column = lax.broadcasted_iota(jnp.int32, (samples, samples), 1)
    blocks = []
    for source in sources:
        offset = row - (source * samples + column)
        sign = (1 - 2 * (offset & 1)).astype(jnp.float32)
        angle = jnp.pi / period * offset.astype(jnp.float32)
        nonzero = offset != 0
        safe = jnp.where(nonzero, angle, 0.5)
        value = sign * jnp.cos(safe) / jnp.sin(safe) / period
        blocks.append(jnp.where(nonzero, value, 0.0))
    high, low = split(jnp.concatenate(blocks, axis=1))
    return jnp.concatenate([high, low], axis=0)


def tables_kernel(groups, near_ref, far_ref):
    samples = near_ref.shape[1] // 2
    me = lax.axis_index("samp")
    partner = me + 1 - 2 * (me & 1)
    near_ref[...] = spectral_rows(me, [me, partner], samples, samples * groups)
    far = []
    for k in range(2, groups, 2):
        for source in (me - k, partner - k):
            far.append(jnp.where(source < 0, source + groups, source))
    far_ref[...] = spectral_rows(me, far, samples, samples * groups)


def prepare_kernel(first_row, last_row, order_ref, stamps_ref, *refs):
    out_ref = refs[-1]
    width = stamps_ref.shape[2]

    def convert(row, carry):
        high, low = split(stamps_ref[order_ref[0, row]])
        out_ref[row, :, :width] = high
        out_ref[row, :, width:] = low
        return carry

    lax.fori_loop(first_row, last_row, convert, 0, unroll=2)


def fetch_kernel(domains, groups, send_ref, field_ref, stamps_hbm, order_ref, out_ref, *refs):
    ext, near_ref, far_ref, buffer, sems = refs
    order_rows(domains, send_ref, order_ref)
    rows, _, width = buffer.shape
    copies = []
    for n in range(rows):
        copies.append(pltpu.make_async_copy(stamps_hbm.at[order_ref[0, n]], buffer.at[n], sems.at[n]))
        copies[-1].start()
    extend_kernel(field_ref, ext)
    tables_kernel(groups, near_ref, far_ref)
    for n, copy in enumerate(copies):
        copy.wait()
        high, low = split(buffer[n])
        out_ref[n, :, :width] = high
        out_ref[n, :, width:] = low


def fetch(send, field, stamps, rows, domains, groups, outputs):
    total, depth, width = stamps.shape
    return pl.pallas_call(
        functools.partial(fetch_kernel, domains, groups),
        in_specs=[scalars(), whole(), pl.BlockSpec(memory_space=pl.ANY)],
        out_specs=[scalars()] + [whole()] * (1 + len(outputs)),
        out_shape=[
            jax.ShapeDtypeStruct((2, total), jnp.int32),
            pltpu.VMEM((total, depth, 2 * width), jnp.bfloat16),
            *[pltpu.VMEM(shape, dtype) for shape, dtype in outputs],
        ],
        scratch_shapes=[pltpu.VMEM((rows, depth, width), stamps.dtype), pltpu.SemaphoreType.DMA((rows,))],
        compiler_params=pltpu.CompilerParams(vmem_limit_bytes=LIMIT),
        name="prepare_0",
    )(far_memory(send), near_memory(field), far_memory(stamps))


def pair_tile(ref, first, second):
    samples = ref.shape[0]
    lane = lax.broadcasted_iota(jnp.int32, (samples, LANES), 1)

    def placed(block, upper):
        start = pl.multiple_of((block // 2) * LANES, LANES)
        tile = ref[:, pl.ds(start, LANES)]
        turned = pltpu.roll(tile, HALF, 1)
        return jnp.where((block & 1) == upper, tile, turned)

    return jnp.where(lane < HALF, placed(first, 0), placed(second, 1))


def gather_blocks(targets, send_ref, field_ref, out_refs, order_ref=None):
    slots = send_ref.shape[0]
    for d, out_ref in zip(targets, out_refs):
        for j in range(0, slots, 2):
            first, second = send_ref[j, d], send_ref[j + 1, d]
            if order_ref is not None:
                first, second = order_ref[1, first], order_ref[1, second]
            out_ref[:, j * HALF : j * HALF + LANES] = pair_tile(field_ref, first, second)


def halo_offsets(domains):
    return sorted(range(1, domains), key=lambda k: (-(k >= domains // 2), k if k >= domains // 2 else -k))


def few(domains):
    return domains <= 8 and domains & (domains - 1) == 0


def gather_all(domains, send_ref, field_ref, out_refs, order_ref=None):
    if few(domains):
        me = lax.axis_index("dom")
        gather_blocks([me ^ k for k in halo_offsets(domains)], send_ref, field_ref, out_refs, order_ref)
    else:
        gather_blocks(range(domains), send_ref, field_ref, [out_refs[0].at[d] for d in range(domains)], order_ref)


COPIES = 4


WORD = 32


def order_rows(domains, send_ref, order_ref):
    rows = order_ref.shape[1]
    masks = [jnp.int32(0)] * (rows // WORD)
    if few(domains):
        me = lax.axis_index("dom")
        for d in range(domains):
            for j in range(send_ref.shape[0]):
                block = send_ref[j, d]
                bit = jnp.where(d == me, 0, jnp.left_shift(jnp.int32(1), block & (WORD - 1)))
                masks = [m | jnp.where(block // WORD == n, bit, 0) for n, m in enumerate(masks)]
    flags = [lax.shift_right_logical(masks[row // WORD], jnp.int32(row % WORD)) & 1 for row in range(rows)]
    first = jnp.int32(0)
    later = sum(flags)
    for row, flag in enumerate(flags):
        position = jnp.where(flag == 1, first, later)
        order_ref[0, position] = row
        order_ref[1, row] = position
        first = first + flag
        later = later + 1 - flag


def gather_kernel(domains, send_hbm, field_hbm, field_ref, *refs):
    *out_refs, field_sem, send_ref, send_sem = refs
    table = pltpu.make_async_copy(send_hbm, send_ref, send_sem)
    table.start()
    width = field_ref.shape[1] // COPIES
    copies = []
    for n in range(COPIES):
        inside = pl.ds(n * width, width)
        copies.append(pltpu.make_async_copy(field_hbm.at[:, inside], field_ref.at[:, inside], field_sem.at[n]))
        copies[-1].start()
    table.wait()
    for copy in copies:
        copy.wait()
    gather_all(domains, send_ref, field_ref, out_refs)


def gather(send, field, domains, outputs):
    return pl.pallas_call(
        functools.partial(gather_kernel, domains),
        in_specs=[pl.BlockSpec(memory_space=pl.ANY)] * 2,
        out_specs=[whole()] * (1 + len(outputs)),
        out_shape=[pltpu.VMEM(shape, dtype) for shape, dtype in ((field.shape, field.dtype), *outputs)],
        scratch_shapes=[
            pltpu.SemaphoreType.DMA((COPIES,)),
            pltpu.SMEM(send.shape, send.dtype),
            pltpu.SemaphoreType.DMA,
        ],
        compiler_params=pltpu.CompilerParams(vmem_limit_bytes=LIMIT),
        name="gather",
    )(far_memory(send), far_memory(field))


def store_tile(ext, index, x):
    high, low = split(x)
    ext[0, index] = jnp.concatenate([high, low], axis=0)
    high, low = split(pltpu.roll(x, HALF, 1))
    ext[1, index] = jnp.concatenate([high, low], axis=0)


def arrange_kernel(first_row, order_ref, field_ref, g_ref, c_ref, g_out, c_out):
    samples = field_ref.shape[0]
    lane = lax.broadcasted_iota(jnp.int32, (samples, LANES), 1)

    def placed(block, upper):
        here = pl.ds(pl.multiple_of((block // 2) * LANES, LANES), LANES)
        own = field_ref[:, here]
        keep = (block & 1) == upper
        return [jnp.where(keep, x, pltpu.roll(x, HALF, 1)) for x in (g_ref[:, here] * own, c_ref[:, here] * own)]

    for i in range(g_out.shape[1] // LANES):
        inside = slice(i * LANES, (i + 1) * LANES)
        low = placed(order_ref[0, first_row + 2 * i], 0)
        high = placed(order_ref[0, first_row + 2 * i + 1], 1)
        g_out[:, inside] = jnp.where(lane < HALF, low[0], high[0])
        c_out[:, inside] = jnp.where(lane < HALF, low[1], high[1])


def restore_kernel(order_ref, u_ref, out_ref):
    for i in range(u_ref.shape[1] // LANES):
        inside = slice(i * LANES, (i + 1) * LANES)
        out_ref[:, inside] = pair_tile(u_ref, order_ref[1, 2 * i], order_ref[1, 2 * i + 1])


def extend_kernel(field_ref, ext):
    for i in range(field_ref.shape[1] // LANES):
        store_tile(ext, i, field_ref[:, i * LANES : (i + 1) * LANES])


def extend_arrived(domains, own_tiles, inc_refs, ext):
    if few(domains):
        me = lax.axis_index("dom")
        arrived = [(me ^ k, ref) for k, ref in zip(halo_offsets(domains), inc_refs)]
    else:
        arrived = [(d, inc_refs[0].at[d]) for d in range(domains)]
    for source, ref in arrived:
        per_domain = ref.shape[1] // LANES
        for j in range(per_domain):
            store_tile(ext, own_tiles + source * per_domain + j, ref[:, j * LANES : (j + 1) * LANES])


def with_arrived(domains, product, own_tiles, cols_near, order_near, *refs):
    *inputs, out_ext, p_ref, q_ref, cols_ref, cols_sem, order_ref, order_sem = refs
    tables = [
        pltpu.make_async_copy(cols_near, cols_ref, cols_sem),
        pltpu.make_async_copy(order_near, order_ref, order_sem),
    ]
    for table in tables:
        table.start()
    offsets = domains - 1 if few(domains) else 1
    own_ext, *inputs = inputs
    extend_arrived(domains, own_tiles, inputs[len(inputs) - offsets :], out_ext)
    for table in tables:
        table.wait()
    product(cols_ref, order_ref, out_ext, *inputs[: len(inputs) - offsets], p_ref, q_ref)


def product_rows(first_row, permuted, cols_ref, order_ref, ext, w_ref, p_ref, q_ref, own_terms):
    samples = p_ref.shape[0]
    per_entry = cols_ref.shape[0]
    lane = lax.broadcasted_iota(jnp.int32, (2 * samples, LANES), 1)
    low_lane = lax.broadcasted_iota(jnp.int32, (samples, LANES), 1) < HALF

    rows = cols_ref.shape[1]

    def entry_of(k, row):
        entry = cols_ref[k, row]
        if permuted:
            return entry
        return jnp.where(entry < rows, order_ref[1, jnp.minimum(entry, rows - 1)], entry)

    def row_product(row):
        source, place = (order_ref[0, row], row) if permuted else (row, order_ref[1, row])
        parts = []
        for k in range(0, per_entry, 2):
            first = entry_of(k, source)
            second = entry_of(k + 1, source)
            a = ext[first & 1, first // 2]
            b = ext[1 - (second & 1), second // 2]
            parts.append(jnp.where(lane < HALF, a, b))
        left = jnp.concatenate(parts, axis=1)
        full = jnp.dot(left, w_ref[place], preferred_element_type=jnp.float32)
        width = full.shape[1] // 2
        both = full[:, :width] + full[:, width:]
        return both[:samples] + both[samples:]

    count = p_ref.shape[1] // HALF
    group = max(n for n in range(2, GROUP + 1, 2) if count % n == 0)

    def block(step, carry):
        for pair in range(group // 2):
            row = step * group + 2 * pair
            first = row_product(first_row + row)
            second = row_product(first_row + row + 1)
            direct = jnp.where(low_lane, first, pltpu.roll(second, HALF, 1))
            charge = jnp.where(low_lane, pltpu.roll(first, HALF, 1), second)
            here = pl.ds(pl.multiple_of(row * HALF, LANES), LANES)
            g_term, c_term = own_terms(row)
            p_ref[:, here] = direct + g_term
            q_ref[:, here] = charge + c_term
        return carry

    lax.fori_loop(0, count // group, block, 0)


def permuted_product(first_row, base_row, cols_ref, order_ref, ext, w_ref, g_ref, c_ref, p_ref, q_ref):
    def own_terms(row):
        there = pl.ds(pl.multiple_of((first_row - base_row + row) * HALF, LANES), LANES)
        return g_ref[:, there], c_ref[:, there]

    product_rows(first_row, True, cols_ref, order_ref, ext, w_ref, p_ref, q_ref, own_terms)


def plain_product(first_row, cols_ref, order_ref, ext, w_ref, field_ref, g_ref, c_ref, p_ref, q_ref):
    def own_terms(row):
        there = pl.ds(pl.multiple_of((first_row + row) * HALF, LANES), LANES)
        own = pair_tile(field_ref, order_ref[1, first_row + row], order_ref[1, first_row + row + 1])
        return g_ref[:, there] * own, c_ref[:, there] * own

    product_rows(first_row, False, cols_ref, order_ref, ext, w_ref, p_ref, q_ref, own_terms)


def slope_columns(matrix, charges):
    samples = charges[0].shape[0]
    parts = [split(x) for x in charges]
    high = jnp.concatenate([h for h, _ in parts], axis=0)
    low = jnp.concatenate([l for _, l in parts], axis=0)
    first = jnp.dot(matrix, high, preferred_element_type=jnp.float32)
    second = jnp.dot(matrix[:samples], low, preferred_element_type=jnp.float32)
    return first[:samples] + first[samples:] + second


CHUNK = 256


def near_kernel(chunks, *refs):
    matrix = refs[0][...]
    p_refs, q_refs, mate_refs, out_refs = [refs[1 + n * chunks : 1 + (n + 1) * chunks] for n in range(4)]
    for p_ref, q_ref, mate_ref, out_ref in zip(p_refs, q_refs, mate_refs, out_refs):
        for start in range(0, p_ref.shape[1], CHUNK):
            inside = slice(start, start + CHUNK)
            out_ref[:, inside] = p_ref[:, inside] + slope_columns(matrix, [q_ref[:, inside], mate_ref[:, inside]])


def far_columns(matrix, p_ref, charge_refs):
    for start in range(0, p_ref.shape[1], CHUNK):
        inside = slice(start, start + CHUNK)
        yield start, p_ref[:, inside] + slope_columns(matrix, [c[:, inside] for c in charge_refs])


def far_kernel(count, base, chunks, *refs):
    matrix = refs[0][...]
    out_ref = refs[-1]
    size = 1 + count
    for n in range(chunks):
        p_ref, *charge_refs = refs[1 + n * size : 1 + (n + 1) * size]
        for start, value in far_columns(matrix, p_ref, charge_refs):
            out_ref[:, base + start : base + start + CHUNK] = value
        base += p_ref.shape[1]


def far_send_kernel(count, chunks, domains, send_near, order_near, *refs):
    size = 1 + count
    u_ref, *out_refs, send_ref, send_sem, order_ref, order_sem = refs[1 + chunks * size :]
    tables = [
        pltpu.make_async_copy(send_near, send_ref, send_sem),
        pltpu.make_async_copy(order_near, order_ref, order_sem),
    ]
    for table in tables:
        table.start()
    far_kernel(count, 0, chunks, *refs[: 1 + chunks * size], u_ref)
    for table in tables:
        table.wait()
    gather_all(domains, send_ref, u_ref, out_refs, order_ref)


def dot_totals(totals, r_ref, u_ref, base, v):
    for i in range(0, v.shape[1], LANES):
        vv = v[:, i : i + LANES]
        rr = r_ref[:, base + i : base + i + LANES]
        uu = u_ref[:, base + i : base + i + LANES]
        for n, (a, b) in enumerate(((uu, uu), (uu, vv), (vv, vv), (rr, uu), (rr, vv))):
            totals[n] = totals[n] + a * b


def far_dots_kernel(count, base, chunks, *refs):
    matrix = refs[0][...]
    out_ref = refs[-1]
    size = 1 + count
    r_ref, u_ref, *before = refs[1 + chunks * size : -1]
    samples = r_ref.shape[0]
    totals = [before[0][n] if before else jnp.zeros((samples, LANES), jnp.float32) for n in range(5)]
    for n in range(chunks):
        p_ref, *charge_refs = refs[1 + n * size : 1 + (n + 1) * size]
        for start, value in far_columns(matrix, p_ref, charge_refs):
            dot_totals(totals, r_ref, u_ref, base + start, value)
        base += p_ref.shape[1]
    if base < u_ref.shape[1]:
        for n in range(5):
            out_ref[n] = totals[n]
        return
    lane = lax.broadcasted_iota(jnp.int32, (1, LANES), 1)
    packed = jnp.zeros((1, LANES), jnp.float32)
    for n, total in enumerate(totals):
        packed = jnp.where(lane == n, jnp.sum(total), packed)
    for d in range(out_ref.shape[0]):
        out_ref[d] = packed


def update_kernel(sums_ref, r_ref, u_ref, out_hbm, out_ref, sems):
    total = jnp.sum(sums_ref[...], axis=0)
    lane = lax.broadcasted_iota(jnp.int32, total.shape, 1)
    uu, uv, vv, ru, rv = [jnp.sum(jnp.where(lane == n, total, 0.0), axis=1, keepdims=True) for n in range(5)]
    length_u = jnp.sqrt(uu)
    length_v = jnp.sqrt(vv)
    cross = uv / length_u / length_v
    target_u = ru / length_u
    target_v = rv / length_v
    determinant = 1.0 - cross * cross
    weight_r = (target_u - cross * target_v) / determinant / length_u
    weight_u = (target_v - cross * target_u) / determinant / length_v
    part = r_ref.shape[0] // COPIES
    copies = []
    for n in range(COPIES):
        rows = slice(n * part, (n + 1) * part)
        for start in range(0, r_ref.shape[1], LANES):
            inside = slice(start, start + LANES)
            out_ref[rows, inside] = weight_r * r_ref[rows, inside] + weight_u * u_ref[rows, inside]
        copies.append(pltpu.make_async_copy(out_ref.at[rows], out_hbm.at[rows], sems.at[n]))
        copies[-1].start()
    for copy in copies:
        copy.wait()


def update(sums, r, u):
    return pl.pallas_call(
        update_kernel,
        in_specs=[whole()] * 3,
        out_specs=pl.BlockSpec(memory_space=pl.ANY),
        out_shape=jax.ShapeDtypeStruct(r.shape, r.dtype),
        scratch_shapes=[pltpu.VMEM(r.shape, r.dtype), pltpu.SemaphoreType.DMA((COPIES,))],
        compiler_params=pltpu.CompilerParams(vmem_limit_bytes=LIMIT),
        name="update",
    )(near_memory(sums), near_memory(r), near_memory(u))


def chunk_sizes(rows, domains, slots):
    unit = rows // 8
    early = (domains - 1) * slots if few(domains) else 3 * unit
    return [unit, early - unit, rows - early], [unit, rows // 16 * 3, 2 * unit, rows // 16 * 5, unit]


def body(residual, conductance, capacitance, stamps, block_cols, send_blocks):
    samples, unknowns = residual.shape
    rows, per_entry = block_cols.shape
    width = stamps.shape[2]
    slots = send_blocks.shape[2]
    domains = lax.axis_size("dom")
    groups = lax.axis_size("samp")
    pairs = [(i, i ^ 1) for i in range(groups)]
    shifts = range(2, groups, 2)
    count = 2 * len(shifts)
    sizes_one, sizes_two = chunk_sizes(rows, domains, slots)
    early = sizes_one[0] + sizes_one[1]
    f32 = jnp.float32
    if few(domains):
        outgoing_shapes = [((samples, slots * width), f32)] * (domains - 1)
    else:
        outgoing_shapes = [((domains, samples, slots * width), f32)]
    field_shape = ((samples, unknowns), f32)
    own_tiles = unknowns // LANES
    tiles = own_tiles + domains * slots * width // LANES
    ext_shape = ((2, tiles, 2 * samples, LANES), jnp.bfloat16)
    weight_shape = ((rows, per_entry * width, 4 * width), jnp.bfloat16)
    cols = block_cols.T
    send = send_blocks[0].T

    def exchange(outgoing):
        if not few(domains):
            return [lax.all_to_all(outgoing[0], "dom", split_axis=0, concat_axis=0, tiled=True)]
        incoming = []
        for k, x in zip(halo_offsets(domains), outgoing):
            incoming.append(lax.ppermute(x, "dom", [(i, i ^ k) for i in range(domains)]))
        return incoming

    def product_call(n, size, product, operands, incoming):
        shape = ((samples, size * width), f32)
        if n:
            p, q = kernel_call(product, operands, [shape, shape])
            return operands[2], p, q
        return kernel_call(
            functools.partial(with_arrived, domains, product, own_tiles),
            (*operands, *incoming),
            [ext_shape, shape, shape],
            aliases={2: 0},
            table_copied=True,
        )

    def spread(q):
        far = [lax.ppermute(q, "samp", [(i, (i + k) % groups) for i in range(groups)]) for k in shifts]
        return far, lax.ppermute(q, "samp", pairs)

    def near_call(chunks):
        return kernel_call(
            functools.partial(near_kernel, len(chunks)),
            (near_matrix, *[p for p, _, _, _ in chunks], *[q for _, q, _, _ in chunks], *[m for _, _, _, m in chunks]),
            [(p.shape, f32) for p, _, _, _ in chunks],
        )

    def forward(half, far):
        charges = []
        for x in far:
            charges += [x, lax.ppermute(x, "samp", pairs)]
        return [half, *charges]

    field, *outgoing = gather(send, residual, domains, outgoing_shapes)
    incoming = exchange(outgoing)
    blocks = stamps.reshape(rows, per_entry * width, 2 * width)
    order, weights, ext, near_matrix, far_matrix = fetch(
        send,
        field,
        blocks,
        early,
        domains,
        groups,
        [
            ext_shape,
            ((2 * samples, 2 * samples), jnp.bfloat16),
            ((2 * samples, count * samples), jnp.bfloat16),
        ],
    )
    own = []
    for n, (low, high) in enumerate(((0, early), (early, rows))):
        if n:
            (weights,) = kernel_call(
                functools.partial(prepare_kernel, low, high), (order, blocks, weights), [weight_shape], aliases={2: 0}
            )
        terms = kernel_call(
            functools.partial(arrange_kernel, low),
            (order, field, conductance, capacitance),
            [((samples, (high - low) * width), f32)] * 2,
        )
        own.append((low, weights, terms))
    chunks = []
    first = 0
    for n, size in enumerate(sizes_one):
        base, w, terms = own[first >= early]
        ext, p, q = product_call(
            n, size, functools.partial(permuted_product, first, base), (cols, order, ext, w, *terms), incoming
        )
        chunks.append((p, q, *spread(q)))
        first += size
    half = near_call(chunks[:2]) + near_call(chunks[2:])
    pieces = [forward(half[n], chunk[2]) for n, chunk in enumerate(chunks)]
    ready = 2 if few(domains) else len(chunks)
    u, *outgoing = kernel_call(
        functools.partial(far_send_kernel, count, ready, domains),
        (send, order, far_matrix, *[x for piece in pieces[:ready] for x in piece]),
        [field_shape, *outgoing_shapes],
        table_copied=True,
    )
    incoming = exchange(outgoing)
    if ready < len(chunks):
        operands = [far_matrix, *[x for piece in pieces[ready:] for x in piece]]
        (u,) = kernel_call(
            functools.partial(far_kernel, count, early * width, len(chunks) - ready),
            operands + [u],
            [field_shape],
            aliases={len(operands): 0},
        )
    (ext,) = kernel_call(extend_kernel, (u,), [ext_shape])
    chunks = []
    first = 0
    for n, size in enumerate(sizes_two):
        operands = (cols, order, ext, weights, u, conductance, capacitance)
        ext, p, q = product_call(n, size, functools.partial(plain_product, first), operands, incoming)
        chunks.append((p, q, *spread(q)))
        first += size
    (u,) = kernel_call(restore_kernel, (order, u), [field_shape])
    half = near_call(chunks)
    pieces = [forward(half[n], chunk[2]) for n, chunk in enumerate(chunks)]
    sums = None
    last = len(chunks) - 1
    for n, (low, high) in enumerate(((0, last - 1), (last - 1, last), (last, last + 1))):
        final = high > last
        (sums,) = kernel_call(
            functools.partial(far_dots_kernel, count, sum(sizes_two[:low]) * width, high - low),
            [far_matrix, *[x for piece in pieces[low:high] for x in piece], field, u] + [sums] * (n > 0),
            [((domains * groups, 1, LANES) if final else (5, samples, LANES), f32)],
        )
    sums = lax.all_to_all(sums, ("dom", "samp"), split_axis=0, concat_axis=0, tiled=True)
    return update(sums, field, u)


def solution(mesh):
    in_specs = (
        P("samp", "dom"),
        P("samp", "dom"),
        P("samp", "dom"),
        P("dom", None, None, None),
        P("dom", None),
        P("dom", None, None),
    )
    out_specs = P("samp", "dom")
    return jax.shard_map(body, mesh=mesh, in_specs=in_specs, out_specs=out_specs, check_vma=False)
```

```python
import functools

import jax
import jax.numpy as jnp
from jax import lax
from jax.experimental import pallas as pl
from jax.experimental.pallas import tpu as pltpu
from jax.sharding import PartitionSpec as P


LANES = 128
HALF = 64
GROUP = 12


LIMIT = 24 * 1024 * 1024


def whole():
    return pl.BlockSpec(memory_space=pltpu.VMEM)


def scalars():
    return pl.BlockSpec(memory_space=pltpu.SMEM)


def near_memory(x):
    return pltpu.with_memory_space_constraint(x, pltpu.VMEM)


def far_memory(x):
    return pltpu.with_memory_space_constraint(x, pltpu.HBM)


def kernel_call(kernel, inputs, outputs, aliases=None, table_copied=False):
    specs = []
    operands = []
    scratch = []
    for x in inputs:
        if x.dtype == jnp.int32 and table_copied:
            specs.append(pl.BlockSpec(memory_space=pl.ANY))
            operands.append(near_memory(x))
            scratch += [pltpu.SMEM(x.shape, x.dtype), pltpu.SemaphoreType.DMA]
        elif x.dtype == jnp.int32:
            specs.append(scalars())
            operands.append(x)
        else:
            specs.append(whole())
            operands.append(near_memory(x))
    integer = [dtype == jnp.int32 for _, dtype in outputs]
    out = [
        jax.ShapeDtypeStruct(shape, dtype) if number else pltpu.VMEM(shape, dtype)
        for (shape, dtype), number in zip(outputs, integer)
    ]
    return pl.pallas_call(
        kernel,
        in_specs=specs,
        out_specs=[scalars() if number else whole() for number in integer],
        out_shape=out,
        input_output_aliases=aliases or {},
        scratch_shapes=scratch,
        compiler_params=pltpu.CompilerParams(vmem_limit_bytes=LIMIT),
    )(*operands)


def split(x):
    high = x.astype(jnp.bfloat16)
    low = (x - high.astype(jnp.float32)).astype(jnp.bfloat16)
    return high, low


def spectral_rows(me, sources, samples, period):
    row = me * samples + lax.broadcasted_iota(jnp.int32, (samples, samples), 0)
    column = lax.broadcasted_iota(jnp.int32, (samples, samples), 1)
    blocks = []
    for source in sources:
        offset = row - (source * samples + column)
        sign = (1 - 2 * (offset & 1)).astype(jnp.float32)
        angle = jnp.pi / period * offset.astype(jnp.float32)
        nonzero = offset != 0
        safe = jnp.where(nonzero, angle, 0.5)
        value = sign * jnp.cos(safe) / jnp.sin(safe) / period
        blocks.append(jnp.where(nonzero, value, 0.0))
    high, low = split(jnp.concatenate(blocks, axis=1))
    return jnp.concatenate([high, low], axis=0)


def tables_kernel(groups, near_ref, far_ref):
    samples = near_ref.shape[1] // 2
    me = lax.axis_index("samp")
    partner = me + 1 - 2 * (me & 1)
    near_ref[...] = spectral_rows(me, [me, partner], samples, samples * groups)
    far = []
    for k in range(2, groups, 2):
        for source in (me - k, partner - k):
            far.append(jnp.where(source < 0, source + groups, source))
    far_ref[...] = spectral_rows(me, far, samples, samples * groups)


def prepare_kernel(first_row, last_row, order_ref, stamps_ref, *refs):
    out_ref = refs[-1]
    width = stamps_ref.shape[2]

    def convert(row, carry):
        high, low = split(stamps_ref[order_ref[0, row]])
        out_ref[row, :, :width] = high
        out_ref[row, :, width:] = low
        return carry

    lax.fori_loop(first_row, last_row, convert, 0, unroll=2)


def fetch_kernel(domains, groups, send_ref, field_ref, stamps_hbm, order_ref, out_ref, *refs):
    ext, near_ref, far_ref, buffer, sems = refs
    order_rows(domains, send_ref, order_ref)
    rows, _, width = buffer.shape
    copies = []
    for n in range(rows):
        copies.append(pltpu.make_async_copy(stamps_hbm.at[order_ref[0, n]], buffer.at[n], sems.at[n]))
        copies[-1].start()
    extend_kernel(field_ref, ext)
    tables_kernel(groups, near_ref, far_ref)
    for n, copy in enumerate(copies):
        copy.wait()
        high, low = split(buffer[n])
        out_ref[n, :, :width] = high
        out_ref[n, :, width:] = low


def fetch(send, field, stamps, rows, domains, groups, outputs):
    total, depth, width = stamps.shape
    return pl.pallas_call(
        functools.partial(fetch_kernel, domains, groups),
        in_specs=[scalars(), whole(), pl.BlockSpec(memory_space=pl.ANY)],
        out_specs=[scalars()] + [whole()] * (1 + len(outputs)),
        out_shape=[
            jax.ShapeDtypeStruct((2, total), jnp.int32),
            pltpu.VMEM((total, depth, 2 * width), jnp.bfloat16),
            *[pltpu.VMEM(shape, dtype) for shape, dtype in outputs],
        ],
        scratch_shapes=[pltpu.VMEM((rows, depth, width), stamps.dtype), pltpu.SemaphoreType.DMA((rows,))],
        compiler_params=pltpu.CompilerParams(vmem_limit_bytes=LIMIT),
        name="prepare_0",
    )(far_memory(send), near_memory(field), far_memory(stamps))


def pair_tile(ref, first, second):
    samples = ref.shape[0]
    lane = lax.broadcasted_iota(jnp.int32, (samples, LANES), 1)

    def placed(block, upper):
        start = pl.multiple_of((block // 2) * LANES, LANES)
        tile = ref[:, pl.ds(start, LANES)]
        turned = pltpu.roll(tile, HALF, 1)
        return jnp.where((block & 1) == upper, tile, turned)

    return jnp.where(lane < HALF, placed(first, 0), placed(second, 1))


def gather_blocks(targets, send_ref, field_ref, out_refs, order_ref=None):
    slots = send_ref.shape[0]
    for d, out_ref in zip(targets, out_refs):
        for j in range(0, slots, 2):
            first, second = send_ref[j, d], send_ref[j + 1, d]
            if order_ref is not None:
                first, second = order_ref[1, first], order_ref[1, second]
            out_ref[:, j * HALF : j * HALF + LANES] = pair_tile(field_ref, first, second)


def halo_offsets(domains):
    return sorted(range(1, domains), key=lambda k: (-(k >= domains // 2), k if k >= domains // 2 else -k))


def few(domains):
    return domains <= 8 and domains & (domains - 1) == 0


def gather_all(domains, send_ref, field_ref, out_refs, order_ref=None):
    if few(domains):
        me = lax.axis_index("dom")
        gather_blocks([me ^ k for k in halo_offsets(domains)], send_ref, field_ref, out_refs, order_ref)
    else:
        gather_blocks(range(domains), send_ref, field_ref, [out_refs[0].at[d] for d in range(domains)], order_ref)


COPIES = 4


WORD = 32


def order_rows(domains, send_ref, order_ref):
    rows = order_ref.shape[1]
    masks = [jnp.int32(0)] * (rows // WORD)
    if few(domains):
        me = lax.axis_index("dom")
        for d in range(domains):
            for j in range(send_ref.shape[0]):
                block = send_ref[j, d]
                bit = jnp.where(d == me, 0, jnp.left_shift(jnp.int32(1), block & (WORD - 1)))
                masks = [m | jnp.where(block // WORD == n, bit, 0) for n, m in enumerate(masks)]
    flags = [lax.shift_right_logical(masks[row // WORD], jnp.int32(row % WORD)) & 1 for row in range(rows)]
    first = jnp.int32(0)
    later = sum(flags)
    for row, flag in enumerate(flags):
        position = jnp.where(flag == 1, first, later)
        order_ref[0, position] = row
        order_ref[1, row] = position
        first = first + flag
        later = later + 1 - flag


def gather_kernel(domains, send_hbm, field_hbm, field_ref, *refs):
    *out_refs, field_sem, send_ref, send_sem = refs
    table = pltpu.make_async_copy(send_hbm, send_ref, send_sem)
    table.start()
    width = field_ref.shape[1] // COPIES
    copies = []
    for n in range(COPIES):
        inside = pl.ds(n * width, width)
        copies.append(pltpu.make_async_copy(field_hbm.at[:, inside], field_ref.at[:, inside], field_sem.at[n]))
        copies[-1].start()
    table.wait()
    for copy in copies:
        copy.wait()
    gather_all(domains, send_ref, field_ref, out_refs)


def gather(send, field, domains, outputs):
    return pl.pallas_call(
        functools.partial(gather_kernel, domains),
        in_specs=[pl.BlockSpec(memory_space=pl.ANY)] * 2,
        out_specs=[whole()] * (1 + len(outputs)),
        out_shape=[pltpu.VMEM(shape, dtype) for shape, dtype in ((field.shape, field.dtype), *outputs)],
        scratch_shapes=[
            pltpu.SemaphoreType.DMA((COPIES,)),
            pltpu.SMEM(send.shape, send.dtype),
            pltpu.SemaphoreType.DMA,
        ],
        compiler_params=pltpu.CompilerParams(vmem_limit_bytes=LIMIT),
        name="gather",
    )(far_memory(send), far_memory(field))


def store_tile(ext, index, x):
    high, low = split(x)
    ext[0, index] = jnp.concatenate([high, low], axis=0)
    high, low = split(pltpu.roll(x, HALF, 1))
    ext[1, index] = jnp.concatenate([high, low], axis=0)


def arrange_kernel(first_row, order_ref, field_ref, g_ref, c_ref, g_out, c_out):
    samples = field_ref.shape[0]
    lane = lax.broadcasted_iota(jnp.int32, (samples, LANES), 1)

    def placed(block, upper):
        here = pl.ds(pl.multiple_of((block // 2) * LANES, LANES), LANES)
        own = field_ref[:, here]
        keep = (block & 1) == upper
        return [jnp.where(keep, x, pltpu.roll(x, HALF, 1)) for x in (g_ref[:, here] * own, c_ref[:, here] * own)]

    for i in range(g_out.shape[1] // LANES):
        inside = slice(i * LANES, (i + 1) * LANES)
        low = placed(order_ref[0, first_row + 2 * i], 0)
        high = placed(order_ref[0, first_row + 2 * i + 1], 1)
        g_out[:, inside] = jnp.where(lane < HALF, low[0], high[0])
        c_out[:, inside] = jnp.where(lane < HALF, low[1], high[1])


def restore_kernel(order_ref, u_ref, out_ref):
    for i in range(u_ref.shape[1] // LANES):
        inside = slice(i * LANES, (i + 1) * LANES)
        out_ref[:, inside] = pair_tile(u_ref, order_ref[1, 2 * i], order_ref[1, 2 * i + 1])


def extend_kernel(field_ref, ext):
    for i in range(field_ref.shape[1] // LANES):
        store_tile(ext, i, field_ref[:, i * LANES : (i + 1) * LANES])


def extend_arrived(domains, own_tiles, inc_refs, ext):
    if few(domains):
        me = lax.axis_index("dom")
        arrived = [(me ^ k, ref) for k, ref in zip(halo_offsets(domains), inc_refs)]
    else:
        arrived = [(d, inc_refs[0].at[d]) for d in range(domains)]
    for source, ref in arrived:
        per_domain = ref.shape[1] // LANES
        for j in range(per_domain):
            store_tile(ext, own_tiles + source * per_domain + j, ref[:, j * LANES : (j + 1) * LANES])


def with_arrived(domains, product, own_tiles, cols_near, order_near, *refs):
    *inputs, out_ext, p_ref, q_ref, cols_ref, cols_sem, order_ref, order_sem = refs
    tables = [
        pltpu.make_async_copy(cols_near, cols_ref, cols_sem),
        pltpu.make_async_copy(order_near, order_ref, order_sem),
    ]
    for table in tables:
        table.start()
    offsets = domains - 1 if few(domains) else 1
    own_ext, *inputs = inputs
    extend_arrived(domains, own_tiles, inputs[len(inputs) - offsets :], out_ext)
    for table in tables:
        table.wait()
    product(cols_ref, order_ref, out_ext, *inputs[: len(inputs) - offsets], p_ref, q_ref)


def product_rows(first_row, permuted, cols_ref, order_ref, ext, w_ref, p_ref, q_ref, own_terms):
    samples = p_ref.shape[0]
    per_entry = cols_ref.shape[0]
    lane = lax.broadcasted_iota(jnp.int32, (2 * samples, LANES), 1)
    low_lane = lax.broadcasted_iota(jnp.int32, (samples, LANES), 1) < HALF

    rows = cols_ref.shape[1]

    def entry_of(k, row):
        entry = cols_ref[k, row]
        if permuted:
            return entry
        return jnp.where(entry < rows, order_ref[1, jnp.minimum(entry, rows - 1)], entry)

    def row_product(row):
        source, place = (order_ref[0, row], row) if permuted else (row, order_ref[1, row])
        parts = []
        for k in range(0, per_entry, 2):
            first = entry_of(k, source)
            second = entry_of(k + 1, source)
            a = ext[first & 1, first // 2]
            b = ext[1 - (second & 1), second // 2]
            parts.append(jnp.where(lane < HALF, a, b))
        left = jnp.concatenate(parts, axis=1)
        full = jnp.dot(left, w_ref[place], preferred_element_type=jnp.float32)
        width = full.shape[1] // 2
        both = full[:, :width] + full[:, width:]
        return both[:samples] + both[samples:]

    count = p_ref.shape[1] // HALF
    group = max(n for n in range(2, GROUP + 1, 2) if count % n == 0)

    def block(step, carry):
        for pair in range(group // 2):
            row = step * group + 2 * pair
            first = row_product(first_row + row)
            second = row_product(first_row + row + 1)
            direct = jnp.where(low_lane, first, pltpu.roll(second, HALF, 1))
            charge = jnp.where(low_lane, pltpu.roll(first, HALF, 1), second)
            here = pl.ds(pl.multiple_of(row * HALF, LANES), LANES)
            g_term, c_term = own_terms(row)
            p_ref[:, here] = direct + g_term
            q_ref[:, here] = charge + c_term
        return carry

    lax.fori_loop(0, count // group, block, 0)


def permuted_product(first_row, cols_ref, order_ref, ext, w_ref, g_ref, c_ref, p_ref, q_ref):
    def own_terms(row):
        there = pl.ds(pl.multiple_of(row * HALF, LANES), LANES)
        return g_ref[:, there], c_ref[:, there]

    product_rows(first_row, True, cols_ref, order_ref, ext, w_ref, p_ref, q_ref, own_terms)


def plain_product(first_row, cols_ref, order_ref, ext, w_ref, field_ref, g_ref, c_ref, p_ref, q_ref):
    def own_terms(row):
        there = pl.ds(pl.multiple_of((first_row + row) * HALF, LANES), LANES)
        own = pair_tile(field_ref, order_ref[1, first_row + row], order_ref[1, first_row + row + 1])
        return g_ref[:, there] * own, c_ref[:, there] * own

    product_rows(first_row, False, cols_ref, order_ref, ext, w_ref, p_ref, q_ref, own_terms)


def slope_columns(matrix, charges):
    samples = charges[0].shape[0]
    parts = [split(x) for x in charges]
    high = jnp.concatenate([h for h, _ in parts], axis=0)
    low = jnp.concatenate([l for _, l in parts], axis=0)
    first = jnp.dot(matrix, high, preferred_element_type=jnp.float32)
    second = jnp.dot(matrix[:samples], low, preferred_element_type=jnp.float32)
    return first[:samples] + first[samples:] + second


CHUNK = 256


def near_kernel(chunks, *refs):
    matrix = refs[0][...]
    p_refs, q_refs, mate_refs, out_refs = [refs[1 + n * chunks : 1 + (n + 1) * chunks] for n in range(4)]
    for p_ref, q_ref, mate_ref, out_ref in zip(p_refs, q_refs, mate_refs, out_refs):
        for start in range(0, p_ref.shape[1], CHUNK):
            inside = slice(start, start + CHUNK)
            out_ref[:, inside] = p_ref[:, inside] + slope_columns(matrix, [q_ref[:, inside], mate_ref[:, inside]])


def far_columns(matrix, p_ref, charge_refs):
    for start in range(0, p_ref.shape[1], CHUNK):
        inside = slice(start, start + CHUNK)
        yield start, p_ref[:, inside] + slope_columns(matrix, [c[:, inside] for c in charge_refs])


def far_kernel(count, base, chunks, *refs):
    matrix = refs[0][...]
    out_ref = refs[-1]
    size = 1 + count
    for n in range(chunks):
        p_ref, *charge_refs = refs[1 + n * size : 1 + (n + 1) * size]
        for start, value in far_columns(matrix, p_ref, charge_refs):
            out_ref[:, base + start : base + start + CHUNK] = value
        base += p_ref.shape[1]


def far_send_kernel(count, chunks, domains, send_near, order_near, *refs):
    size = 1 + count
    u_ref, *out_refs, send_ref, send_sem, order_ref, order_sem = refs[1 + chunks * size :]
    tables = [
        pltpu.make_async_copy(send_near, send_ref, send_sem),
        pltpu.make_async_copy(order_near, order_ref, order_sem),
    ]
    for table in tables:
        table.start()
    far_kernel(count, 0, chunks, *refs[: 1 + chunks * size], u_ref)
    for table in tables:
        table.wait()
    gather_all(domains, send_ref, u_ref, out_refs, order_ref)


def dot_totals(totals, r_ref, u_ref, base, v):
    for i in range(0, v.shape[1], LANES):
        vv = v[:, i : i + LANES]
        rr = r_ref[:, base + i : base + i + LANES]
        uu = u_ref[:, base + i : base + i + LANES]
        for n, (a, b) in enumerate(((uu, uu), (uu, vv), (vv, vv), (rr, uu), (rr, vv))):
            totals[n] = totals[n] + a * b


def far_dots_kernel(count, base, chunks, *refs):
    matrix = refs[0][...]
    out_ref = refs[-1]
    size = 1 + count
    r_ref, u_ref, *before = refs[1 + chunks * size : -1]
    samples = r_ref.shape[0]
    totals = [before[0][n] if before else jnp.zeros((samples, LANES), jnp.float32) for n in range(5)]
    for n in range(chunks):
        p_ref, *charge_refs = refs[1 + n * size : 1 + (n + 1) * size]
        for start, value in far_columns(matrix, p_ref, charge_refs):
            dot_totals(totals, r_ref, u_ref, base + start, value)
        base += p_ref.shape[1]
    if base < u_ref.shape[1]:
        for n in range(5):
            out_ref[n] = totals[n]
        return
    lane = lax.broadcasted_iota(jnp.int32, (1, LANES), 1)
    packed = jnp.zeros((1, LANES), jnp.float32)
    for n, total in enumerate(totals):
        packed = jnp.where(lane == n, jnp.sum(total), packed)
    for d in range(out_ref.shape[0]):
        out_ref[d] = packed


def update_kernel(sums_ref, r_ref, u_ref, out_hbm, out_ref, sems):
    total = jnp.sum(sums_ref[...], axis=0)
    lane = lax.broadcasted_iota(jnp.int32, total.shape, 1)
    uu, uv, vv, ru, rv = [jnp.sum(jnp.where(lane == n, total, 0.0), axis=1, keepdims=True) for n in range(5)]
    length_u = jnp.sqrt(uu)
    length_v = jnp.sqrt(vv)
    cross = uv / length_u / length_v
    target_u = ru / length_u
    target_v = rv / length_v
    determinant = 1.0 - cross * cross
    weight_r = (target_u - cross * target_v) / determinant / length_u
    weight_u = (target_v - cross * target_u) / determinant / length_v
    part = r_ref.shape[0] // COPIES
    copies = []
    for n in range(COPIES):
        rows = slice(n * part, (n + 1) * part)
        for start in range(0, r_ref.shape[1], LANES):
            inside = slice(start, start + LANES)
            out_ref[rows, inside] = weight_r * r_ref[rows, inside] + weight_u * u_ref[rows, inside]
        copies.append(pltpu.make_async_copy(out_ref.at[rows], out_hbm.at[rows], sems.at[n]))
        copies[-1].start()
    for copy in copies:
        copy.wait()


def update(sums, r, u):
    return pl.pallas_call(
        update_kernel,
        in_specs=[whole()] * 3,
        out_specs=pl.BlockSpec(memory_space=pl.ANY),
        out_shape=jax.ShapeDtypeStruct(r.shape, r.dtype),
        scratch_shapes=[pltpu.VMEM(r.shape, r.dtype), pltpu.SemaphoreType.DMA((COPIES,))],
        compiler_params=pltpu.CompilerParams(vmem_limit_bytes=LIMIT),
        name="update",
    )(near_memory(sums), near_memory(r), near_memory(u))


def chunk_sizes(rows, domains, slots):
    unit = rows // 8
    early = (domains - 1) * slots if few(domains) else 3 * unit
    return [unit, early - unit, rows - early], [unit, rows // 16 * 3, 2 * unit, rows // 16 * 5, unit]


def body(residual, conductance, capacitance, stamps, block_cols, send_blocks):
    samples, unknowns = residual.shape
    rows, per_entry = block_cols.shape
    width = stamps.shape[2]
    slots = send_blocks.shape[2]
    domains = lax.axis_size("dom")
    groups = lax.axis_size("samp")
    pairs = [(i, i ^ 1) for i in range(groups)]
    shifts = range(2, groups, 2)
    count = 2 * len(shifts)
    sizes_one, sizes_two = chunk_sizes(rows, domains, slots)
    early = sizes_one[0] + sizes_one[1]
    f32 = jnp.float32
    if few(domains):
        outgoing_shapes = [((samples, slots * width), f32)] * (domains - 1)
    else:
        outgoing_shapes = [((domains, samples, slots * width), f32)]
    field_shape = ((samples, unknowns), f32)
    own_tiles = unknowns // LANES
    tiles = own_tiles + domains * slots * width // LANES
    ext_shape = ((2, tiles, 2 * samples, LANES), jnp.bfloat16)
    weight_shape = ((rows, per_entry * width, 4 * width), jnp.bfloat16)
    cols = block_cols.T
    send = send_blocks[0].T

    def exchange(outgoing):
        if not few(domains):
            return [lax.all_to_all(outgoing[0], "dom", split_axis=0, concat_axis=0, tiled=True)]
        incoming = []
        for k, x in zip(halo_offsets(domains), outgoing):
            incoming.append(lax.ppermute(x, "dom", [(i, i ^ k) for i in range(domains)]))
        return incoming

    def product_call(n, size, product, operands, incoming):
        shape = ((samples, size * width), f32)
        if n:
            p, q = kernel_call(product, operands, [shape, shape])
            return operands[2], p, q
        return kernel_call(
            functools.partial(with_arrived, domains, product, own_tiles),
            (*operands, *incoming),
            [ext_shape, shape, shape],
            aliases={2: 0},
            table_copied=True,
        )

    def spread(q):
        far = [lax.ppermute(q, "samp", [(i, (i + k) % groups) for i in range(groups)]) for k in shifts]
        return far, lax.ppermute(q, "samp", pairs)

    def near_call(chunks):
        return kernel_call(
            functools.partial(near_kernel, len(chunks)),
            (near_matrix, *[p for p, _, _, _ in chunks], *[q for _, q, _, _ in chunks], *[m for _, _, _, m in chunks]),
            [(p.shape, f32) for p, _, _, _ in chunks],
        )

    def forward(half, far):
        charges = []
        for x in far:
            charges += [x, lax.ppermute(x, "samp", pairs)]
        return [half, *charges]

    field, *outgoing = gather(send, residual, domains, outgoing_shapes)
    incoming = exchange(outgoing)
    blocks = stamps.reshape(rows, per_entry * width, 2 * width)
    order, weights, ext, near_matrix, far_matrix = fetch(
        send,
        field,
        blocks,
        early,
        domains,
        groups,
        [
            ext_shape,
            ((2 * samples, 2 * samples), jnp.bfloat16),
            ((2 * samples, count * samples), jnp.bfloat16),
        ],
    )
    (all_weights,) = kernel_call(
        functools.partial(prepare_kernel, early, rows), (order, blocks, weights), [weight_shape], aliases={2: 0}
    )
    chunks = []
    first = 0
    for n, size in enumerate(sizes_one):
        terms = kernel_call(
            functools.partial(arrange_kernel, first),
            (order, field, conductance, capacitance),
            [((samples, size * width), f32)] * 2,
        )
        operands = (cols, order, ext, weights if first < early else all_weights, *terms)
        ext, p, q = product_call(n, size, functools.partial(permuted_product, first), operands, incoming)
        chunks.append((p, q, *spread(q)))
        first += size
    weights = all_weights
    half = near_call(chunks[:2]) + near_call(chunks[2:])
    pieces = [forward(half[n], chunk[2]) for n, chunk in enumerate(chunks)]
    ready = 2 if few(domains) else len(chunks)
    u, *outgoing = kernel_call(
        functools.partial(far_send_kernel, count, ready, domains),
        (send, order, far_matrix, *[x for piece in pieces[:ready] for x in piece]),
        [field_shape, *outgoing_shapes],
        table_copied=True,
    )
    incoming = exchange(outgoing)
    if ready < len(chunks):
        operands = [far_matrix, *[x for piece in pieces[ready:] for x in piece]]
        (u,) = kernel_call(
            functools.partial(far_kernel, count, early * width, len(chunks) - ready),
            operands + [u],
            [field_shape],
            aliases={len(operands): 0},
        )
    (ext,) = kernel_call(extend_kernel, (u,), [ext_shape])
    chunks = []
    first = 0
    for n, size in enumerate(sizes_two):
        operands = (cols, order, ext, weights, u, conductance, capacitance)
        ext, p, q = product_call(n, size, functools.partial(plain_product, first), operands, incoming)
        chunks.append((p, q, *spread(q)))
        first += size
    (u,) = kernel_call(restore_kernel, (order, u), [field_shape])
    half = near_call(chunks)
    pieces = [forward(half[n], chunk[2]) for n, chunk in enumerate(chunks)]
    sums = None
    last = len(chunks) - 1
    for n, (low, high) in enumerate(((0, last - 1), (last - 1, last), (last, last + 1))):
        final = high > last
        (sums,) = kernel_call(
            functools.partial(far_dots_kernel, count, sum(sizes_two[:low]) * width, high - low),
            [far_matrix, *[x for piece in pieces[low:high] for x in piece], field, u] + [sums] * (n > 0),
            [((domains * groups, 1, LANES) if final else (5, samples, LANES), f32)],
        )
    sums = lax.all_to_all(sums, ("dom", "samp"), split_axis=0, concat_axis=0, tiled=True)
    return update(sums, field, u)


def solution(mesh):
    in_specs = (
        P("samp", "dom"),
        P("samp", "dom"),
        P("samp", "dom"),
        P("dom", None, None, None),
        P("dom", None),
        P("dom", None, None),
    )
    out_specs = P("samp", "dom")
    return jax.shard_map(body, mesh=mesh, in_specs=in_specs, out_specs=out_specs, check_vma=False)
```

```python
import functools

import jax
import jax.numpy as jnp
from jax import lax
from jax.experimental import pallas as pl
from jax.experimental.pallas import tpu as pltpu
from jax.sharding import PartitionSpec as P


LANES = 128
HALF = 64
GROUP = 12


LIMIT = 24 * 1024 * 1024


def whole():
    return pl.BlockSpec(memory_space=pltpu.VMEM)


def scalars():
    return pl.BlockSpec(memory_space=pltpu.SMEM)


def near_memory(x):
    return pltpu.with_memory_space_constraint(x, pltpu.VMEM)


def far_memory(x):
    return pltpu.with_memory_space_constraint(x, pltpu.HBM)


def kernel_call(kernel, inputs, outputs, aliases=None, table_copied=False):
    specs = []
    operands = []
    scratch = []
    for x in inputs:
        if x.dtype == jnp.int32 and table_copied:
            specs.append(pl.BlockSpec(memory_space=pl.ANY))
            operands.append(near_memory(x))
            scratch += [pltpu.SMEM(x.shape, x.dtype), pltpu.SemaphoreType.DMA]
        elif x.dtype == jnp.int32:
            specs.append(scalars())
            operands.append(x)
        else:
            specs.append(whole())
            operands.append(near_memory(x))
    integer = [dtype == jnp.int32 for _, dtype in outputs]
    out = [
        jax.ShapeDtypeStruct(shape, dtype) if number else pltpu.VMEM(shape, dtype)
        for (shape, dtype), number in zip(outputs, integer)
    ]
    return pl.pallas_call(
        kernel,
        in_specs=specs,
        out_specs=[scalars() if number else whole() for number in integer],
        out_shape=out,
        input_output_aliases=aliases or {},
        scratch_shapes=scratch,
        compiler_params=pltpu.CompilerParams(vmem_limit_bytes=LIMIT),
    )(*operands)


def split(x):
    high = x.astype(jnp.bfloat16)
    low = (x - high.astype(jnp.float32)).astype(jnp.bfloat16)
    return high, low


def spectral_rows(me, sources, samples, period):
    row = me * samples + lax.broadcasted_iota(jnp.int32, (samples, samples), 0)
    column = lax.broadcasted_iota(jnp.int32, (samples, samples), 1)
    blocks = []
    for source in sources:
        offset = row - (source * samples + column)
        sign = (1 - 2 * (offset & 1)).astype(jnp.float32)
        angle = jnp.pi / period * offset.astype(jnp.float32)
        nonzero = offset != 0
        safe = jnp.where(nonzero, angle, 0.5)
        value = sign * jnp.cos(safe) / jnp.sin(safe) / period
        blocks.append(jnp.where(nonzero, value, 0.0))
    high, low = split(jnp.concatenate(blocks, axis=1))
    return jnp.concatenate([high, low], axis=0)


def tables_kernel(groups, near_ref, far_ref):
    samples = near_ref.shape[1] // 2
    me = lax.axis_index("samp")
    partner = me + 1 - 2 * (me & 1)
    near_ref[...] = spectral_rows(me, [me, partner], samples, samples * groups)
    far = []
    for k in range(2, groups, 2):
        for source in (me - k, partner - k):
            far.append(jnp.where(source < 0, source + groups, source))
    far_ref[...] = spectral_rows(me, far, samples, samples * groups)


def prepare_kernel(first_row, last_row, order_ref, stamps_ref, *refs):
    out_ref = refs[-1]
    width = stamps_ref.shape[2]

    def convert(row, carry):
        high, low = split(stamps_ref[order_ref[0, row]])
        out_ref[row, :, :width] = high
        out_ref[row, :, width:] = low
        return carry

    lax.fori_loop(first_row, last_row, convert, 0, unroll=2)


def fetch_kernel(groups, order_ref, field_ref, stamps_hbm, out_ref, *refs):
    ext, near_ref, far_ref, buffer, sems = refs
    rows, _, width = buffer.shape
    copies = []
    for n in range(rows):
        copies.append(pltpu.make_async_copy(stamps_hbm.at[order_ref[0, n]], buffer.at[n], sems.at[n]))
        copies[-1].start()
    extend_kernel(field_ref, ext)
    tables_kernel(groups, near_ref, far_ref)
    for n, copy in enumerate(copies):
        copy.wait()
        high, low = split(buffer[n])
        out_ref[n, :, :width] = high
        out_ref[n, :, width:] = low


def fetch(order, field, stamps, rows, groups, outputs):
    total, depth, width = stamps.shape
    return pl.pallas_call(
        functools.partial(fetch_kernel, groups),
        in_specs=[scalars(), whole(), pl.BlockSpec(memory_space=pl.ANY)],
        out_specs=[whole()] * (1 + len(outputs)),
        out_shape=[
            pltpu.VMEM((total, depth, 2 * width), jnp.bfloat16),
            *[pltpu.VMEM(shape, dtype) for shape, dtype in outputs],
        ],
        scratch_shapes=[pltpu.VMEM((rows, depth, width), stamps.dtype), pltpu.SemaphoreType.DMA((rows,))],
        compiler_params=pltpu.CompilerParams(vmem_limit_bytes=LIMIT),
        name="prepare_0",
    )(order, near_memory(field), far_memory(stamps))


def pair_tile(ref, first, second):
    samples = ref.shape[0]
    lane = lax.broadcasted_iota(jnp.int32, (samples, LANES), 1)

    def placed(block, upper):
        start = pl.multiple_of((block // 2) * LANES, LANES)
        tile = ref[:, pl.ds(start, LANES)]
        turned = pltpu.roll(tile, HALF, 1)
        return jnp.where((block & 1) == upper, tile, turned)

    return jnp.where(lane < HALF, placed(first, 0), placed(second, 1))


def gather_blocks(targets, send_ref, field_ref, out_refs, order_ref=None):
    slots = send_ref.shape[0]
    for d, out_ref in zip(targets, out_refs):
        for j in range(0, slots, 2):
            first, second = send_ref[j, d], send_ref[j + 1, d]
            if order_ref is not None:
                first, second = order_ref[1, first], order_ref[1, second]
            out_ref[:, j * HALF : j * HALF + LANES] = pair_tile(field_ref, first, second)


def halo_offsets(domains):
    return sorted(range(1, domains), key=lambda k: (-(k >= domains // 2), k if k >= domains // 2 else -k))


def few(domains):
    return domains <= 8 and domains & (domains - 1) == 0


def gather_all(domains, send_ref, field_ref, out_refs, order_ref=None):
    if few(domains):
        me = lax.axis_index("dom")
        gather_blocks([me ^ k for k in halo_offsets(domains)], send_ref, field_ref, out_refs, order_ref)
    else:
        gather_blocks(range(domains), send_ref, field_ref, [out_refs[0].at[d] for d in range(domains)], order_ref)


COPIES = 4


WORD = 32


def order_rows(domains, send_ref, order_ref):
    rows = order_ref.shape[1]
    masks = [jnp.int32(0)] * (rows // WORD)
    if few(domains):
        me = lax.axis_index("dom")
        for d in range(domains):
            for j in range(send_ref.shape[0]):
                block = send_ref[j, d]
                bit = jnp.where(d == me, 0, jnp.left_shift(jnp.int32(1), block & (WORD - 1)))
                masks = [m | jnp.where(block // WORD == n, bit, 0) for n, m in enumerate(masks)]
    flags = [lax.shift_right_logical(masks[row // WORD], jnp.int32(row % WORD)) & 1 for row in range(rows)]
    first = jnp.int32(0)
    later = sum(flags)
    for row, flag in enumerate(flags):
        position = jnp.where(flag == 1, first, later)
        order_ref[0, position] = row
        order_ref[1, row] = position
        first = first + flag
        later = later + 1 - flag


def gather_kernel(domains, send_hbm, field_hbm, order_ref, field_ref, *refs):
    *out_refs, field_sem, send_ref, send_sem = refs
    table = pltpu.make_async_copy(send_hbm, send_ref, send_sem)
    table.start()
    width = field_ref.shape[1] // COPIES
    copies = []
    for n in range(COPIES):
        inside = pl.ds(n * width, width)
        copies.append(pltpu.make_async_copy(field_hbm.at[:, inside], field_ref.at[:, inside], field_sem.at[n]))
        copies[-1].start()
    table.wait()
    order_rows(domains, send_ref, order_ref)
    for copy in copies:
        copy.wait()
    gather_all(domains, send_ref, field_ref, out_refs)


def gather(send, field, rows, domains, outputs):
    return pl.pallas_call(
        functools.partial(gather_kernel, domains),
        in_specs=[pl.BlockSpec(memory_space=pl.ANY)] * 2,
        out_specs=[scalars()] + [whole()] * (1 + len(outputs)),
        out_shape=[
            jax.ShapeDtypeStruct((2, rows), jnp.int32),
            *[pltpu.VMEM(shape, dtype) for shape, dtype in ((field.shape, field.dtype), *outputs)],
        ],
        scratch_shapes=[
            pltpu.SemaphoreType.DMA((COPIES,)),
            pltpu.SMEM(send.shape, send.dtype),
            pltpu.SemaphoreType.DMA,
        ],
        compiler_params=pltpu.CompilerParams(vmem_limit_bytes=LIMIT),
        name="gather",
    )(far_memory(send), far_memory(field))


def store_tile(ext, index, x):
    high, low = split(x)
    ext[0, index] = jnp.concatenate([high, low], axis=0)
    high, low = split(pltpu.roll(x, HALF, 1))
    ext[1, index] = jnp.concatenate([high, low], axis=0)


def arrange_kernel(first_row, order_ref, field_ref, g_ref, c_ref, g_out, c_out):
    samples = field_ref.shape[0]
    lane = lax.broadcasted_iota(jnp.int32, (samples, LANES), 1)

    def placed(block, upper):
        here = pl.ds(pl.multiple_of((block // 2) * LANES, LANES), LANES)
        own = field_ref[:, here]
        keep = (block & 1) == upper
        return [jnp.where(keep, x, pltpu.roll(x, HALF, 1)) for x in (g_ref[:, here] * own, c_ref[:, here] * own)]

    for i in range(g_out.shape[1] // LANES):
        inside = slice(i * LANES, (i + 1) * LANES)
        low = placed(order_ref[0, first_row + 2 * i], 0)
        high = placed(order_ref[0, first_row + 2 * i + 1], 1)
        g_out[:, inside] = jnp.where(lane < HALF, low[0], high[0])
        c_out[:, inside] = jnp.where(lane < HALF, low[1], high[1])


def restore_kernel(order_ref, u_ref, out_ref):
    for i in range(u_ref.shape[1] // LANES):
        inside = slice(i * LANES, (i + 1) * LANES)
        out_ref[:, inside] = pair_tile(u_ref, order_ref[1, 2 * i], order_ref[1, 2 * i + 1])


def extend_kernel(field_ref, ext):
    for i in range(field_ref.shape[1] // LANES):
        store_tile(ext, i, field_ref[:, i * LANES : (i + 1) * LANES])


def extend_arrived(domains, own_tiles, inc_refs, ext):
    if few(domains):
        me = lax.axis_index("dom")
        arrived = [(me ^ k, ref) for k, ref in zip(halo_offsets(domains), inc_refs)]
    else:
        arrived = [(d, inc_refs[0].at[d]) for d in range(domains)]
    for source, ref in arrived:
        per_domain = ref.shape[1] // LANES
        for j in range(per_domain):
            store_tile(ext, own_tiles + source * per_domain + j, ref[:, j * LANES : (j + 1) * LANES])


def with_arrived(domains, product, own_tiles, cols_near, order_near, *refs):
    *inputs, out_ext, p_ref, q_ref, cols_ref, cols_sem, order_ref, order_sem = refs
    tables = [
        pltpu.make_async_copy(cols_near, cols_ref, cols_sem),
        pltpu.make_async_copy(order_near, order_ref, order_sem),
    ]
    for table in tables:
        table.start()
    offsets = domains - 1 if few(domains) else 1
    own_ext, *inputs = inputs
    extend_arrived(domains, own_tiles, inputs[len(inputs) - offsets :], out_ext)
    for table in tables:
        table.wait()
    product(cols_ref, order_ref, out_ext, *inputs[: len(inputs) - offsets], p_ref, q_ref)


def product_rows(first_row, permuted, cols_ref, order_ref, ext, w_ref, p_ref, q_ref, own_terms):
    samples = p_ref.shape[0]
    per_entry = cols_ref.shape[0]
    lane = lax.broadcasted_iota(jnp.int32, (2 * samples, LANES), 1)
    low_lane = lax.broadcasted_iota(jnp.int32, (samples, LANES), 1) < HALF

    rows = cols_ref.shape[1]

    def entry_of(k, row):
        entry = cols_ref[k, row]
        if permuted:
            return entry
        return jnp.where(entry < rows, order_ref[1, jnp.minimum(entry, rows - 1)], entry)

    def row_product(row):
        source, place = (order_ref[0, row], row) if permuted else (row, order_ref[1, row])
        parts = []
        for k in range(0, per_entry, 2):
            first = entry_of(k, source)
            second = entry_of(k + 1, source)
            a = ext[first & 1, first // 2]
            b = ext[1 - (second & 1), second // 2]
            parts.append(jnp.where(lane < HALF, a, b))
        left = jnp.concatenate(parts, axis=1)
        full = jnp.dot(left, w_ref[place], preferred_element_type=jnp.float32)
        width = full.shape[1] // 2
        both = full[:, :width] + full[:, width:]
        return both[:samples] + both[samples:]

    count = p_ref.shape[1] // HALF
    group = max(n for n in range(2, GROUP + 1, 2) if count % n == 0)

    def block(step, carry):
        for pair in range(group // 2):
            row = step * group + 2 * pair
            first = row_product(first_row + row)
            second = row_product(first_row + row + 1)
            direct = jnp.where(low_lane, first, pltpu.roll(second, HALF, 1))
            charge = jnp.where(low_lane, pltpu.roll(first, HALF, 1), second)
            here = pl.ds(pl.multiple_of(row * HALF, LANES), LANES)
            g_term, c_term = own_terms(row)
            p_ref[:, here] = direct + g_term
            q_ref[:, here] = charge + c_term
        return carry

    lax.fori_loop(0, count // group, block, 0)


def permuted_product(first_row, base_row, cols_ref, order_ref, ext, w_ref, g_ref, c_ref, p_ref, q_ref):
    def own_terms(row):
        there = pl.ds(pl.multiple_of((first_row - base_row + row) * HALF, LANES), LANES)
        return g_ref[:, there], c_ref[:, there]

    product_rows(first_row, True, cols_ref, order_ref, ext, w_ref, p_ref, q_ref, own_terms)


def plain_product(first_row, cols_ref, order_ref, ext, w_ref, field_ref, g_ref, c_ref, p_ref, q_ref):
    def own_terms(row):
        there = pl.ds(pl.multiple_of((first_row + row) * HALF, LANES), LANES)
        own = pair_tile(field_ref, order_ref[1, first_row + row], order_ref[1, first_row + row + 1])
        return g_ref[:, there] * own, c_ref[:, there] * own

    product_rows(first_row, False, cols_ref, order_ref, ext, w_ref, p_ref, q_ref, own_terms)


def slope_columns(matrix, charges):
    samples = charges[0].shape[0]
    parts = [split(x) for x in charges]
    high = jnp.concatenate([h for h, _ in parts], axis=0)
    low = jnp.concatenate([l for _, l in parts], axis=0)
    first = jnp.dot(matrix, high, preferred_element_type=jnp.float32)
    second = jnp.dot(matrix[:samples], low, preferred_element_type=jnp.float32)
    return first[:samples] + first[samples:] + second


CHUNK = 256


def near_kernel(chunks, *refs):
    matrix = refs[0][...]
    p_refs, q_refs, mate_refs, out_refs = [refs[1 + n * chunks : 1 + (n + 1) * chunks] for n in range(4)]
    for p_ref, q_ref, mate_ref, out_ref in zip(p_refs, q_refs, mate_refs, out_refs):
        for start in range(0, p_ref.shape[1], CHUNK):
            inside = slice(start, start + CHUNK)
            out_ref[:, inside] = p_ref[:, inside] + slope_columns(matrix, [q_ref[:, inside], mate_ref[:, inside]])


def far_columns(matrix, p_ref, charge_refs):
    for start in range(0, p_ref.shape[1], CHUNK):
        inside = slice(start, start + CHUNK)
        yield start, p_ref[:, inside] + slope_columns(matrix, [c[:, inside] for c in charge_refs])


def far_kernel(count, base, chunks, *refs):
    matrix = refs[0][...]
    out_ref = refs[-1]
    size = 1 + count
    for n in range(chunks):
        p_ref, *charge_refs = refs[1 + n * size : 1 + (n + 1) * size]
        for start, value in far_columns(matrix, p_ref, charge_refs):
            out_ref[:, base + start : base + start + CHUNK] = value
        base += p_ref.shape[1]


def far_send_kernel(count, chunks, domains, send_near, order_near, *refs):
    size = 1 + count
    u_ref, *out_refs, send_ref, send_sem, order_ref, order_sem = refs[1 + chunks * size :]
    tables = [
        pltpu.make_async_copy(send_near, send_ref, send_sem),
        pltpu.make_async_copy(order_near, order_ref, order_sem),
    ]
    for table in tables:
        table.start()
    far_kernel(count, 0, chunks, *refs[: 1 + chunks * size], u_ref)
    for table in tables:
        table.wait()
    gather_all(domains, send_ref, u_ref, out_refs, order_ref)


def dot_totals(totals, r_ref, u_ref, base, v):
    for i in range(0, v.shape[1], LANES):
        vv = v[:, i : i + LANES]
        rr = r_ref[:, base + i : base + i + LANES]
        uu = u_ref[:, base + i : base + i + LANES]
        for n, (a, b) in enumerate(((uu, uu), (uu, vv), (vv, vv), (rr, uu), (rr, vv))):
            totals[n] = totals[n] + a * b


def far_dots_kernel(count, base, chunks, *refs):
    matrix = refs[0][...]
    out_ref = refs[-1]
    size = 1 + count
    r_ref, u_ref, *before = refs[1 + chunks * size : -1]
    samples = r_ref.shape[0]
    totals = [before[0][n] if before else jnp.zeros((samples, LANES), jnp.float32) for n in range(5)]
    for n in range(chunks):
        p_ref, *charge_refs = refs[1 + n * size : 1 + (n + 1) * size]
        for start, value in far_columns(matrix, p_ref, charge_refs):
            dot_totals(totals, r_ref, u_ref, base + start, value)
        base += p_ref.shape[1]
    if base < u_ref.shape[1]:
        for n in range(5):
            out_ref[n] = totals[n]
        return
    lane = lax.broadcasted_iota(jnp.int32, (1, LANES), 1)
    packed = jnp.zeros((1, LANES), jnp.float32)
    for n, total in enumerate(totals):
        packed = jnp.where(lane == n, jnp.sum(total), packed)
    for d in range(out_ref.shape[0]):
        out_ref[d] = packed


def update_kernel(sums_ref, r_ref, u_ref, out_hbm, out_ref, sems):
    total = jnp.sum(sums_ref[...], axis=0)
    lane = lax.broadcasted_iota(jnp.int32, total.shape, 1)
    uu, uv, vv, ru, rv = [jnp.sum(jnp.where(lane == n, total, 0.0), axis=1, keepdims=True) for n in range(5)]
    length_u = jnp.sqrt(uu)
    length_v = jnp.sqrt(vv)
    cross = uv / length_u / length_v
    target_u = ru / length_u
    target_v = rv / length_v
    determinant = 1.0 - cross * cross
    weight_r = (target_u - cross * target_v) / determinant / length_u
    weight_u = (target_v - cross * target_u) / determinant / length_v
    part = r_ref.shape[0] // COPIES
    copies = []
    for n in range(COPIES):
        rows = slice(n * part, (n + 1) * part)
        for start in range(0, r_ref.shape[1], LANES):
            inside = slice(start, start + LANES)
            out_ref[rows, inside] = weight_r * r_ref[rows, inside] + weight_u * u_ref[rows, inside]
        copies.append(pltpu.make_async_copy(out_ref.at[rows], out_hbm.at[rows], sems.at[n]))
        copies[-1].start()
    for copy in copies:
        copy.wait()


def update(sums, r, u):
    return pl.pallas_call(
        update_kernel,
        in_specs=[whole()] * 3,
        out_specs=pl.BlockSpec(memory_space=pl.ANY),
        out_shape=jax.ShapeDtypeStruct(r.shape, r.dtype),
        scratch_shapes=[pltpu.VMEM(r.shape, r.dtype), pltpu.SemaphoreType.DMA((COPIES,))],
        compiler_params=pltpu.CompilerParams(vmem_limit_bytes=LIMIT),
        name="update",
    )(near_memory(sums), near_memory(r), near_memory(u))


def chunk_sizes(rows, domains, slots):
    unit = rows // 8
    early = (domains - 1) * slots if few(domains) else 3 * unit
    return [unit, early - unit, rows - early], [unit, rows // 16 * 3, 2 * unit, rows // 16 * 5, unit]


def body(residual, conductance, capacitance, stamps, block_cols, send_blocks):
    samples, unknowns = residual.shape
    rows, per_entry = block_cols.shape
    width = stamps.shape[2]
    slots = send_blocks.shape[2]
    domains = lax.axis_size("dom")
    groups = lax.axis_size("samp")
    pairs = [(i, i ^ 1) for i in range(groups)]
    shifts = range(2, groups, 2)
    count = 2 * len(shifts)
    sizes_one, sizes_two = chunk_sizes(rows, domains, slots)
    early = sizes_one[0] + sizes_one[1]
    f32 = jnp.float32
    if few(domains):
        outgoing_shapes = [((samples, slots * width), f32)] * (domains - 1)
    else:
        outgoing_shapes = [((domains, samples, slots * width), f32)]
    field_shape = ((samples, unknowns), f32)
    own_tiles = unknowns // LANES
    tiles = own_tiles + domains * slots * width // LANES
    ext_shape = ((2, tiles, 2 * samples, LANES), jnp.bfloat16)
    weight_shape = ((rows, per_entry * width, 4 * width), jnp.bfloat16)
    cols = block_cols.T
    send = send_blocks[0].T

    def exchange(outgoing):
        if not few(domains):
            return [lax.all_to_all(outgoing[0], "dom", split_axis=0, concat_axis=0, tiled=True)]
        incoming = []
        for k, x in zip(halo_offsets(domains), outgoing):
            incoming.append(lax.ppermute(x, "dom", [(i, i ^ k) for i in range(domains)]))
        return incoming

    def product_call(n, size, product, operands, incoming):
        shape = ((samples, size * width), f32)
        if n:
            p, q = kernel_call(product, operands, [shape, shape])
            return operands[2], p, q
        return kernel_call(
            functools.partial(with_arrived, domains, product, own_tiles),
            (*operands, *incoming),
            [ext_shape, shape, shape],
            aliases={2: 0},
            table_copied=True,
        )

    def spread(q):
        far = [lax.ppermute(q, "samp", [(i, (i + k) % groups) for i in range(groups)]) for k in shifts]
        return far, lax.ppermute(q, "samp", pairs)

    def near_call(chunks):
        return kernel_call(
            functools.partial(near_kernel, len(chunks)),
            (near_matrix, *[p for p, _, _, _ in chunks], *[q for _, q, _, _ in chunks], *[m for _, _, _, m in chunks]),
            [(p.shape, f32) for p, _, _, _ in chunks],
        )

    def forward(half, far):
        charges = []
        for x in far:
            charges += [x, lax.ppermute(x, "samp", pairs)]
        return [half, *charges]

    order, field, *outgoing = gather(send, residual, rows, domains, outgoing_shapes)
    incoming = exchange(outgoing)
    blocks = stamps.reshape(rows, per_entry * width, 2 * width)
    weights, ext, near_matrix, far_matrix = fetch(
        order,
        field,
        blocks,
        early,
        groups,
        [
            ext_shape,
            ((2 * samples, 2 * samples), jnp.bfloat16),
            ((2 * samples, count * samples), jnp.bfloat16),
        ],
    )
    own = []
    for n, (low, high) in enumerate(((0, early), (early, rows))):
        if n:
            (weights,) = kernel_call(
                functools.partial(prepare_kernel, low, high), (order, blocks, weights), [weight_shape], aliases={2: 0}
            )
        terms = kernel_call(
            functools.partial(arrange_kernel, low),
            (order, field, conductance, capacitance),
            [((samples, (high - low) * width), f32)] * 2,
        )
        own.append((low, weights, terms))
    chunks = []
    first = 0
    for n, size in enumerate(sizes_one):
        base, w, terms = own[first >= early]
        ext, p, q = product_call(
            n, size, functools.partial(permuted_product, first, base), (cols, order, ext, w, *terms), incoming
        )
        chunks.append((p, q, *spread(q)))
        first += size
    half = near_call(chunks[:2]) + near_call(chunks[2:])
    pieces = [forward(half[n], chunk[2]) for n, chunk in enumerate(chunks)]
    ready = 2 if few(domains) else len(chunks)
    u, *outgoing = kernel_call(
        functools.partial(far_send_kernel, count, ready, domains),
        (send, order, far_matrix, *[x for piece in pieces[:ready] for x in piece]),
        [field_shape, *outgoing_shapes],
        table_copied=True,
    )
    incoming = exchange(outgoing)
    if ready < len(chunks):
        operands = [far_matrix, *[x for piece in pieces[ready:] for x in piece]]
        (u,) = kernel_call(
            functools.partial(far_kernel, count, early * width, len(chunks) - ready),
            operands + [u],
            [field_shape],
            aliases={len(operands): 0},
        )
    (ext,) = kernel_call(extend_kernel, (u,), [ext_shape])
    chunks = []
    first = 0
    for n, size in enumerate(sizes_two):
        operands = (cols, order, ext, weights, u, conductance, capacitance)
        ext, p, q = product_call(n, size, functools.partial(plain_product, first), operands, incoming)
        chunks.append((p, q, *spread(q)))
        first += size
    (u,) = kernel_call(restore_kernel, (order, u), [field_shape])
    half = near_call(chunks)
    pieces = [forward(half[n], chunk[2]) for n, chunk in enumerate(chunks)]
    sums = None
    last = len(chunks) - 1
    for n, (low, high) in enumerate(((0, last - 1), (last - 1, last), (last, last + 1))):
        final = high > last
        (sums,) = kernel_call(
            functools.partial(far_dots_kernel, count, sum(sizes_two[:low]) * width, high - low),
            [far_matrix, *[x for piece in pieces[low:high] for x in piece], field, u] + [sums] * (n > 0),
            [((domains * groups, 1, LANES) if final else (5, samples, LANES), f32)],
        )
    sums = lax.all_to_all(sums, ("dom", "samp"), split_axis=0, concat_axis=0, tiled=True)
    return update(sums, field, u)


def solution(mesh):
    in_specs = (
        P("samp", "dom"),
        P("samp", "dom"),
        P("samp", "dom"),
        P("dom", None, None, None),
        P("dom", None),
        P("dom", None, None),
    )
    out_specs = P("samp", "dom")
    return jax.shard_map(body, mesh=mesh, in_specs=in_specs, out_specs=out_specs, check_vma=False)
```
